512 devices in a mesh: ctx: 64 (over z, y), vid: 8 (over x, core).
Axes of the slice: x: 4, y: 4, z: 16, core: 2. Of those that a mesh axis runs over, the one named last changes fastest.
Arguments:
- features: bfloat16 [8, 128, 8, 32, 256], P('vid', 'ctx'), may hold values from -6 to 6
- grad_out: bfloat16 [8, 128, 8, 32, 128], P('vid', 'ctx'), may hold values from -6 to 6
- mean_saved: float32 [8, 32], P('vid'), may hold values from -3 to 3
- rstd_saved: float32 [8, 32], P('vid'), may hold values from 0.5 to 2
- latent: float32 [8, 32, 16, 16], P('vid'), may hold values from -6 to 6
- gamma: float32 [256], replicated, may hold values from 0.5 to 1.5
- beta: float32 [256], replicated, may hold values from -3 to 3
- w_scale: float32 [16, 256], replicated, may hold values from -1.5 to 1.5
- b_scale: float32 [256], replicated, may hold values from -3 to 3
- w_shift: float32 [16, 256], replicated, may hold values from -1.5 to 1.5
- b_shift: float32 [256], replicated, may hold values from -3 to 3
- kernel: bfloat16 [6912, 128], replicated, may hold values from -0.078125 to 0.078125
Outputs:
- features_grad: bfloat16 [8, 128, 8, 32, 256], P('vid', 'ctx')
- kernel_grad: float32 [6912, 128], P('ctx', 'vid')
- mod_grads: float32 [2, 16, 256], replicated
- vector_grads: float32 [4, 256], replicated
- latent_grad: float32 [8, 64, 16, 8], P('vid', 'ctx')
The draws below stay inside these ranges and needn't reach their ends.
All inputs are finite; a program needn't handle non-finite values.
Results may differ from the reference program's by a relative error of at most 0.0029.
Values may be sent and summed in bfloat16 or wider, within the bound.
A program may use at most 64 MiB of HBM per device.

```python
import math
import jax
import jax.numpy as jnp
from jax import lax

H = 8
W = 32
C = 256
CO = 128
CZ = 16
G = 32
VIDEOS = 8
FRAMES = 128
LATENT = 32
LP = 16


def block_levels(own_key, extent, cuts, smallest, largest):
    loudness, own = 1.0, jax.random.fold_in(own_key, 6)
    for position, parts in cuts:
        steps = jnp.exp(jax.random.uniform(jax.random.fold_in(own, position), (parts,), jnp.float32, smallest / len(cuts), largest / len(cuts)))
        loudness = loudness * jnp.repeat(steps, extent[position] // parts).reshape([-1 if axis == position else 1 for axis in range(len(extent))])
    return loudness


def bell_draw(rng, dims, width, reach, cuts=(), kind=jnp.bfloat16):
    drawn = jax.random.normal(rng, dims, jnp.float32) * width
    if len(cuts) > 0:
        drawn = block_levels(rng, dims, cuts, -0.22, 0.18) * drawn
    return jnp.clip(drawn, min=-reach, max=reach).astype(kind)


def setup_inputs(seed: int = 0) -> dict:
    keys = jax.random.split(jax.random.key(seed), 13)
    features = bell_draw(keys[0], (VIDEOS, FRAMES, H, W, C), 1.0, 6.0, ((0, 8), (1, 64)))
    grad_out = bell_draw(keys[1], (VIDEOS, FRAMES, H, W, CO), 1.0, 6.0, ((0, 8), (1, 64)))
    mean_saved = bell_draw(keys[2], (VIDEOS, G), 0.4, 3.0, ((0, 8),), jnp.float32)
    rstd_saved = jnp.clip(jnp.exp(math.log(2.0) - 1.3862944 * jax.random.uniform(keys[3], (VIDEOS, G), jnp.float32) ** block_levels(keys[3], (VIDEOS, G), ((0, 8),), -0.2, 0.2)), 0.5, 2.0)
    latent = bell_draw(keys[4], (VIDEOS, LATENT, CZ, LP), 1.0, 6.0, ((0, 8),), jnp.float32)
    gamma = jnp.clip(jax.random.uniform(keys[5], (C,), jnp.float32, 0.5, 1.5), 0.5, 1.5)
    beta = bell_draw(keys[6], (C,), 0.5, 3.0, (), jnp.float32)
    w_scale = bell_draw(keys[7], (CZ, C), CZ ** -0.5, 1.5, (), jnp.float32)
    b_scale = bell_draw(keys[8], (C,), 0.5, 3.0, (), jnp.float32)
    w_shift = bell_draw(keys[9], (CZ, C), CZ ** -0.5, 1.5, (), jnp.float32)
    b_shift = bell_draw(keys[10], (C,), 0.5, 3.0, (), jnp.float32)
    kernel = bell_draw(keys[11], (27 * C, CO), (27 * C) ** -0.5, 0.078125)
    return dict(features=features, grad_out=grad_out, mean_saved=mean_saved, rstd_saved=rstd_saved, latent=latent, gamma=gamma, beta=beta, w_scale=w_scale, b_scale=b_scale, w_shift=w_shift, b_shift=b_shift, kernel=kernel)


highest = lax.Precision.HIGHEST


def spread(table):
    count = table.shape[0]
    grid = table.reshape(count, H // 4, W // 4, C)
    wide = jnp.broadcast_to(grid[:, None, :, None, :, None, :], (count, 4, H // 4, 4, W // 4, 4, C))
    return wide.reshape(count * 4, H, W, C)


def pool_blocks(field):
    count = field.shape[0] // 4
    return field.reshape(count, 4, H // 4, 4, W // 4, 4, C).sum(axis=(1, 3, 5)).reshape(count, LP, C)


def reference(features, grad_out, mean_saved, rstd_saved, latent, gamma, beta, w_scale, b_scale, w_shift, b_shift, kernel):
    tap_weights = kernel.reshape(3, 3, 3, C, CO)

    def one_video(operands):
        frames_in, grads_in, mean_row, rstd_row, latent_row = operands
        mean_chan = jnp.broadcast_to(mean_row[:, None], (G, C // G)).reshape(C)
        rstd_chan = jnp.broadcast_to(rstd_row[:, None], (G, C // G)).reshape(C)
        normed = (frames_in.astype(jnp.float32) - mean_chan) * rstd_chan
        scale_tab = jnp.einsum('tzp,zc->tpc', latent_row, w_scale, precision=highest) + b_scale
        shift_tab = jnp.einsum('tzp,zc->tpc', latent_row, w_shift, precision=highest) + b_shift
        scale_map = spread(scale_tab)
        shift_map = spread(shift_tab)
        base_map = normed * gamma + beta
        modulated = base_map * scale_map + shift_map
        squashed = jax.nn.sigmoid(modulated)
        activated = (modulated * squashed).astype(jnp.bfloat16)
        padded = jnp.concatenate([activated[:1], activated[:1], activated], 0)
        padded = jnp.pad(padded, ((0, 0), (1, 1), (1, 1), (0, 0)))
        grads_rows = grads_in.reshape(FRAMES * H * W, CO)
        grad_pad = jnp.pad(grads_in, ((2, 2), (1, 1), (1, 1), (0, 0)))
        extended = jnp.zeros(((FRAMES + 2) * H * W, C), jnp.float32)
        pieces = []
        for frame_tap in range(3):
            for row_tap in range(3):
                for col_tap in range(3):
                    window = padded[frame_tap:frame_tap + FRAMES, row_tap:row_tap + H, col_tap:col_tap + W].reshape(FRAMES * H * W, C)
                    pieces.append(lax.dot_general(window, grads_rows, (((0,), (0,)), ((), ())), preferred_element_type=jnp.float32))
                    source = grad_pad[2 - frame_tap:4 - frame_tap + FRAMES, 2 - row_tap:2 - row_tap + H, 2 - col_tap:2 - col_tap + W].reshape((FRAMES + 2) * H * W, CO)
                    extended = extended + lax.dot_general(source, tap_weights[frame_tap, row_tap, col_tap], (((1,), (1,)), ((), ())), preferred_element_type=jnp.float32)
        kernel_part = jnp.stack(pieces).reshape(27 * C, CO)
        extended = extended.reshape(FRAMES + 2, H, W, C)
        act_grad = extended[2:].at[0].add(extended[0] + extended[1])
        pre_grad = act_grad * squashed * (1.0 + modulated * (1.0 - squashed))
        features_grad = (pre_grad * scale_map * gamma * rstd_chan).astype(jnp.bfloat16)
        scale_pool = pool_blocks(pre_grad * base_map)
        shift_pool = pool_blocks(pre_grad)
        mod_part = jnp.stack([jnp.einsum('tzp,tpc->zc', latent_row, scale_pool, precision=highest),
                              jnp.einsum('tzp,tpc->zc', latent_row, shift_pool, precision=highest)])
        vec_part = jnp.stack([jnp.sum(pre_grad * scale_map * normed, axis=(0, 1, 2)),
                              jnp.sum(pre_grad * scale_map, axis=(0, 1, 2)),
                              jnp.sum(scale_pool, axis=(0, 1)),
                              jnp.sum(shift_pool, axis=(0, 1))])
        latent_sum = jnp.einsum('zc,tpc->tzp', w_scale, scale_pool, precision=highest) + jnp.einsum('zc,tpc->tzp', w_shift, shift_pool, precision=highest)
        latent_part = latent_sum.reshape(LATENT, CZ, 2, LP // 2).transpose(0, 2, 1, 3).reshape(2 * LATENT, CZ, LP // 2)
        return features_grad, kernel_part, mod_part, vec_part, latent_part

    results = lax.map(one_video, (features, grad_out, mean_saved, rstd_saved, latent))
    return (results[0], results[1].sum(axis=0), results[2].sum(axis=0), results[3].sum(axis=0), results[4])
```

```python
import jax
import jax.numpy as jnp
from jax import lax
from jax.experimental import pallas as pl
from jax.experimental.pallas import tpu as pltpu
from jax.sharding import PartitionSpec as P

MESH = pl.DeviceIdType.MESH
F32 = jnp.float32
BF16 = jnp.bfloat16
HIGHEST = lax.Precision.HIGHEST

NX, NY, NZ = 4, 4, 16
NCTX = NY * NZ
H, W, C, CO, CZ, G, LP = 8, 32, 256, 128, 16, 32, 16
PX = H * W
ROWS = 108
TILES = 10
HALF = NZ // 2
WIDE = HALF * 128


def exact(lhs, rhs, dims):
    return lax.dot_general(lhs, rhs, (dims, ((), ())), precision=HIGHEST, preferred_element_type=F32)


def wide_dot(lhs, rhs, dims):
    return lax.dot_general(lhs, rhs, (dims, ((), ())), preferred_element_type=F32)


def body(
    feat_ref, grad_ref, mean_ref, rstd_ref, lat_ref, gamma_ref, beta_ref, ws_ref, bs_ref, wh_ref, bh_ref, kern_hbm,
    fg_ref, kg_ref, mod_ref, vec_ref, lg_ref,
    kern, halo, act, dmod, norm, patch, gsum, agrad, tabs, maps, pools,
    own_a, own_b, cs_a, cs_b, cr_a, cr_b, fs_a, fs_b, fr_a, fr_b, ss_a, ss_b, sr_a, sr_b,
    zo, zs, zr, small, gathered, crossed, final, ls, lr,
    kern_sem, halo_s, halo_r, core_s, core_r, first_s, first_r, second_s, second_r, z_s, z_r,
    small_s, small_r, cross_s, cross_r, final_s, final_r, lat_s, lat_r,
):
    ctx = lax.axis_index("ctx")
    vid = lax.axis_index("vid")
    z, y = lax.div(ctx, NY), lax.rem(ctx, NY)
    x, core = lax.div(vid, 2), lax.rem(vid, 2)
    plane = y * 8 + vid

    def plane_id(p):
        return (z * NY + lax.div(p, 8), lax.rem(p, 8))

    def z_id(zz):
        return (zz * NY + y, vid)

    def x_id(xx):
        return (ctx, 2 * xx + core)

    def y_id(yy):
        return (z * NY + yy, vid)

    mate = (ctx, vid + 1 - 2 * core)
    sharer = (ctx + 1 - 2 * lax.rem(ctx, 2), vid)

    fetch = pltpu.make_async_copy(kern_hbm, kern, kern_sem)
    fetch.start()

    barrier = pltpu.get_barrier_semaphore()

    def greet(device):
        pl.semaphore_signal(barrier, inc=1, device_id=device, device_id_type=MESH)

    @pl.loop(1, 32)
    def _(k):
        greet(plane_id(lax.rem(plane + k, 32)))

    @pl.loop(1, NZ)
    def _(k):
        greet(z_id(lax.rem(z + k, NZ)))

    greet((lax.rem(ctx + 1, NCTX), vid))
    greet((lax.rem(ctx + NCTX - 1, NCTX), vid))

    def remote(src, dst, send, recv, device):
        return pltpu.make_async_remote_copy(
            src_ref=src, dst_ref=dst, send_sem=send, recv_sem=recv, device_id=device, device_id_type=MESH
        )

    pick = (lax.broadcasted_iota(jnp.int32, (G, C), 1) // (C // G) == lax.broadcasted_iota(jnp.int32, (G, C), 0)).astype(F32)
    mean_c = exact(jnp.broadcast_to(mean_ref[...], (8, G)), pick, ((1,), (0,)))[0:1]
    rstd_c = exact(jnp.broadcast_to(rstd_ref[...], (8, G)), pick, ((1,), (0,)))[0:1]
    gamma = gamma_ref[...].reshape(1, C)
    beta = beta_ref[...].reshape(1, C)
    lat = lat_ref[0, lax.div(ctx, 2)]
    scale_tab = exact(lat, ws_ref[...], ((0,), (0,))) + bs_ref[...].reshape(1, C)
    shift_tab = exact(lat, wh_ref[...], ((0,), (0,))) + bh_ref[...].reshape(1, C)
    tabs[...] = scale_tab
    pix = lax.broadcasted_iota(jnp.int32, (2 * W, LP), 0)
    latent_pixel = lax.broadcasted_iota(jnp.int32, (2 * W, LP), 1)
    spread = ((pix // W) * (W // 4) + (pix % W) // 4 == latent_pixel).astype(F32)
    scale_map = exact(spread, scale_tab, ((1,), (0,)))
    shift_map = exact(spread, shift_tab, ((1,), (0,)))
    maps[0] = scale_map.reshape(2, W, C)
    maps[1] = shift_map.reshape(2, W, C)

    @pl.loop(0, 2 * H)
    def _(i):
        f, h = lax.div(i, H), lax.rem(i, H)
        hh = lax.div(h, 4)
        normed = (feat_ref[0, f, h].astype(F32) - mean_c) * rstd_c
        modulated = (normed * gamma + beta) * maps[0, hh] + maps[1, hh]
        s = jax.nn.sigmoid(modulated)
        norm[i] = normed
        dmod[i] = s * (1.0 + modulated * (1.0 - s))
        act[pl.ds(pl.multiple_of(i * W, W), W), :] = (modulated * s).astype(BF16)

    pl.semaphore_wait(barrier, 48)
    before = (lax.rem(ctx + NCTX - 1, NCTX), vid)
    halo_copies = [
        remote(grad_ref.at[0, f], halo.at[f], halo_s.at[f], halo_r.at[f], before) for f in range(2)
    ]
    for copy in halo_copies:
        copy.start()

    col = lax.broadcasted_iota(jnp.int32, (PX, CO), 0) % W

    def lay_patches(f, g):
        for c in range(3):
            if c == 0:
                moved = jnp.where(col == W - 1, 0.0, pltpu.roll(g, PX - 1, 0))
            elif c == 1:
                moved = g
            else:
                moved = jnp.where(col == 0, 0.0, pltpu.roll(g, 1, 0))
            moved = moved.astype(BF16)
            blank = jnp.zeros((W, CO), BF16)
            for b in range(3):
                lanes = slice((b * 3 + c) * CO, (b * 3 + c + 1) * CO)
                base = f * PX
                if b == 0:
                    patch[base : base + PX - W, lanes] = moved[W:]
                    patch[base + PX - W : base + PX, lanes] = blank
                elif b == 1:
                    patch[base : base + PX, lanes] = moved
                else:
                    patch[base : base + W, lanes] = blank
                    patch[base + W : base + PX, lanes] = moved[: PX - W]

    for f in range(2):
        lay_patches(f, grad_ref[0, f].astype(F32).reshape(PX, CO))

    def filter_term(a, first, last, images):
        for bc in range(9):
            lanes = slice(bc * CO, (bc + 1) * CO)
            tap = a * 9 + bc
            yield slice(tap * C, (tap + 1) * C), wide_dot(patch[first:last, lanes], images, ((0,), (0,)))

    def taps(a):
        return jnp.concatenate([kern[(a * 9 + bc) * C : (a * 9 + bc + 1) * C, :] for bc in range(9)], axis=1)

    def input_term(a, first, last):
        return wide_dot(patch[first:last, :], taps(a), ((1,), (1,)))

    gsum[:, 27 * C :] = jnp.zeros((CO, 128), F32)
    for span, term in filter_term(2, 0, 2 * PX, act[...]):
        gsum[:, span] = term
    fetch.wait()
    agrad[...] = input_term(2, 0, 2 * PX)

    for f in range(2):
        halo_copies[f].wait_recv()
        beyond = jnp.where(ctx == NCTX - 1, 0.0, halo[f].astype(F32).reshape(PX, CO))
        lay_patches(2 + f, beyond)
    for a in (1, 0):
        for span, term in filter_term(a, (2 - a) * PX, (4 - a) * PX, act[...]):
            gsum[:, span] = term

    @pl.when(ctx == 0)
    def _():
        for span, term in filter_term(1, 0, PX, act[0:PX]):
            gsum[:, span] += term
        for f in range(2):
            for span, term in filter_term(0, f * PX, (f + 1) * PX, act[0:PX]):
                gsum[:, span] += term

    lane = lax.broadcasted_iota(jnp.int32, (CO, 128), 1)

    def deal(first_z, own, cs, x_major):
        @pl.loop(0, HALF * NY)
        def _(i):
            zl, yy = lax.div(i, NY), lax.rem(i, NY)
            start = ROWS * ((first_z + zl) * NY + yy)
            tile = lax.div(start, 128)
            off = start - tile * 128
            low = gsum[:, pl.ds(pl.multiple_of(tile * 128, 128), 128)]
            high = gsum[:, pl.ds(pl.multiple_of(tile * 128 + 128, 128), 128)]
            turn = lax.rem(128 - off, 128)
            block = jnp.where(lane < 128 - off, pltpu.roll(low, turn, 1), pltpu.roll(high, turn, 1))
            block = block.reshape(NX, 2, 16, 128)
            mine = jnp.where(core == 0, block[:, 0], block[:, 1])
            theirs = jnp.where(core == 0, block[:, 1], block[:, 0]).astype(BF16)
            lanes = pl.ds(pl.multiple_of(zl * 128, 128), 128)
            for xx in range(NX):
                if x_major:
                    own[xx, yy, :, lanes] = mine[xx]
                    cs[xx, yy, :, lanes] = theirs[xx]
                else:
                    own[yy, xx, :, lanes] = mine[xx]
                    cs[yy, xx, :, lanes] = theirs[xx]

    deal(HALF, own_a, cs_a, True)
    core_a = remote(cs_a, cr_a, core_s.at[0], core_r.at[0], mate)
    core_a.start()
    deal(0, own_b, cs_b, False)
    core_b = remote(cs_b, cr_b, core_s.at[1], core_r.at[1], mate)
    core_b.start()

    for a in (1, 0):
        agrad[...] += input_term(a, (2 - a) * PX, (4 - a) * PX)

    @pl.when(ctx == 0)
    def _():
        agrad[0:PX, :] += input_term(1, 0, PX) + input_term(0, 0, PX) + input_term(0, PX, 2 * PX)

    def pair_sum(own, cr, fs):
        @pl.loop(0, 16)
        def _(i):
            j, m = lax.div(i, 4), lax.rem(i, 4)
            total = own[j, m] + cr[j, m].astype(F32)
            own[j, m] = total
            fs[j, m] = total.astype(BF16)

    core_a.wait_recv()
    pair_sum(own_a, cr_a, fs_a)
    first_a = []
    for k in range(1, 4):
        xx = lax.rem(x + k, NX)
        first_a.append(remote(fs_a.at[xx], fr_a.at[k - 1], first_s.at[0, k - 1], first_r.at[0, k - 1], x_id(xx)))
        first_a[-1].start()
    core_b.wait_recv()
    pair_sum(own_b, cr_b, fs_b)
    first_b = []
    for k in range(1, 4):
        yy = lax.rem(y + k, NY)
        first_b.append(remote(fs_b.at[yy], fr_b.at[k - 1], first_s.at[1, k - 1], first_r.at[1, k - 1], y_id(yy)))
        first_b[-1].start()

    pools[...] = jnp.zeros_like(pools)

    @pl.loop(0, 2 * H)
    def _(i):
        f, h = lax.div(i, H), lax.rem(i, H)
        hh = lax.div(h, 4)
        pre = agrad[pl.ds(pl.multiple_of(i * W, W), W), :] * dmod[i]
        fg_ref[0, f, h] = (pre * maps[0, hh] * gamma * rstd_c).astype(BF16)
        pools[0, hh] += pre * norm[i]
        pools[1, hh] += pre

    normed_pool = exact(spread, pools[0].reshape(2 * W, C), ((0,), (0,)))
    shift_pool = exact(spread, pools[1].reshape(2 * W, C), ((0,), (0,)))
    scale_pool = normed_pool * gamma + shift_pool * beta
    tab = tabs[...]
    rows = [
        exact(lat, scale_pool, ((1,), (0,))),
        exact(lat, shift_pool, ((1,), (0,))),
        jnp.concatenate(
            [
                jnp.sum(tab * normed_pool, axis=0, keepdims=True),
                jnp.sum(tab * shift_pool, axis=0, keepdims=True),
                jnp.sum(scale_pool, axis=0, keepdims=True),
                jnp.sum(shift_pool, axis=0, keepdims=True),
                jnp.zeros((4, C), F32),
            ],
            axis=0,
        ),
    ]
    for t in range(TILES):
        block, half = t // 2, t % 2
        source = rows[block // 2][(block % 2) * 8 : (block % 2) * 8 + 8]
        small[t] = source[:, half * 128 : (half + 1) * 128]
    latent_sum = exact(ws_ref[...], scale_pool, ((1,), (1,))) + exact(wh_ref[...], shift_pool, ((1,), (1,)))
    ls[...] = jnp.zeros_like(ls)
    ls[:, 0:LP] = latent_sum
    lat_copy = remote(ls, lr, lat_s, lat_r, sharer)
    lat_copy.start()

    chip = y * NX + x
    owner = jnp.logical_and(core == 0, chip < TILES)

    def tile_plane(t):
        return lax.div(t, NX) * 8 + 2 * lax.rem(t, NX)

    @pl.loop(0, TILES)
    def _(t):
        @pl.when(tile_plane(t) != plane)
        def _():
            remote(small.at[t], gathered.at[plane], small_s.at[t], small_r.at[plane], plane_id(tile_plane(t))).start()

    def line_sum(own, place, fr, ss):
        @pl.loop(0, 4)
        def _(j):
            ss[j] = own[place, j] + fr[0, j].astype(F32) + fr[1, j].astype(F32) + fr[2, j].astype(F32)

    for copy in first_a:
        copy.wait_recv()
    line_sum(own_a, x, fr_a, ss_a)
    second_a = []
    for k in range(1, 4):
        yy = lax.rem(y + k, NY)
        second_a.append(remote(ss_a.at[yy], sr_a.at[k - 1], second_s.at[0, k - 1], second_r.at[0, k - 1], y_id(yy)))
        second_a[-1].start()
    for copy in first_b:
        copy.wait_recv()
    line_sum(own_b, y, fr_b, ss_b)
    second_b = []
    for k in range(1, 4):
        xx = lax.rem(x + k, NX)
        second_b.append(remote(ss_b.at[xx], sr_b.at[k - 1], second_s.at[1, k - 1], second_r.at[1, k - 1], x_id(xx)))
        second_b[-1].start()

    @pl.when(owner)
    def _():
        gathered[plane] = small[chip]

        @pl.loop(1, 32)
        def _(k):
            p = lax.rem(plane + k, 32)
            remote(small.at[0], gathered.at[p], small_s.at[0], small_r.at[p], plane_id(p)).wait_recv()

        crossed[z] = jnp.sum(gathered[...], axis=0)

        @pl.loop(1, NZ)
        def _(k):
            zz = lax.rem(z + k, NZ)
            remote(crossed.at[z], crossed.at[z], cross_s.at[k - 1], cross_r.at[k - 1], z_id(zz)).start()

    def settle(second, ss, place, sr, first_z):
        for copy in second:
            copy.wait_recv()
        total = ss[place] + sr[0] + sr[1] + sr[2]
        for j in range(HALF):
            piece = total[:, j * 128 : (j + 1) * 128]
            zo[first_z + j] = piece
            zs[first_z + j] = piece.astype(BF16)

    settle(second_a, ss_a, y, sr_a, HALF)
    settle(second_b, ss_b, x, sr_b, 0)

    def z_copy(k):
        zz = lax.rem(z + k, NZ)
        return remote(zs.at[zz], zr.at[k - 1], z_s.at[k - 1], z_r.at[k - 1], z_id(zz))

    @pl.loop(1, NZ)
    def _(k):
        z_copy(k).start()

    @pl.when(owner)
    def _():
        @pl.loop(1, NZ)
        def _(k):
            zz = lax.rem(z + NZ - k, NZ)
            remote(crossed.at[z], crossed.at[zz], cross_s.at[k - 1], cross_r.at[k - 1], z_id(zz)).wait_recv()

        final[chip] = jnp.sum(crossed[...], axis=0)

        @pl.loop(1, 32)
        def _(k):
            p = lax.rem(plane + k, 32)
            remote(final.at[chip], final.at[chip], final_s.at[k - 1], final_r.at[chip], plane_id(p)).start()

    @pl.loop(1, NZ)
    def _(k):
        z_copy(k).wait_recv()

    total = zo[z]
    for k in range(NZ - 1):
        total = total + zr[k].astype(F32)
    kg_ref[...] = total.T[:ROWS]

    lat_copy.wait_recv()
    both = ls[...] + lr[...]
    lg_ref[0, 0] = jnp.where(lax.rem(ctx, 2) == 0, both[:, 0 : LP // 2], both[:, LP // 2 : LP])

    @pl.loop(0, TILES)
    def _(t):
        @pl.when(tile_plane(t) != plane)
        def _():
            remote(final.at[t], final.at[t], final_s.at[0], final_r.at[t], mate).wait_recv()

    for t in range(8):
        block, half = t // 2, t % 2
        mod_ref[block // 2, (block % 2) * 8 : (block % 2) * 8 + 8, half * 128 : (half + 1) * 128] = final[t]
    for half in range(2):
        vec_ref[:, half * 128 : (half + 1) * 128] = final[8 + half, 0:4]

    for copy in halo_copies + [core_a, core_b, lat_copy] + first_a + first_b + second_a + second_b:
        copy.wait_send()

    @pl.loop(1, NZ)
    def _(k):
        z_copy(k).wait_send()

    @pl.loop(0, TILES)
    def _(t):
        @pl.when(tile_plane(t) != plane)
        def _():
            remote(small.at[t], gathered.at[plane], small_s.at[t], small_r.at[plane], plane_id(tile_plane(t))).wait_send()

    @pl.when(owner)
    def _():
        @pl.loop(1, NZ)
        def _(k):
            zz = lax.rem(z + k, NZ)
            remote(crossed.at[z], crossed.at[z], cross_s.at[k - 1], cross_r.at[k - 1], z_id(zz)).wait_send()

        @pl.loop(1, 32)
        def _(k):
            p = lax.rem(plane + k, 32)
            remote(final.at[chip], final.at[chip], final_s.at[k - 1], final_r.at[chip], plane_id(p)).wait_send()


def local(*operands):
    vmem = pl.BlockSpec(memory_space=pltpu.VMEM)
    dma = pltpu.SemaphoreType.DMA
    quad = (4, 4, 16, WIDE)
    return pl.pallas_call(
        body,
        out_shape=(
            jax.ShapeDtypeStruct((1, 2, H, W, C), BF16),
            jax.ShapeDtypeStruct((ROWS, 16), F32),
            jax.ShapeDtypeStruct((2, CZ, C), F32),
            jax.ShapeDtypeStruct((4, C), F32),
            jax.ShapeDtypeStruct((1, 1, CZ, LP // 2), F32),
        ),
        in_specs=[vmem] * 11 + [pl.BlockSpec(memory_space=pl.ANY)],
        out_specs=(vmem,) * 5,
        scratch_shapes=[
            pltpu.VMEM((27 * C, CO), BF16),
            pltpu.VMEM((2, H, W, CO), BF16),
            pltpu.VMEM((2 * PX, C), BF16),
            pltpu.VMEM((2 * H, W, C), F32),
            pltpu.VMEM((2 * H, W, C), F32),
            pltpu.VMEM((4 * PX, 9 * CO), BF16),
            pltpu.VMEM((CO, 27 * C + 128), F32),
            pltpu.VMEM((2 * PX, C), F32),
            pltpu.VMEM((LP, C), F32),
            pltpu.VMEM((2, 2, W, C), F32),
            pltpu.VMEM((2, 2, W, C), F32),
            pltpu.VMEM(quad, F32),
            pltpu.VMEM(quad, F32),
            pltpu.VMEM(quad, BF16),
            pltpu.VMEM(quad, BF16),
            pltpu.VMEM(quad, BF16),
            pltpu.VMEM(quad, BF16),
            pltpu.VMEM(quad, BF16),
            pltpu.VMEM(quad, BF16),
            pltpu.VMEM((3,) + quad[1:], BF16),
            pltpu.VMEM((3,) + quad[1:], BF16),
            pltpu.VMEM(quad[1:], F32),
            pltpu.VMEM(quad[1:], F32),
            pltpu.VMEM((3, 16, WIDE), F32),
            pltpu.VMEM((3, 16, WIDE), F32),
            pltpu.VMEM((NZ, 16, 128), F32),
            pltpu.VMEM((NZ, 16, 128), BF16),
            pltpu.VMEM((NZ - 1, 16, 128), BF16),
            pltpu.VMEM((TILES, 8, 128), F32),
            pltpu.VMEM((32, 8, 128), F32),
            pltpu.VMEM((NZ, 8, 128), F32),
            pltpu.VMEM((TILES, 8, 128), F32),
            pltpu.VMEM((16, 128), F32),
            pltpu.VMEM((16, 128), F32),
            dma,
            dma((2,)),
            dma((2,)),
            dma((2,)),
            dma((2,)),
            dma((2, 3)),
            dma((2, 3)),
            dma((2, 3)),
            dma((2, 3)),
            dma((NZ - 1,)),
            dma((NZ - 1,)),
            dma((TILES,)),
            dma((32,)),
            dma((NZ - 1,)),
            dma((NZ - 1,)),
            dma((31,)),
            dma((TILES,)),
            dma,
            dma,
        ],
        compiler_params=pltpu.CompilerParams(
            collective_id=0, has_side_effects=True, vmem_limit_bytes=60 * 1024 * 1024
        ),
    )(*operands)


def solution(mesh):
    placed = (
        P("vid", "ctx", None, None, None),
        P("vid", "ctx", None, None, None),
        P("vid", None),
        P("vid", None),
        P("vid", None, None, None),
        P(),
        P(),
        P(),
        P(),
        P(),
        P(),
        P(),
    )
    return jax.shard_map(
        local,
        mesh=mesh,
        in_specs=placed,
        out_specs=(
            P("vid", "ctx", None, None, None),
            P("ctx", "vid"),
            P(),
            P(),
            P("vid", "ctx", None, None),
        ),
        check_vma=False,
    )
```

```python
import jax
import jax.numpy as jnp
from jax import lax
from jax.experimental import pallas as pl
from jax.experimental.pallas import tpu as pltpu
from jax.sharding import PartitionSpec as P

MESH = pl.DeviceIdType.MESH
F32 = jnp.float32
BF16 = jnp.bfloat16
HIGHEST = lax.Precision.HIGHEST

NX, NY, NZ = 4, 4, 16
NCTX = NY * NZ
H, W, C, CO, CZ, G, LP = 8, 32, 256, 128, 16, 32, 16
PX = H * W
ROWS = 108
TILES = 10
PARTS = ((13, 3, "x"), (11, 2, "y"), (0, 5, "x"), (5, 6, "y"))
EARLY = 11
FAR_FIRST = (8, 7, 9, 6, 10, 5, 11, 4, 12, 3, 13, 2, 14, 1, 15)


def exact(lhs, rhs, dims):
    return lax.dot_general(lhs, rhs, (dims, ((), ())), precision=HIGHEST, preferred_element_type=F32)


def wide_dot(lhs, rhs, dims):
    return lax.dot_general(lhs, rhs, (dims, ((), ())), preferred_element_type=F32)


def body(
    feat_hbm, grad_hbm, mean_hbm, rstd_hbm, lat_hbm, gamma_hbm, beta_hbm, ws_hbm, bs_hbm, wh_hbm, bh_hbm, kern_hbm,
    fg_ref, kg_ref, final, lg_ref,
    feat_ref, grad_ref, mean_ref, rstd_ref, lat_ref, gamma_ref, beta_ref, ws_ref, bs_ref, wh_ref, bh_ref, kern,
    halo, act, dmod, norm, patch, gsum, agrad, tabs, maps, pools,
    zo, zs, zr, small, gathered, crossed, ls, lr,
    load_sems, halo_s, halo_r, core_s, core_r, first_s, first_r, second_s, second_r, z_s, z_r,
    small_s, small_r, cross_s, cross_r, final_s, final_r, lat_s, lat_r, relay,
    *part_refs,
):
    ctx = lax.axis_index("ctx")
    vid = lax.axis_index("vid")
    z, y = lax.div(ctx, NY), lax.rem(ctx, NY)
    x, core = lax.div(vid, 2), lax.rem(vid, 2)
    plane = y * 8 + vid

    def plane_id(p):
        return (z * NY + lax.div(p, 8), lax.rem(p, 8))

    def z_id(zz):
        return (zz * NY + y, vid)

    def x_id(xx):
        return (ctx, 2 * xx + core)

    def y_id(yy):
        return (z * NY + yy, vid)

    mate = (ctx, vid + 1 - 2 * core)
    sharer = (ctx + 1 - 2 * lax.rem(ctx, 2), vid)
    before = (lax.rem(ctx + NCTX - 1, NCTX), vid)
    after = (lax.rem(ctx + 1, NCTX), vid)

    loads = [
        pltpu.make_async_copy(source, target, load_sems.at[n])
        for n, (source, target) in enumerate(
            (
                (lat_hbm, lat_ref),
                (mean_hbm, mean_ref),
                (rstd_hbm, rstd_ref),
                (ws_hbm, ws_ref),
                (wh_hbm, wh_ref),
                (bs_hbm, bs_ref),
                (bh_hbm, bh_ref),
                (gamma_hbm, gamma_ref),
                (beta_hbm, beta_ref),
                (feat_hbm, feat_ref),
                (grad_hbm, grad_ref),
                (kern_hbm, kern),
            )
        )
    ]
    for load in loads:
        load.start()

    barrier = pltpu.get_barrier_semaphore()

    def signal(semaphore, device):
        pl.semaphore_signal(semaphore, inc=1, device_id=device, device_id_type=MESH)

    signal(barrier, before)
    signal(barrier, after)

    @pl.loop(1, 32)
    def _(k):
        signal(barrier, plane_id(lax.rem(plane + k, 32)))

    @pl.loop(1, 5)
    def _(k):
        signal(barrier, z_id(lax.rem(z + k, NZ)))
        signal(barrier, z_id(lax.rem(z + NZ - k, NZ)))

    def remote(src, dst, send, recv, device):
        return pltpu.make_async_remote_copy(
            src_ref=src, dst_ref=dst, send_sem=send, recv_sem=recv, device_id=device, device_id_type=MESH
        )

    for load in loads[:9]:
        load.wait()

    pick = (lax.broadcasted_iota(jnp.int32, (G, C), 1) // (C // G) == lax.broadcasted_iota(jnp.int32, (G, C), 0)).astype(F32)
    saved = jnp.concatenate([mean_ref[...], rstd_ref[...], jnp.zeros((6, G), F32)], axis=0)
    saved = exact(saved, pick, ((1,), (0,)))
    mean_c, rstd_c = saved[0:1], saved[1:2]
    gamma = gamma_ref[...].reshape(1, C)
    beta = beta_ref[...].reshape(1, C)
    here = (lax.broadcasted_iota(jnp.int32, (NCTX // 2, 128), 0) == lax.div(ctx, 2)).astype(F32)
    lat = exact(lat_ref[0].reshape(CZ * LP, NCTX // 2), here, ((1,), (0,))).reshape(CZ, LP, 128)
    corner = lax.broadcasted_iota(jnp.int32, (CZ, LP, 128), 1) == lax.broadcasted_iota(jnp.int32, (CZ, LP, 128), 2)
    lat = jnp.sum(jnp.where(corner, lat, 0.0), axis=1)[:, :LP]
    weights = jnp.concatenate([ws_ref[...], wh_ref[...]], axis=1)
    bias = jnp.concatenate([bs_ref[...].reshape(1, C), bh_ref[...].reshape(1, C)], axis=1)
    both_tabs = exact(lat, weights, ((0,), (0,))) + bias
    tabs[...] = both_tabs[:, :C]
    pix = lax.broadcasted_iota(jnp.int32, (2 * W, LP), 0)
    latent_pixel = lax.broadcasted_iota(jnp.int32, (2 * W, LP), 1)
    spread = ((pix // W) * (W // 4) + (pix % W) // 4 == latent_pixel).astype(F32)
    both_maps = exact(spread, both_tabs, ((1,), (0,)))
    maps[0] = both_maps[:, :C].reshape(2, W, C)
    maps[1] = both_maps[:, C:].reshape(2, W, C)

    loads[9].wait()

    @pl.loop(0, 2 * H, unroll=4)
    def _(i):
        f, h = lax.div(i, H), lax.rem(i, H)
        hh = lax.div(h, 4)
        normed = (feat_ref[0, f, h].astype(F32) - mean_c) * rstd_c
        modulated = (normed * gamma + beta) * maps[0, hh] + maps[1, hh]
        s = jax.nn.sigmoid(modulated)
        norm[i] = normed
        dmod[i] = s * (1.0 + modulated * (1.0 - s))
        act[pl.ds(pl.multiple_of(i * W, W), W), :] = (modulated * s).astype(BF16)

    loads[10].wait()
    pl.semaphore_wait(barrier, 41)
    halo_copies = [
        remote(grad_ref.at[0, f], halo.at[f], halo_s.at[f], halo_r.at[f], before) for f in range(2)
    ]
    for copy in halo_copies:
        copy.start()
    signal(relay, z_id(lax.rem(z + 4, NZ)))
    signal(relay, z_id(lax.rem(z + NZ - 4, NZ)))

    col = lax.broadcasted_iota(jnp.int32, (PX, CO), 0) % W

    def lay_patches(f, g):
        for c in range(3):
            if c == 0:
                moved = jnp.where(col == W - 1, 0.0, pltpu.roll(g, PX - 1, 0))
            elif c == 1:
                moved = g
            else:
                moved = jnp.where(col == 0, 0.0, pltpu.roll(g, 1, 0))
            moved = moved.astype(BF16)
            blank = jnp.zeros((W, CO), BF16)
            for b in range(3):
                lanes = slice((b * 3 + c) * CO, (b * 3 + c + 1) * CO)
                base = f * PX
                if b == 0:
                    patch[base : base + PX - W, lanes] = moved[W:]
                    patch[base + PX - W : base + PX, lanes] = blank
                elif b == 1:
                    patch[base : base + PX, lanes] = moved
                else:
                    patch[base : base + W, lanes] = blank
                    patch[base + W : base + PX, lanes] = moved[: PX - W]

    for f in range(2):
        lay_patches(f, grad_ref[0, f].astype(F32).reshape(PX, CO))

    def filter_term(a, first, last, images):
        for bc in range(9):
            lanes = slice(bc * CO, (bc + 1) * CO)
            tap = a * 9 + bc
            yield slice(tap * C, (tap + 1) * C), wide_dot(patch[first:last, lanes], images, ((0,), (0,)))

    def taps(a):
        return jnp.concatenate([kern[(a * 9 + bc) * C : (a * 9 + bc + 1) * C, :] for bc in range(9)], axis=1)

    def input_term(a, first, last):
        return wide_dot(patch[first:last, :], taps(a), ((1,), (1,)))

    lane = lax.broadcasted_iota(jnp.int32, (CO, 128), 1)
    parts = []
    for n, (first_z, count, axis) in enumerate(PARTS):
        own, cs, cr, fs, fr, ss, sr = part_refs[7 * n : 7 * n + 7]
        places = (x, y) if axis == "x" else (y, x)
        ids = (x_id, y_id) if axis == "x" else (y_id, x_id)
        parts.append(dict(n=n, first_z=first_z, count=count, axis=axis, own=own, cs=cs, cr=cr, fs=fs, fr=fr, ss=ss, sr=sr, places=places, ids=ids))

    def deal(part):
        own, cs = part["own"], part["cs"]

        @pl.loop(0, part["count"] * NY, unroll=4)
        def _(i):
            zl, yy = lax.div(i, NY), lax.rem(i, NY)
            start = ROWS * ((part["first_z"] + zl) * NY + yy)
            tile = lax.div(start, 128)
            off = start - tile * 128
            low = gsum[:, pl.ds(pl.multiple_of(tile * 128, 128), 128)]
            high = gsum[:, pl.ds(pl.multiple_of(tile * 128 + 128, 128), 128)]
            turn = lax.rem(128 - off, 128)
            block = jnp.where(lane < 128 - off, pltpu.roll(low, turn, 1), pltpu.roll(high, turn, 1))
            block = block.reshape(NX, 2, 16, 128)
            mine = jnp.where(core == 0, block[:, 0], block[:, 1])
            theirs = jnp.where(core == 0, block[:, 1], block[:, 0]).astype(BF16)
            lanes = pl.ds(pl.multiple_of(zl * 128, 128), 128)
            for xx in range(NX):
                if part["axis"] == "x":
                    own[xx, yy, :, lanes] = mine[xx]
                    cs[xx, yy, :, lanes] = theirs[xx]
                else:
                    own[yy, xx, :, lanes] = mine[xx]
                    cs[yy, xx, :, lanes] = theirs[xx]

        n = part["n"]
        part["core"] = remote(cs, part["cr"], core_s.at[n], core_r.at[n], mate)
        part["core"].start()

    def first_stage(part):
        own, cr, fs, n = part["own"], part["cr"], part["fs"], part["n"]
        part["core"].wait_recv()

        @pl.loop(0, 16, unroll=2)
        def _(i):
            j, m = lax.div(i, 4), lax.rem(i, 4)
            total = own[j, m] + cr[j, m].astype(F32)
            own[j, m] = total
            fs[j, m] = total.astype(BF16)

        part["first"] = []
        for k in (2, 1, 3):
            there = lax.rem(part["places"][0] + k, 4)
            copy = remote(fs.at[there], part["fr"].at[k - 1], first_s.at[n, k - 1], first_r.at[n, k - 1], part["ids"][0](there))
            copy.start()
            part["first"].append(copy)

    def second_stage(part):
        own, fr, ss, n = part["own"], part["fr"], part["ss"], part["n"]
        for copy in part["first"]:
            copy.wait_recv()
        place = part["places"][0]
        for j in range(4):
            ss[j] = own[place, j] + fr[0, j].astype(F32) + fr[1, j].astype(F32) + fr[2, j].astype(F32)
        part["second"] = []
        for k in (2, 1, 3):
            there = lax.rem(part["places"][1] + k, 4)
            copy = remote(ss.at[there], part["sr"].at[k - 1], second_s.at[n, k - 1], second_r.at[n, k - 1], part["ids"][1](there))
            copy.start()
            part["second"].append(copy)

    def settle(part):
        for copy in part["second"]:
            copy.wait_recv()
        sr = part["sr"]
        total = part["ss"][part["places"][1]] + sr[0] + sr[1] + sr[2]
        for j in range(part["count"]):
            piece = total[:, j * 128 : (j + 1) * 128]
            zo[part["first_z"] + j] = piece
            zs[part["first_z"] + j] = piece.astype(BF16)

    def z_copy(k):
        zz = lax.rem(z + k, NZ)
        return zz, remote(zs.at[zz], zr.at[k - 1], z_s.at[k - 1], z_r.at[k - 1], z_id(zz))

    def send_along_z(early):
        for k in FAR_FIRST:
            zz, copy = z_copy(k)

            @pl.when(zz >= EARLY if early else zz < EARLY)
            def _():
                copy.start()

    gsum[:, 27 * C :] = jnp.zeros((CO, 128), F32)
    for span, term in filter_term(2, 0, 2 * PX, act[...]):
        gsum[:, span] = term
    deal(parts[0])
    deal(parts[1])
    loads[11].wait()
    agrad[...] = input_term(2, 0, 2 * PX)
    first_stage(parts[0])
    first_stage(parts[1])

    for f in range(2):
        halo_copies[f].wait_recv()
        beyond = jnp.where(ctx == NCTX - 1, 0.0, halo[f].astype(F32).reshape(PX, CO))
        lay_patches(2 + f, beyond)
    for a in (1, 0):
        for span, term in filter_term(a, (2 - a) * PX, (4 - a) * PX, act[...]):
            gsum[:, span] = term

    @pl.when(ctx == 0)
    def _():
        for span, term in filter_term(1, 0, PX, act[0:PX]):
            gsum[:, span] += term
        for f in range(2):
            for span, term in filter_term(0, f * PX, (f + 1) * PX, act[0:PX]):
                gsum[:, span] += term

    deal(parts[2])
    deal(parts[3])
    second_stage(parts[0])
    second_stage(parts[1])
    first_stage(parts[2])
    first_stage(parts[3])

    for a in (1, 0):
        agrad[...] += input_term(a, (2 - a) * PX, (4 - a) * PX)

    @pl.when(ctx == 0)
    def _():
        agrad[0:PX, :] += input_term(1, 0, PX) + input_term(0, 0, PX) + input_term(0, PX, 2 * PX)

    pools[...] = jnp.zeros_like(pools)

    @pl.loop(0, 2 * H, unroll=4)
    def _(i):
        f, h = lax.div(i, H), lax.rem(i, H)
        hh = lax.div(h, 4)
        pre = agrad[pl.ds(pl.multiple_of(i * W, W), W), :] * dmod[i]
        fg_ref[0, f, h] = (pre * maps[0, hh] * gamma * rstd_c).astype(BF16)
        pools[0, hh] += pre * norm[i]
        pools[1, hh] += pre

    normed_pool = exact(spread, pools[0].reshape(2 * W, C), ((0,), (0,)))
    shift_pool = exact(spread, pools[1].reshape(2 * W, C), ((0,), (0,)))
    scale_pool = normed_pool * gamma + shift_pool * beta
    tab = tabs[...]
    rows = [
        exact(lat, scale_pool, ((1,), (0,))),
        exact(lat, shift_pool, ((1,), (0,))),
        jnp.concatenate(
            [
                jnp.sum(tab * normed_pool, axis=0, keepdims=True),
                jnp.sum(tab * shift_pool, axis=0, keepdims=True),
                jnp.sum(scale_pool, axis=0, keepdims=True),
                jnp.sum(shift_pool, axis=0, keepdims=True),
                jnp.zeros((4, C), F32),
            ],
            axis=0,
        ),
    ]
    for t in range(TILES):
        block, half = t // 2, t % 2
        source = rows[block // 2][(block % 2) * 8 : (block % 2) * 8 + 8]
        small[t] = source[:, half * 128 : (half + 1) * 128]

    chip = y * NX + x
    owner = jnp.logical_and(core == 0, chip < TILES)

    def tile_plane(t):
        return lax.div(t, NX) * 8 + 2 * lax.rem(t, NX)

    @pl.loop(0, TILES)
    def _(t):
        @pl.when(tile_plane(t) != plane)
        def _():
            remote(small.at[t], gathered.at[plane], small_s.at[t], small_r.at[plane], plane_id(tile_plane(t))).start()

    latent_sum = exact(scale_pool, ws_ref[...], ((1,), (1,))) + exact(shift_pool, wh_ref[...], ((1,), (1,)))
    ls[...] = jnp.zeros_like(ls)
    ls[:, 0:CZ] = latent_sum
    lat_copy = remote(ls, lr, lat_s, lat_r, sharer)
    lat_copy.start()

    settle(parts[0])
    settle(parts[1])
    pl.semaphore_wait(relay, 2)
    send_along_z(True)
    second_stage(parts[2])
    second_stage(parts[3])

    @pl.when(owner)
    def _():
        gathered[plane] = small[chip]

        @pl.loop(1, 32)
        def _(k):
            p = lax.rem(plane + k, 32)
            remote(small.at[0], gathered.at[p], small_s.at[0], small_r.at[p], plane_id(p)).wait_recv()

        crossed[z] = jnp.sum(gathered[...], axis=0)

        @pl.loop(1, NZ)
        def _(k):
            zz = lax.rem(z + k, NZ)
            remote(crossed.at[z], crossed.at[z], cross_s.at[k - 1], cross_r.at[k - 1], z_id(zz)).start()

    settle(parts[2])
    settle(parts[3])
    send_along_z(False)

    @pl.when(owner)
    def _():
        @pl.loop(1, NZ)
        def _(k):
            zz = lax.rem(z + NZ - k, NZ)
            remote(crossed.at[z], crossed.at[zz], cross_s.at[k - 1], cross_r.at[k - 1], z_id(zz)).wait_recv()

        final[chip] = jnp.sum(crossed[...], axis=0)

        @pl.loop(1, 32)
        def _(k):
            p = lax.rem(plane + k, 32)
            remote(final.at[chip], final.at[chip], final_s.at[k - 1], final_r.at[chip], plane_id(p)).start()

    lat_copy.wait_recv()
    half = pl.ds(pl.multiple_of(lax.rem(ctx, 2) * 8, 8), 8)
    lg_ref[...] = ls[half, :] + lr[half, :]

    for k in range(1, NZ):
        z_copy(k)[1].wait_recv()
    total = zo[z]
    for k in range(NZ - 1):
        total = total + zr[k].astype(F32)
    kg_ref[...] = total

    @pl.loop(0, TILES)
    def _(t):
        @pl.when(tile_plane(t) != plane)
        def _():
            remote(final.at[t], final.at[t], final_s.at[0], final_r.at[t], mate).wait_recv()

    for copy in halo_copies + [lat_copy]:
        copy.wait_send()
    for part in parts:
        for copy in [part["core"]] + part["first"] + part["second"]:
            copy.wait_send()
    for k in range(1, NZ):
        z_copy(k)[1].wait_send()

    @pl.loop(0, TILES)
    def _(t):
        @pl.when(tile_plane(t) != plane)
        def _():
            remote(small.at[t], gathered.at[plane], small_s.at[t], small_r.at[plane], plane_id(tile_plane(t))).wait_send()

    @pl.when(owner)
    def _():
        @pl.loop(1, NZ)
        def _(k):
            zz = lax.rem(z + k, NZ)
            remote(crossed.at[z], crossed.at[z], cross_s.at[k - 1], cross_r.at[k - 1], z_id(zz)).wait_send()

        @pl.loop(1, 32)
        def _(k):
            p = lax.rem(plane + k, 32)
            remote(final.at[chip], final.at[chip], final_s.at[k - 1], final_r.at[chip], plane_id(p)).wait_send()


def finish(fg_in, kg_in, sums, lg_in, fg_ref, kg_ref, mod_ref, vec_ref, lg_ref):
    fg_ref[...] = fg_in[...]
    kg_ref[...] = kg_in[:, 0:ROWS]
    for t in range(8):
        block, half = t // 2, t % 2
        mod_ref[block // 2, (block % 2) * 8 : (block % 2) * 8 + 8, half * 128 : (half + 1) * 128] = sums[t]
    for half in range(2):
        vec_ref[:, half * 128 : (half + 1) * 128] = sums[8 + half, 0:4]
    lg_ref[0, 0] = lg_in[:, 0:CZ]


def local(features, grad_out, mean_saved, rstd_saved, latent, *others):
    operands = (features, grad_out, mean_saved, rstd_saved, jnp.transpose(latent, (0, 2, 3, 1))) + others
    vmem = pl.BlockSpec(memory_space=pltpu.VMEM)
    dma = pltpu.SemaphoreType.DMA
    buffers = []
    for _, count, _ in PARTS:
        wide = (16, count * 128)
        buffers += [
            pltpu.VMEM((4, 4) + wide, F32),
            pltpu.VMEM((4, 4) + wide, BF16),
            pltpu.VMEM((4, 4) + wide, BF16),
            pltpu.VMEM((4, 4) + wide, BF16),
            pltpu.VMEM((3, 4) + wide, BF16),
            pltpu.VMEM((4,) + wide, F32),
            pltpu.VMEM((3,) + wide, F32),
        ]
    parts = len(PARTS)
    partial = pl.pallas_call(
        body,
        out_shape=(
            jax.ShapeDtypeStruct((1, 2, H, W, C), BF16),
            jax.ShapeDtypeStruct((16, 128), F32),
            jax.ShapeDtypeStruct((TILES, 8, 128), F32),
            jax.ShapeDtypeStruct((8, 128), F32),
        ),
        in_specs=[pl.BlockSpec(memory_space=pltpu.HBM)] * 12,
        out_specs=(vmem,) * 4,
        scratch_shapes=[
            pltpu.VMEM((1, 2, H, W, C), BF16),
            pltpu.VMEM((1, 2, H, W, CO), BF16),
            pltpu.VMEM((1, G), F32),
            pltpu.VMEM((1, G), F32),
            pltpu.VMEM((1, CZ, LP, NCTX // 2), F32),
            pltpu.VMEM((C,), F32),
            pltpu.VMEM((C,), F32),
            pltpu.VMEM((CZ, C), F32),
            pltpu.VMEM((C,), F32),
            pltpu.VMEM((CZ, C), F32),
            pltpu.VMEM((C,), F32),
            pltpu.VMEM((27 * C, CO), BF16),
            pltpu.VMEM((2, H, W, CO), BF16),
            pltpu.VMEM((2 * PX, C), BF16),
            pltpu.VMEM((2 * H, W, C), F32),
            pltpu.VMEM((2 * H, W, C), F32),
            pltpu.VMEM((4 * PX, 9 * CO), BF16),
            pltpu.VMEM((CO, 27 * C + 128), F32),
            pltpu.VMEM((2 * PX, C), F32),
            pltpu.VMEM((LP, C), F32),
            pltpu.VMEM((2, 2, W, C), F32),
            pltpu.VMEM((2, 2, W, C), F32),
            pltpu.VMEM((NZ, 16, 128), F32),
            pltpu.VMEM((NZ, 16, 128), BF16),
            pltpu.VMEM((NZ - 1, 16, 128), BF16),
            pltpu.VMEM((TILES, 8, 128), F32),
            pltpu.VMEM((32, 8, 128), F32),
            pltpu.VMEM((NZ, 8, 128), F32),
            pltpu.VMEM((16, 128), F32),
            pltpu.VMEM((16, 128), F32),
            dma((12,)),
            dma((2,)),
            dma((2,)),
            dma((parts,)),
            dma((parts,)),
            dma((parts, 3)),
            dma((parts, 3)),
            dma((parts, 3)),
            dma((parts, 3)),
            dma((NZ - 1,)),
            dma((NZ - 1,)),
            dma((TILES,)),
            dma((32,)),
            dma((NZ - 1,)),
            dma((NZ - 1,)),
            dma((31,)),
            dma((TILES,)),
            dma,
            dma,
            pltpu.SemaphoreType.REGULAR,
        ]
        + buffers,
        compiler_params=pltpu.CompilerParams(
            collective_id=0, has_side_effects=True, vmem_limit_bytes=36 * 1024 * 1024
        ),
    )(*(pltpu.with_memory_space_constraint(value, pltpu.HBM) for value in operands))
    fg, kg, mod, vec, lg = pl.pallas_call(
        finish,
        out_shape=(
            jax.ShapeDtypeStruct((1, 2, H, W, C), BF16),
            jax.ShapeDtypeStruct((16, ROWS), F32),
            jax.ShapeDtypeStruct((2, CZ, C), F32),
            jax.ShapeDtypeStruct((4, C), F32),
            jax.ShapeDtypeStruct((1, 1, LP // 2, CZ), F32),
        ),
        in_specs=[vmem] * 4,
        out_specs=(vmem,) * 5,
        compiler_params=pltpu.CompilerParams(vmem_limit_bytes=8 * 1024 * 1024),
    )(*partial)
    return fg, kg.T, mod, vec, jnp.swapaxes(lg, 2, 3)


def solution(mesh):
    placed = (
        P("vid", "ctx", None, None, None),
        P("vid", "ctx", None, None, None),
        P("vid", None),
        P("vid", None),
        P("vid", None, None, None),
        P(),
        P(),
        P(),
        P(),
        P(),
        P(),
        P(),
    )
    return jax.shard_map(
        local,
        mesh=mesh,
        in_specs=placed,
        out_specs=(
            P("vid", "ctx", None, None, None),
            P("ctx", "vid"),
            P(),
            P(),
            P("vid", "ctx", None, None),
        ),
        check_vma=False,
    )
```

```python
import jax
import jax.numpy as jnp
from jax import lax
from jax.experimental import pallas as pl
from jax.experimental.pallas import tpu as pltpu
from jax.sharding import PartitionSpec as P

MESH = pl.DeviceIdType.MESH
F32 = jnp.float32
BF16 = jnp.bfloat16
HIGHEST = lax.Precision.HIGHEST

NX, NY, NZ = 4, 4, 16
NCTX = NY * NZ
H, W, C, CO, CZ, G, LP = 8, 32, 256, 128, 16, 32, 16
PX = H * W
ROWS = 108
TILES = 10
PARTS = ((11, 5, "x"), (9, 2, "x"), (6, 3, "y"), (0, 3, "x"), (3, 3, "y"))
GROUPS = ((11, 16), (6, 11), (0, 6))
FAR_FIRST = (8, 7, 9, 6, 10, 5, 11, 4, 12, 3, 13, 2, 14, 1, 15)


def span_of(first_z, count):
    low = ROWS * NY * first_z // 128
    high = -(-ROWS * NY * (first_z + count) // 128)
    return low * 128, high * 128


def exact(lhs, rhs, dims):
    return lax.dot_general(lhs, rhs, (dims, ((), ())), precision=HIGHEST, preferred_element_type=F32)


def wide_dot(lhs, rhs, dims):
    return lax.dot_general(lhs, rhs, (dims, ((), ())), preferred_element_type=F32)


def body(
    feat_hbm, grad_hbm, mean_hbm, rstd_hbm, lat_hbm, gamma_hbm, beta_hbm, ws_hbm, bs_hbm, wh_hbm, bh_hbm, kern_hbm,
    fg_ref, kg_ref, final, lg_ref,
    feat_ref, grad_ref, mean_ref, rstd_ref, lat_ref, gamma_ref, beta_ref, ws_ref, bs_ref, wh_ref, bh_ref, kern,
    halo, act, dmod, norm, patch, gsum, agrad, tabs, maps, pools,
    zo, zs, zr, small, gathered, crossed, ls, lr,
    load_sems, halo_s, halo_r, core_s, core_r, first_s, first_r, second_s, second_r, z_s, z_r,
    small_s, small_r, cross_s, cross_r, final_s, final_r, lat_s, lat_r, relay, relay_far,
    *part_refs,
):
    ctx = lax.axis_index("ctx")
    vid = lax.axis_index("vid")
    z, y = lax.div(ctx, NY), lax.rem(ctx, NY)
    x, core = lax.div(vid, 2), lax.rem(vid, 2)
    plane = y * 8 + vid

    def plane_id(p):
        return (z * NY + lax.div(p, 8), lax.rem(p, 8))

    def z_id(zz):
        return (zz * NY + y, vid)

    def x_id(xx):
        return (ctx, 2 * xx + core)

    def y_id(yy):
        return (z * NY + yy, vid)

    mate = (ctx, vid + 1 - 2 * core)
    sharer = (ctx + 1 - 2 * lax.rem(ctx, 2), vid)
    before = (lax.rem(ctx + NCTX - 1, NCTX), vid)
    after = (lax.rem(ctx + 1, NCTX), vid)

    loads = [
        pltpu.make_async_copy(source, target, load_sems.at[n])
        for n, (source, target) in enumerate(
            (
                (lat_hbm, lat_ref),
                (mean_hbm, mean_ref),
                (rstd_hbm, rstd_ref),
                (ws_hbm, ws_ref),
                (wh_hbm, wh_ref),
                (bs_hbm, bs_ref),
                (bh_hbm, bh_ref),
                (gamma_hbm, gamma_ref),
                (beta_hbm, beta_ref),
                (feat_hbm, feat_ref),
                (grad_hbm, grad_ref),
                (kern_hbm, kern),
            )
        )
    ]
    for load in loads:
        load.start()

    barrier = pltpu.get_barrier_semaphore()

    def signal(semaphore, device):
        pl.semaphore_signal(semaphore, inc=1, device_id=device, device_id_type=MESH)

    signal(barrier, before)
    signal(barrier, after)
    signal(barrier, mate)
    for k in range(1, 4):
        signal(barrier, x_id(lax.rem(x + k, NX)))
        signal(barrier, y_id(lax.rem(y + k, NY)))
    for k in (2, NZ - 2, 1, NZ - 1):
        signal(barrier, z_id(lax.rem(z + k, NZ)))

    def remote(src, dst, send, recv, device):
        return pltpu.make_async_remote_copy(
            src_ref=src, dst_ref=dst, send_sem=send, recv_sem=recv, device_id=device, device_id_type=MESH
        )

    pl.semaphore_wait(barrier, 13)
    halo_copies = [
        remote(grad_hbm.at[0, f], halo.at[f], halo_s.at[f], halo_r.at[f], before) for f in range(2)
    ]
    for copy in halo_copies:
        copy.start()
    signal(relay, z_id(lax.rem(z + 2, NZ)))
    signal(relay, z_id(lax.rem(z + NZ - 2, NZ)))

    for load in loads[:9]:
        load.wait()

    pick = (lax.broadcasted_iota(jnp.int32, (G, C), 1) // (C // G) == lax.broadcasted_iota(jnp.int32, (G, C), 0)).astype(F32)
    saved = jnp.concatenate([mean_ref[...], rstd_ref[...], jnp.zeros((6, G), F32)], axis=0)
    saved = exact(saved, pick, ((1,), (0,)))
    mean_c, rstd_c = saved[0:1], saved[1:2]
    gamma = gamma_ref[...].reshape(1, C)
    beta = beta_ref[...].reshape(1, C)
    here = (lax.broadcasted_iota(jnp.int32, (NCTX // 2, 128), 0) == lax.div(ctx, 2)).astype(F32)
    lat = exact(lat_ref[0].reshape(CZ * LP, NCTX // 2), here, ((1,), (0,))).reshape(CZ, LP, 128)
    corner = lax.broadcasted_iota(jnp.int32, (CZ, LP, 128), 1) == lax.broadcasted_iota(jnp.int32, (CZ, LP, 128), 2)
    lat = jnp.sum(jnp.where(corner, lat, 0.0), axis=1)[:, :LP]
    weights = jnp.concatenate([ws_ref[...], wh_ref[...]], axis=1)
    bias = jnp.concatenate([bs_ref[...].reshape(1, C), bh_ref[...].reshape(1, C)], axis=1)
    both_tabs = exact(lat, weights, ((0,), (0,))) + bias
    tabs[...] = both_tabs[:, :C]
    pix = lax.broadcasted_iota(jnp.int32, (2 * W, LP), 0)
    latent_pixel = lax.broadcasted_iota(jnp.int32, (2 * W, LP), 1)
    spread = ((pix // W) * (W // 4) + (pix % W) // 4 == latent_pixel).astype(F32)
    both_maps = exact(spread, both_tabs, ((1,), (0,)))
    maps[0] = both_maps[:, :C].reshape(2, W, C)
    maps[1] = both_maps[:, C:].reshape(2, W, C)

    loads[9].wait()

    @pl.loop(0, 2 * H, unroll=4)
    def _(i):
        f, h = lax.div(i, H), lax.rem(i, H)
        hh = lax.div(h, 4)
        normed = (feat_ref[0, f, h].astype(F32) - mean_c) * rstd_c
        modulated = (normed * gamma + beta) * maps[0, hh] + maps[1, hh]
        s = jax.nn.sigmoid(modulated)
        norm[i] = normed
        dmod[i] = s * (1.0 + modulated * (1.0 - s))
        act[pl.ds(pl.multiple_of(i * W, W), W), :] = (modulated * s).astype(BF16)

    loads[10].wait()
    col = lax.broadcasted_iota(jnp.int32, (PX, CO), 0) % W

    def lay_patches(f, g):
        for c in range(3):
            if c == 0:
                moved = jnp.where(col == W - 1, 0.0, pltpu.roll(g, PX - 1, 0))
            elif c == 1:
                moved = g
            else:
                moved = jnp.where(col == 0, 0.0, pltpu.roll(g, 1, 0))
            moved = moved.astype(BF16)
            blank = jnp.zeros((W, CO), BF16)
            for b in range(3):
                lanes = slice((b * 3 + c) * CO, (b * 3 + c + 1) * CO)
                base = f * PX
                if b == 0:
                    patch[base : base + PX - W, lanes] = moved[W:]
                    patch[base + PX - W : base + PX, lanes] = blank
                elif b == 1:
                    patch[base : base + PX, lanes] = moved
                else:
                    patch[base : base + W, lanes] = blank
                    patch[base + W : base + PX, lanes] = moved[: PX - W]

    for f in range(2):
        lay_patches(f, grad_ref[0, f].astype(F32).reshape(PX, CO))

    def filter_term(a, first, last, images):
        for bc in range(9):
            lanes = slice(bc * CO, (bc + 1) * CO)
            tap = a * 9 + bc
            yield slice(tap * C, (tap + 1) * C), wide_dot(patch[first:last, lanes], images, ((0,), (0,)))

    def taps(a):
        return jnp.concatenate([kern[(a * 9 + bc) * C : (a * 9 + bc + 1) * C, :] for bc in range(9)], axis=1)

    def input_term(a, first, last):
        return wide_dot(patch[first:last, :], taps(a), ((1,), (1,)))

    lane = lax.broadcasted_iota(jnp.int32, (16, 128), 1)
    parts = []
    refs = list(part_refs)
    for n, (first_z, count, axis) in enumerate(PARTS):
        places = (x, y) if axis == "x" else (y, x)
        ids = (x_id, y_id) if axis == "x" else (y_id, x_id)
        names = ("own", "cs", "cr", "fs", "fr", "ss", "sr")
        part = dict(zip(names, refs[:7]))
        del refs[:7]
        part.update(n=n, first_z=first_z, count=count, axis=axis, places=places, ids=ids)
        parts.append(part)

    def owned(place, parity):
        return pl.ds(pl.multiple_of((2 * place + parity) * 16, 16), 16)

    def shifted(low, high, off, turn):
        return jnp.where(lane < 128 - off, pltpu.roll(low, turn, 1), pltpu.roll(high, turn, 1))

    def deal(part):
        own, cs, n = part["own"], part["cs"], part["n"]
        if part["axis"] == "x":
            low, high = span_of(part["first_z"], part["count"])
            for xx in range(NX):
                cs[xx] = gsum[owned(xx, 1 - core), low:high].astype(BF16)
        else:

            @pl.loop(0, part["count"] * NY, unroll=4)
            def _(i):
                zl, yy = lax.div(i, NY), lax.rem(i, NY)
                start = ROWS * ((part["first_z"] + zl) * NY + yy)
                tile = lax.div(start, 128)
                off = start - tile * 128
                turn = lax.rem(128 - off, 128)
                first = pl.ds(pl.multiple_of(tile * 128, 128), 128)
                second = pl.ds(pl.multiple_of(tile * 128 + 128, 128), 128)
                lanes = pl.ds(pl.multiple_of(zl * 128, 128), 128)
                for xx in range(NX):
                    mine, theirs = owned(xx, core), owned(xx, 1 - core)
                    cs[yy, xx, :, lanes] = shifted(gsum[theirs, first], gsum[theirs, second], off, turn).astype(BF16)
                    own[yy, xx, :, lanes] = shifted(gsum[mine, first], gsum[mine, second], off, turn)

        part["core"] = remote(cs, part["cr"], core_s.at[n], core_r.at[n], mate)
        part["core"].start()

    def first_stage(part):
        own, cr, fs, n = part["own"], part["cr"], part["fs"], part["n"]
        part["core"].wait_recv()
        if part["axis"] == "x":
            low, high = span_of(part["first_z"], part["count"])
            for xx in range(NX):
                fs[xx] = (gsum[owned(xx, core), low:high] + cr[xx].astype(F32)).astype(BF16)
        else:

            @pl.loop(0, 16, unroll=2)
            def _(i):
                j, m = lax.div(i, 4), lax.rem(i, 4)
                total = own[j, m] + cr[j, m].astype(F32)
                own[j, m] = total
                fs[j, m] = total.astype(BF16)

        part["first"] = []
        for k in (2, 1, 3):
            there = lax.rem(part["places"][0] + k, 4)
            copy = remote(fs.at[there], part["fr"].at[k - 1], first_s.at[n, k - 1], first_r.at[n, k - 1], part["ids"][0](there))
            copy.start()
            part["first"].append(copy)

    def second_stage(part):
        own, cr, fr, ss, n = part["own"], part["cr"], part["fr"], part["ss"], part["n"]
        for copy in part["first"]:
            copy.wait_recv()
        if part["axis"] == "x":
            low, high = span_of(part["first_z"], part["count"])
            width = high - low
            own[:, 0:width] = (
                gsum[owned(x, core), low:high]
                + cr[x].astype(F32)
                + fr[0].astype(F32)
                + fr[1].astype(F32)
                + fr[2].astype(F32)
            )
            own[:, width:] = jnp.zeros((16, 128), F32)
            for i in range(part["count"] * NY):
                zl, yy = i // NY, i % NY
                start = ROWS * (part["first_z"] * NY + i) - low
                tile, off = start // 128, start % 128
                block = own[:, tile * 128 : tile * 128 + 128]
                if off:
                    block = shifted(block, own[:, tile * 128 + 128 : tile * 128 + 256], off, 128 - off)
                ss[yy, :, zl * 128 : zl * 128 + 128] = block
        else:
            for j in range(4):
                ss[j] = own[y, j] + fr[0, j].astype(F32) + fr[1, j].astype(F32) + fr[2, j].astype(F32)
        part["second"] = []
        for k in (2, 1, 3):
            there = lax.rem(part["places"][1] + k, 4)
            copy = remote(ss.at[there], part["sr"].at[k - 1], second_s.at[n, k - 1], second_r.at[n, k - 1], part["ids"][1](there))
            copy.start()
            part["second"].append(copy)

    def settle(part):
        for copy in part["second"]:
            copy.wait_recv()
        sr = part["sr"]
        total = part["ss"][part["places"][1]] + sr[0] + sr[1] + sr[2]
        for j in range(part["count"]):
            piece = total[:, j * 128 : (j + 1) * 128]
            zo[part["first_z"] + j] = piece
            zs[part["first_z"] + j] = piece.astype(BF16)

    def z_copy(k):
        zz = lax.rem(z + k, NZ)
        return zz, remote(zs.at[zz], zr.at[k - 1], z_s.at[k - 1], z_r.at[k - 1], z_id(zz))

    def send_along_z(first, last):
        for k in FAR_FIRST:
            zz, copy = z_copy(k)

            @pl.when(jnp.logical_and(zz >= first, zz < last))
            def _():
                copy.start()

    gsum[:, 27 * C :] = jnp.zeros((CO, 128), F32)
    for span, term in filter_term(2, 0, 2 * PX, act[...]):
        gsum[:, span] = term
    deal(parts[0])
    for span, term in filter_term(1, PX, 2 * PX, act[0:PX]):
        gsum[:, span] = term
    loads[11].wait()
    agrad[...] = input_term(2, 0, 2 * PX)
    agrad[0:PX, :] += input_term(1, PX, 2 * PX)
    pl.semaphore_wait(relay, 2)
    signal(relay_far, z_id(lax.rem(z + 4, NZ)))
    signal(relay_far, z_id(lax.rem(z + NZ - 4, NZ)))
    first_stage(parts[0])

    @pl.when(ctx == 0)
    def _():
        for span, term in filter_term(1, 0, PX, act[0:PX]):
            gsum[:, span] += term
        for span, term in filter_term(0, 0, PX, act[0:PX]):
            gsum[:, span] = term
        for span, term in filter_term(0, PX, 2 * PX, act[0:PX]):
            gsum[:, span] += term
        agrad[0:PX, :] += input_term(1, 0, PX) + input_term(0, 0, PX) + input_term(0, PX, 2 * PX)

    @pl.when(ctx != 0)
    def _():
        gsum[:, 0 : 9 * C] = jnp.zeros((CO, 9 * C), F32)

    def take_halo(f):
        halo_copies[f].wait_recv()
        lay_patches(2 + f, jnp.where(ctx == NCTX - 1, 0.0, halo[f].astype(F32).reshape(PX, CO)))

    take_halo(0)
    for span, term in filter_term(1, 2 * PX, 3 * PX, act[PX : 2 * PX]):
        gsum[:, span] += term
    deal(parts[1])
    deal(parts[2])
    take_halo(1)
    for span, term in filter_term(0, 2 * PX, 4 * PX, act[...]):
        gsum[:, span] += term
    deal(parts[3])
    deal(parts[4])
    for part in parts[1:]:
        first_stage(part)

    agrad[...] += input_term(0, 2 * PX, 4 * PX)
    agrad[PX : 2 * PX, :] += input_term(1, 2 * PX, 3 * PX)

    pools[...] = jnp.zeros_like(pools)

    @pl.loop(0, 2 * H, unroll=4)
    def _(i):
        f, h = lax.div(i, H), lax.rem(i, H)
        hh = lax.div(h, 4)
        pre = agrad[pl.ds(pl.multiple_of(i * W, W), W), :] * dmod[i]
        fg_ref[0, f, h] = (pre * maps[0, hh] * gamma * rstd_c).astype(BF16)
        pools[0, hh] += pre * norm[i]
        pools[1, hh] += pre

    normed_pool = exact(spread, pools[0].reshape(2 * W, C), ((0,), (0,)))
    shift_pool = exact(spread, pools[1].reshape(2 * W, C), ((0,), (0,)))
    scale_pool = normed_pool * gamma + shift_pool * beta
    tab = tabs[...]
    rows = [
        exact(lat, scale_pool, ((1,), (0,))),
        exact(lat, shift_pool, ((1,), (0,))),
        jnp.concatenate(
            [
                jnp.sum(tab * normed_pool, axis=0, keepdims=True),
                jnp.sum(tab * shift_pool, axis=0, keepdims=True),
                jnp.sum(scale_pool, axis=0, keepdims=True),
                jnp.sum(shift_pool, axis=0, keepdims=True),
                jnp.zeros((4, C), F32),
            ],
            axis=0,
        ),
    ]
    for t in range(TILES):
        block, half = t // 2, t % 2
        source = rows[block // 2][(block % 2) * 8 : (block % 2) * 8 + 8]
        small[t] = source[:, half * 128 : (half + 1) * 128]

    chip = y * NX + x
    owner = jnp.logical_and(core == 0, chip < TILES)

    def tile_plane(t):
        return lax.div(t, NX) * 8 + 2 * lax.rem(t, NX)

    second_stage(parts[0])

    @pl.loop(0, TILES)
    def _(t):
        @pl.when(tile_plane(t) != plane)
        def _():
            remote(small.at[t], gathered.at[plane], small_s.at[t], small_r.at[plane], plane_id(tile_plane(t))).start()

    latent_sum = exact(scale_pool, ws_ref[...], ((1,), (1,))) + exact(shift_pool, wh_ref[...], ((1,), (1,)))
    ls[...] = jnp.zeros_like(ls)
    ls[:, 0:CZ] = latent_sum
    lat_copy = remote(ls, lr, lat_s, lat_r, sharer)
    lat_copy.start()

    second_stage(parts[1])
    second_stage(parts[2])
    second_stage(parts[3])
    second_stage(parts[4])
    settle(parts[0])
    pl.semaphore_wait(relay_far, 2)
    send_along_z(*GROUPS[0])

    @pl.when(owner)
    def _():
        gathered[plane] = small[chip]

        @pl.loop(1, 32)
        def _(k):
            p = lax.rem(plane + k, 32)
            remote(small.at[0], gathered.at[p], small_s.at[0], small_r.at[p], plane_id(p)).wait_recv()

        crossed[z] = jnp.sum(gathered[...], axis=0)

        @pl.loop(1, NZ)
        def _(k):
            zz = lax.rem(z + k, NZ)
            remote(crossed.at[z], crossed.at[z], cross_s.at[k - 1], cross_r.at[k - 1], z_id(zz)).start()

    settle(parts[1])
    settle(parts[2])
    send_along_z(*GROUPS[1])
    settle(parts[3])
    settle(parts[4])
    send_along_z(*GROUPS[2])

    @pl.when(owner)
    def _():
        @pl.loop(1, NZ)
        def _(k):
            zz = lax.rem(z + NZ - k, NZ)
            remote(crossed.at[z], crossed.at[zz], cross_s.at[k - 1], cross_r.at[k - 1], z_id(zz)).wait_recv()

        final[chip] = jnp.sum(crossed[...], axis=0)

        @pl.loop(1, 32)
        def _(k):
            p = lax.rem(plane + k, 32)
            remote(final.at[chip], final.at[chip], final_s.at[k - 1], final_r.at[chip], plane_id(p)).start()

    lat_copy.wait_recv()
    half = pl.ds(pl.multiple_of(lax.rem(ctx, 2) * 8, 8), 8)
    lg_ref[...] = ls[half, :] + lr[half, :]

    for k in range(1, NZ):
        z_copy(k)[1].wait_recv()
    total = zo[z]
    for k in range(NZ - 1):
        total = total + zr[k].astype(F32)
    kg_ref[...] = total

    @pl.loop(0, TILES)
    def _(t):
        @pl.when(tile_plane(t) != plane)
        def _():
            remote(final.at[t], final.at[t], final_s.at[0], final_r.at[t], mate).wait_recv()

    for copy in halo_copies + [lat_copy]:
        copy.wait_send()
    for part in parts:
        for copy in [part["core"]] + part["first"] + part["second"]:
            copy.wait_send()
    for k in range(1, NZ):
        z_copy(k)[1].wait_send()

    @pl.loop(0, TILES)
    def _(t):
        @pl.when(tile_plane(t) != plane)
        def _():
            remote(small.at[t], gathered.at[plane], small_s.at[t], small_r.at[plane], plane_id(tile_plane(t))).wait_send()

    @pl.when(owner)
    def _():
        @pl.loop(1, NZ)
        def _(k):
            zz = lax.rem(z + k, NZ)
            remote(crossed.at[z], crossed.at[z], cross_s.at[k - 1], cross_r.at[k - 1], z_id(zz)).wait_send()

        @pl.loop(1, 32)
        def _(k):
            p = lax.rem(plane + k, 32)
            remote(final.at[chip], final.at[chip], final_s.at[k - 1], final_r.at[chip], plane_id(p)).wait_send()


def finish(fg_in, kg_in, sums, lg_in, fg_ref, kg_ref, mod_ref, vec_ref, lg_ref):
    fg_ref[...] = fg_in[...]
    kg_ref[...] = kg_in[:, 0:ROWS]
    for t in range(8):
        block, half = t // 2, t % 2
        mod_ref[block // 2, (block % 2) * 8 : (block % 2) * 8 + 8, half * 128 : (half + 1) * 128] = sums[t]
    for half in range(2):
        vec_ref[:, half * 128 : (half + 1) * 128] = sums[8 + half, 0:4]
    lg_ref[0, 0] = lg_in[:, 0:CZ]


def local(features, grad_out, mean_saved, rstd_saved, latent, *others):
    operands = (features, grad_out, mean_saved, rstd_saved, jnp.transpose(latent, (0, 2, 3, 1))) + others
    vmem = pl.BlockSpec(memory_space=pltpu.VMEM)
    dma = pltpu.SemaphoreType.DMA
    buffers = []
    for first_z, count, axis in PARTS:
        wide = (16, count * 128)
        low, high = span_of(first_z, count)
        first = (16, high - low) if axis == "x" else (4,) + wide
        buffers += [
            pltpu.VMEM((16, high - low + 128) if axis == "x" else (4,) + first, F32),
            pltpu.VMEM((4,) + first, BF16),
            pltpu.VMEM((4,) + first, BF16),
            pltpu.VMEM((4,) + first, BF16),
            pltpu.VMEM((3,) + first, BF16),
            pltpu.VMEM((4,) + wide, F32),
            pltpu.VMEM((3,) + wide, F32),
        ]
    parts = len(PARTS)
    partial = pl.pallas_call(
        body,
        out_shape=(
            jax.ShapeDtypeStruct((1, 2, H, W, C), BF16),
            jax.ShapeDtypeStruct((16, 128), F32),
            jax.ShapeDtypeStruct((TILES, 8, 128), F32),
            jax.ShapeDtypeStruct((8, 128), F32),
        ),
        in_specs=[pl.BlockSpec(memory_space=pltpu.HBM)] * 12,
        out_specs=(vmem,) * 4,
        scratch_shapes=[
            pltpu.VMEM((1, 2, H, W, C), BF16),
            pltpu.VMEM((1, 2, H, W, CO), BF16),
            pltpu.VMEM((1, G), F32),
            pltpu.VMEM((1, G), F32),
            pltpu.VMEM((1, CZ, LP, NCTX // 2), F32),
            pltpu.VMEM((C,), F32),
            pltpu.VMEM((C,), F32),
            pltpu.VMEM((CZ, C), F32),
            pltpu.VMEM((C,), F32),
            pltpu.VMEM((CZ, C), F32),
            pltpu.VMEM((C,), F32),
            pltpu.VMEM((27 * C, CO), BF16),
            pltpu.VMEM((2, H, W, CO), BF16),
            pltpu.VMEM((2 * PX, C), BF16),
            pltpu.VMEM((2 * H, W, C), F32),
            pltpu.VMEM((2 * H, W, C), F32),
            pltpu.VMEM((4 * PX, 9 * CO), BF16),
            pltpu.VMEM((CO, 27 * C + 128), F32),
            pltpu.VMEM((2 * PX, C), F32),
            pltpu.VMEM((LP, C), F32),
            pltpu.VMEM((2, 2, W, C), F32),
            pltpu.VMEM((2, 2, W, C), F32),
            pltpu.VMEM((NZ, 16, 128), F32),
            pltpu.VMEM((NZ, 16, 128), BF16),
            pltpu.VMEM((NZ - 1, 16, 128), BF16),
            pltpu.VMEM((TILES, 8, 128), F32),
            pltpu.VMEM((32, 8, 128), F32),
            pltpu.VMEM((NZ, 8, 128), F32),
            pltpu.VMEM((16, 128), F32),
            pltpu.VMEM((16, 128), F32),
            dma((12,)),
            dma((2,)),
            dma((2,)),
            dma((parts,)),
            dma((parts,)),
            dma((parts, 3)),
            dma((parts, 3)),
            dma((parts, 3)),
            dma((parts, 3)),
            dma((NZ - 1,)),
            dma((NZ - 1,)),
            dma((TILES,)),
            dma((32,)),
            dma((NZ - 1,)),
            dma((NZ - 1,)),
            dma((31,)),
            dma((TILES,)),
            dma,
            dma,
            pltpu.SemaphoreType.REGULAR,
            pltpu.SemaphoreType.REGULAR,
        ]
        + buffers,
        compiler_params=pltpu.CompilerParams(
            collective_id=0, has_side_effects=True, vmem_limit_bytes=36 * 1024 * 1024
        ),
    )(*(pltpu.with_memory_space_constraint(value, pltpu.HBM) for value in operands))
    fg, kg, mod, vec, lg = pl.pallas_call(
        finish,
        out_shape=(
            jax.ShapeDtypeStruct((1, 2, H, W, C), BF16),
            jax.ShapeDtypeStruct((16, ROWS), F32),
            jax.ShapeDtypeStruct((2, CZ, C), F32),
            jax.ShapeDtypeStruct((4, C), F32),
            jax.ShapeDtypeStruct((1, 1, LP // 2, CZ), F32),
        ),
        in_specs=[vmem] * 4,
        out_specs=(vmem,) * 5,
        compiler_params=pltpu.CompilerParams(vmem_limit_bytes=8 * 1024 * 1024),
    )(*partial)
    return fg, kg.T, mod, vec, jnp.swapaxes(lg, 2, 3)


def solution(mesh):
    placed = (
        P("vid", "ctx", None, None, None),
        P("vid", "ctx", None, None, None),
        P("vid", None),
        P("vid", None),
        P("vid", None, None, None),
        P(),
        P(),
        P(),
        P(),
        P(),
        P(),
        P(),
    )
    return jax.shard_map(
        local,
        mesh=mesh,
        in_specs=placed,
        out_specs=(
            P("vid", "ctx", None, None, None),
            P("ctx", "vid"),
            P(),
            P(),
            P("vid", "ctx", None, None),
        ),
        check_vma=False,
    )
```

```python
import jax
import jax.numpy as jnp
from jax import lax
from jax.experimental import pallas as pl
from jax.experimental.pallas import tpu as pltpu
from jax.sharding import PartitionSpec as P

MESH = pl.DeviceIdType.MESH
F32 = jnp.float32
BF16 = jnp.bfloat16
HIGHEST = lax.Precision.HIGHEST

NX, NY, NZ = 4, 4, 16
NCTX = NY * NZ
H, W, C, CO, CZ, G, LP = 8, 32, 256, 128, 16, 32, 16
PX = H * W
ROWS = 108
TILES = 10
PARTS = ((11, 5, "x"), (9, 2, "x"), (6, 3, "y"), (0, 3, "x"), (3, 3, "y"))
GROUPS = ((11, 16), (6, 11), (0, 6))
FAR_FIRST = (8, 7, 9, 6, 10, 5, 11, 4, 12, 3, 13, 2, 14, 1, 15)


def span_of(first_z, count):
    low = ROWS * NY * first_z // 128
    high = -(-ROWS * NY * (first_z + count) // 128)
    return low * 128, high * 128


def exact(lhs, rhs, dims):
    return lax.dot_general(lhs, rhs, (dims, ((), ())), precision=HIGHEST, preferred_element_type=F32)


def wide_dot(lhs, rhs, dims):
    return lax.dot_general(lhs, rhs, (dims, ((), ())), preferred_element_type=F32)


def body(
    feat_hbm, grad_hbm, mean_hbm, rstd_hbm, lat_hbm, gamma_hbm, beta_hbm, ws_hbm, bs_hbm, wh_hbm, bh_hbm, kern_hbm,
    fg_ref, kg_ref, final, lg_ref,
    feat_ref, grad_ref, mean_ref, rstd_ref, lat_ref, gamma_ref, beta_ref, ws_ref, bs_ref, wh_ref, bh_ref, kern,
    halo, act, dmod, norm, patch, gsum, agrad, tabs, maps, pools,
    zo, zs, zr, small, gathered, crossed, ls, lr,
    load_sems, halo_s, halo_r, core_s, core_r, first_s, first_r, second_s, second_r, z_s, z_r,
    small_s, small_r, cross_s, cross_r, final_s, final_r, lat_s, lat_r, relay, relay_far, relay_plane, relay_mate, image, image_s,
    *part_refs,
):
    ctx = lax.axis_index("ctx")
    vid = lax.axis_index("vid")
    z, y = lax.div(ctx, NY), lax.rem(ctx, NY)
    x, core = lax.div(vid, 2), lax.rem(vid, 2)
    plane = y * 8 + vid

    def plane_id(p):
        return (z * NY + lax.div(p, 8), lax.rem(p, 8))

    def z_id(zz):
        return (zz * NY + y, vid)

    def x_id(xx):
        return (ctx, 2 * xx + core)

    def y_id(yy):
        return (z * NY + yy, vid)

    mate = (ctx, vid + 1 - 2 * core)
    sharer = (ctx + 1 - 2 * lax.rem(ctx, 2), vid)
    before = (lax.rem(ctx + NCTX - 1, NCTX), vid)
    after = (lax.rem(ctx + 1, NCTX), vid)

    loads = [
        pltpu.make_async_copy(source, target, load_sems.at[n])
        for n, (source, target) in enumerate(
            (
                (lat_hbm, lat_ref),
                (mean_hbm, mean_ref),
                (rstd_hbm, rstd_ref),
                (ws_hbm, ws_ref),
                (wh_hbm, wh_ref),
                (bs_hbm, bs_ref),
                (bh_hbm, bh_ref),
                (gamma_hbm, gamma_ref),
                (beta_hbm, beta_ref),
                (feat_hbm, feat_ref),
                (grad_hbm, grad_ref),
                (kern_hbm, kern),
            )
        )
    ]
    for load in loads:
        load.start()

    barrier = pltpu.get_barrier_semaphore()

    def signal(semaphore, device):
        pl.semaphore_signal(semaphore, inc=1, device_id=device, device_id_type=MESH)

    signal(barrier, before)
    signal(barrier, after)
    signal(barrier, mate)
    for k in range(1, 4):
        signal(barrier, x_id(lax.rem(x + k, NX)))
        signal(barrier, y_id(lax.rem(y + k, NY)))
    for k in (2, NZ - 2, 1, NZ - 1):
        signal(barrier, z_id(lax.rem(z + k, NZ)))

    def remote(src, dst, send, recv, device):
        return pltpu.make_async_remote_copy(
            src_ref=src, dst_ref=dst, send_sem=send, recv_sem=recv, device_id=device, device_id_type=MESH
        )

    pl.semaphore_wait(barrier, 13)
    halo_copies = [
        remote(grad_hbm.at[0, f], halo.at[f], halo_s.at[f], halo_r.at[f], before) for f in range(2)
    ]
    for copy in halo_copies:
        copy.start()
    signal(relay, z_id(lax.rem(z + 2, NZ)))
    signal(relay, z_id(lax.rem(z + NZ - 2, NZ)))
    for k in range(1, 4):
        signal(relay_plane, y_id(lax.rem(y + k, NY)))

    for load in loads[:9]:
        load.wait()

    pick = (lax.broadcasted_iota(jnp.int32, (G, C), 1) // (C // G) == lax.broadcasted_iota(jnp.int32, (G, C), 0)).astype(F32)
    saved = jnp.concatenate([mean_ref[...], rstd_ref[...], jnp.zeros((6, G), F32)], axis=0)
    saved = exact(saved, pick, ((1,), (0,)))
    mean_c, rstd_c = saved[0:1], saved[1:2]
    gamma = gamma_ref[...].reshape(1, C)
    beta = beta_ref[...].reshape(1, C)
    here = (lax.broadcasted_iota(jnp.int32, (NCTX // 2, 128), 0) == lax.div(ctx, 2)).astype(F32)
    lat = exact(lat_ref[0].reshape(CZ * LP, NCTX // 2), here, ((1,), (0,))).reshape(CZ, LP, 128)
    corner = lax.broadcasted_iota(jnp.int32, (CZ, LP, 128), 1) == lax.broadcasted_iota(jnp.int32, (CZ, LP, 128), 2)
    lat = jnp.sum(jnp.where(corner, lat, 0.0), axis=1)[:, :LP]
    weights = jnp.concatenate([ws_ref[...], wh_ref[...]], axis=1)
    bias = jnp.concatenate([bs_ref[...].reshape(1, C), bh_ref[...].reshape(1, C)], axis=1)
    both_tabs = exact(lat, weights, ((0,), (0,))) + bias
    tabs[...] = both_tabs[:, :C]
    pix = lax.broadcasted_iota(jnp.int32, (2 * W, LP), 0)
    latent_pixel = lax.broadcasted_iota(jnp.int32, (2 * W, LP), 1)
    spread = ((pix // W) * (W // 4) + (pix % W) // 4 == latent_pixel).astype(F32)
    both_maps = exact(spread, both_tabs, ((1,), (0,)))
    maps[0] = both_maps[:, :C].reshape(2, W, C)
    maps[1] = both_maps[:, C:].reshape(2, W, C)

    loads[9].wait()

    @pl.loop(0, 2 * H, unroll=4)
    def _(i):
        f, h = lax.div(i, H), lax.rem(i, H)
        hh = lax.div(h, 4)
        normed = (feat_ref[0, f, h].astype(F32) - mean_c) * rstd_c
        modulated = (normed * gamma + beta) * maps[0, hh] + maps[1, hh]
        s = jax.nn.sigmoid(modulated)
        norm[i] = normed
        dmod[i] = s * (1.0 + modulated * (1.0 - s))
        act[pl.ds(pl.multiple_of(i * W, W), W), :] = (modulated * s).astype(BF16)

    loads[10].wait()
    col = lax.broadcasted_iota(jnp.int32, (PX, CO), 0) % W

    def lay_patches(f, g):
        for c in range(3):
            if c == 0:
                moved = jnp.where(col == W - 1, 0.0, pltpu.roll(g, PX - 1, 0))
            elif c == 1:
                moved = g
            else:
                moved = jnp.where(col == 0, 0.0, pltpu.roll(g, 1, 0))
            moved = moved.astype(BF16)
            blank = jnp.zeros((W, CO), BF16)
            for b in range(3):
                lanes = slice((b * 3 + c) * CO, (b * 3 + c + 1) * CO)
                base = f * PX
                if b == 0:
                    patch[base : base + PX - W, lanes] = moved[W:]
                    patch[base + PX - W : base + PX, lanes] = blank
                elif b == 1:
                    patch[base : base + PX, lanes] = moved
                else:
                    patch[base : base + W, lanes] = blank
                    patch[base + W : base + PX, lanes] = moved[: PX - W]

    for f in range(2):
        lay_patches(f, grad_ref[0, f].astype(F32).reshape(PX, CO))

    def filter_term(a, first, last, images):
        for bc in range(9):
            lanes = slice(bc * CO, (bc + 1) * CO)
            tap = a * 9 + bc
            yield slice(tap * C, (tap + 1) * C), wide_dot(patch[first:last, lanes], images, ((0,), (0,)))

    def taps(a):
        return jnp.concatenate([kern[(a * 9 + bc) * C : (a * 9 + bc + 1) * C, :] for bc in range(9)], axis=1)

    def input_term(a, first, last):
        return wide_dot(patch[first:last, :], taps(a), ((1,), (1,)))

    lane = lax.broadcasted_iota(jnp.int32, (16, 128), 1)
    parts = []
    refs = list(part_refs)
    for n, (first_z, count, axis) in enumerate(PARTS):
        places = (x, y) if axis == "x" else (y, x)
        ids = (x_id, y_id) if axis == "x" else (y_id, x_id)
        names = ("own", "cs", "cr", "fs", "fr", "ss", "sr")
        part = dict(zip(names, refs[:7]))
        del refs[:7]
        part.update(n=n, first_z=first_z, count=count, axis=axis, places=places, ids=ids)
        parts.append(part)

    def owned(place, parity):
        return pl.ds(pl.multiple_of((2 * place + parity) * 16, 16), 16)

    def shifted(low, high, off, turn):
        return jnp.where(lane < 128 - off, pltpu.roll(low, turn, 1), pltpu.roll(high, turn, 1))

    def deal(part):
        own, cs, n = part["own"], part["cs"], part["n"]
        if part["axis"] == "x":
            low, high = span_of(part["first_z"], part["count"])
            for xx in range(NX):
                cs[xx] = gsum[owned(xx, 1 - core), low:high].astype(BF16)
        else:

            @pl.loop(0, part["count"] * NY, unroll=4)
            def _(i):
                zl, yy = lax.div(i, NY), lax.rem(i, NY)
                start = ROWS * ((part["first_z"] + zl) * NY + yy)
                tile = lax.div(start, 128)
                off = start - tile * 128
                turn = lax.rem(128 - off, 128)
                first = pl.ds(pl.multiple_of(tile * 128, 128), 128)
                second = pl.ds(pl.multiple_of(tile * 128 + 128, 128), 128)
                lanes = pl.ds(pl.multiple_of(zl * 128, 128), 128)
                for xx in range(NX):
                    mine, theirs = owned(xx, core), owned(xx, 1 - core)
                    cs[yy, xx, :, lanes] = shifted(gsum[theirs, first], gsum[theirs, second], off, turn).astype(BF16)
                    own[yy, xx, :, lanes] = shifted(gsum[mine, first], gsum[mine, second], off, turn)

        part["core"] = remote(cs, part["cr"], core_s.at[n], core_r.at[n], mate)
        part["core"].start()

    def first_stage(part):
        own, cr, fs, n = part["own"], part["cr"], part["fs"], part["n"]
        part["core"].wait_recv()
        if part["axis"] == "x":
            low, high = span_of(part["first_z"], part["count"])
            for xx in range(NX):
                fs[xx] = (gsum[owned(xx, core), low:high] + cr[xx].astype(F32)).astype(BF16)
        else:

            @pl.loop(0, 16, unroll=2)
            def _(i):
                j, m = lax.div(i, 4), lax.rem(i, 4)
                total = own[j, m] + cr[j, m].astype(F32)
                own[j, m] = total
                fs[j, m] = total.astype(BF16)

        part["first"] = []
        for k in (2, 1, 3):
            there = lax.rem(part["places"][0] + k, 4)
            copy = remote(fs.at[there], part["fr"].at[k - 1], first_s.at[n, k - 1], first_r.at[n, k - 1], part["ids"][0](there))
            copy.start()
            part["first"].append(copy)

    def second_stage(part):
        own, cr, fr, ss, n = part["own"], part["cr"], part["fr"], part["ss"], part["n"]
        for copy in part["first"]:
            copy.wait_recv()
        if part["axis"] == "x":
            low, high = span_of(part["first_z"], part["count"])
            width = high - low
            own[:, 0:width] = (
                gsum[owned(x, core), low:high]
                + cr[x].astype(F32)
                + fr[0].astype(F32)
                + fr[1].astype(F32)
                + fr[2].astype(F32)
            )
            own[:, width:] = jnp.zeros((16, 128), F32)
            for i in range(part["count"] * NY):
                zl, yy = i // NY, i % NY
                start = ROWS * (part["first_z"] * NY + i) - low
                tile, off = start // 128, start % 128
                block = own[:, tile * 128 : tile * 128 + 128]
                if off:
                    block = shifted(block, own[:, tile * 128 + 128 : tile * 128 + 256], off, 128 - off)
                ss[yy, :, zl * 128 : zl * 128 + 128] = block
        else:
            for j in range(4):
                ss[j] = own[y, j] + fr[0, j].astype(F32) + fr[1, j].astype(F32) + fr[2, j].astype(F32)
        part["second"] = []
        for k in (2, 1, 3):
            there = lax.rem(part["places"][1] + k, 4)
            copy = remote(ss.at[there], part["sr"].at[k - 1], second_s.at[n, k - 1], second_r.at[n, k - 1], part["ids"][1](there))
            copy.start()
            part["second"].append(copy)

    def settle(part):
        for copy in part["second"]:
            copy.wait_recv()
        sr = part["sr"]
        total = part["ss"][part["places"][1]] + sr[0] + sr[1] + sr[2]
        for j in range(part["count"]):
            piece = total[:, j * 128 : (j + 1) * 128]
            zo[part["first_z"] + j] = piece
            zs[part["first_z"] + j] = piece.astype(BF16)

    def z_copy(k):
        zz = lax.rem(z + k, NZ)
        return zz, remote(zs.at[zz], zr.at[k - 1], z_s.at[k - 1], z_r.at[k - 1], z_id(zz))

    def send_along_z(first, last):
        for k in FAR_FIRST:
            zz, copy = z_copy(k)

            @pl.when(jnp.logical_and(zz >= first, zz < last))
            def _():
                copy.start()

    gsum[:, 27 * C :] = jnp.zeros((CO, 128), F32)
    for span, term in filter_term(2, 0, 2 * PX, act[...]):
        gsum[:, span] = term
    deal(parts[0])
    for span, term in filter_term(1, PX, 2 * PX, act[0:PX]):
        gsum[:, span] = term
    loads[11].wait()
    agrad[...] = input_term(2, 0, 2 * PX)
    agrad[0:PX, :] += input_term(1, PX, 2 * PX)
    pl.semaphore_wait(relay, 2)
    signal(relay_far, z_id(lax.rem(z + 4, NZ)))
    signal(relay_far, z_id(lax.rem(z + NZ - 4, NZ)))
    pl.semaphore_wait(relay_plane, 3)
    signal(relay_mate, mate)
    first_stage(parts[0])

    @pl.when(ctx == 0)
    def _():
        for span, term in filter_term(1, 0, PX, act[0:PX]):
            gsum[:, span] += term
        for span, term in filter_term(0, 0, PX, act[0:PX]):
            gsum[:, span] = term
        for span, term in filter_term(0, PX, 2 * PX, act[0:PX]):
            gsum[:, span] += term
        agrad[0:PX, :] += input_term(1, 0, PX) + input_term(0, 0, PX) + input_term(0, PX, 2 * PX)

    @pl.when(ctx != 0)
    def _():
        gsum[:, 0 : 9 * C] = jnp.zeros((CO, 9 * C), F32)

    def take_halo(f):
        halo_copies[f].wait_recv()
        lay_patches(2 + f, jnp.where(ctx == NCTX - 1, 0.0, halo[f].astype(F32).reshape(PX, CO)))

    take_halo(0)
    for span, term in filter_term(1, 2 * PX, 3 * PX, act[PX : 2 * PX]):
        gsum[:, span] += term
    deal(parts[1])
    deal(parts[2])
    take_halo(1)
    agrad[...] += input_term(0, 2 * PX, 4 * PX)
    agrad[PX : 2 * PX, :] += input_term(1, 2 * PX, 3 * PX)

    pools[...] = jnp.zeros_like(pools)

    @pl.loop(0, 2 * H, unroll=4)
    def _(i):
        f, h = lax.div(i, H), lax.rem(i, H)
        hh = lax.div(h, 4)
        pre = agrad[pl.ds(pl.multiple_of(i * W, W), W), :] * dmod[i]
        image[0, f, h] = (pre * maps[0, hh] * gamma * rstd_c).astype(BF16)
        pools[0, hh] += pre * norm[i]
        pools[1, hh] += pre

    write_image = pltpu.make_async_copy(image, fg_ref, image_s)
    write_image.start()
    normed_pool = exact(spread, pools[0].reshape(2 * W, C), ((0,), (0,)))
    shift_pool = exact(spread, pools[1].reshape(2 * W, C), ((0,), (0,)))
    scale_pool = normed_pool * gamma + shift_pool * beta
    tab = tabs[...]
    rows = [
        exact(lat, scale_pool, ((1,), (0,))),
        exact(lat, shift_pool, ((1,), (0,))),
        jnp.concatenate(
            [
                jnp.sum(tab * normed_pool, axis=0, keepdims=True),
                jnp.sum(tab * shift_pool, axis=0, keepdims=True),
                jnp.sum(scale_pool, axis=0, keepdims=True),
                jnp.sum(shift_pool, axis=0, keepdims=True),
                jnp.zeros((4, C), F32),
            ],
            axis=0,
        ),
    ]
    for t in range(TILES):
        block, half = t // 2, t % 2
        source = rows[block // 2][(block % 2) * 8 : (block % 2) * 8 + 8]
        small[t] = source[:, half * 128 : (half + 1) * 128]

    chip = y * NX + x
    owner = jnp.logical_and(core == 0, chip < TILES)

    def tile_plane(t):
        return lax.div(t, NX) * 8 + 2 * lax.rem(t, NX)

    pl.semaphore_wait(relay_mate, 1)

    @pl.loop(0, TILES)
    def _(t):
        @pl.when(tile_plane(t) != plane)
        def _():
            remote(small.at[t], gathered.at[plane], small_s.at[t], small_r.at[plane], plane_id(tile_plane(t))).start()

    for span, term in filter_term(0, 2 * PX, 4 * PX, act[...]):
        gsum[:, span] += term
    deal(parts[3])
    deal(parts[4])
    for part in parts[1:]:
        first_stage(part)

    second_stage(parts[0])
    latent_sum = exact(scale_pool, ws_ref[...], ((1,), (1,))) + exact(shift_pool, wh_ref[...], ((1,), (1,)))
    ls[...] = jnp.zeros_like(ls)
    ls[:, 0:CZ] = latent_sum
    lat_copy = remote(ls, lr, lat_s, lat_r, sharer)
    lat_copy.start()

    pl.semaphore_wait(relay_far, 2)
    @pl.when(owner)
    def _():
        gathered[plane] = small[chip]

        @pl.loop(1, 32)
        def _(k):
            p = lax.rem(plane + k, 32)
            remote(small.at[0], gathered.at[p], small_s.at[0], small_r.at[p], plane_id(p)).wait_recv()

        crossed[z] = jnp.sum(gathered[...], axis=0)

        @pl.loop(1, NZ)
        def _(k):
            zz = lax.rem(z + k, NZ)
            remote(crossed.at[z], crossed.at[z], cross_s.at[k - 1], cross_r.at[k - 1], z_id(zz)).start()

    second_stage(parts[1])
    second_stage(parts[2])
    second_stage(parts[3])
    second_stage(parts[4])
    settle(parts[0])
    send_along_z(*GROUPS[0])

    settle(parts[1])
    settle(parts[2])
    send_along_z(*GROUPS[1])
    settle(parts[3])
    settle(parts[4])
    send_along_z(*GROUPS[2])

    @pl.when(owner)
    def _():
        @pl.loop(1, NZ)
        def _(k):
            zz = lax.rem(z + NZ - k, NZ)
            remote(crossed.at[z], crossed.at[zz], cross_s.at[k - 1], cross_r.at[k - 1], z_id(zz)).wait_recv()

        final[chip] = jnp.sum(crossed[...], axis=0)

        @pl.loop(1, 32)
        def _(k):
            p = lax.rem(plane + k, 32)
            remote(final.at[chip], final.at[chip], final_s.at[k - 1], final_r.at[chip], plane_id(p)).start()

    lat_copy.wait_recv()
    half = pl.ds(pl.multiple_of(lax.rem(ctx, 2) * 8, 8), 8)
    lg_ref[...] = ls[half, :] + lr[half, :]

    for k in range(1, NZ):
        z_copy(k)[1].wait_recv()
    total = zo[z]
    for k in range(NZ - 1):
        total = total + zr[k].astype(F32)
    kg_ref[...] = total

    @pl.loop(0, TILES)
    def _(t):
        @pl.when(tile_plane(t) != plane)
        def _():
            remote(final.at[t], final.at[t], final_s.at[0], final_r.at[t], mate).wait_recv()

    write_image.wait()
    for copy in halo_copies + [lat_copy]:
        copy.wait_send()
    for part in parts:
        for copy in [part["core"]] + part["first"] + part["second"]:
            copy.wait_send()
    for k in range(1, NZ):
        z_copy(k)[1].wait_send()

    @pl.loop(0, TILES)
    def _(t):
        @pl.when(tile_plane(t) != plane)
        def _():
            remote(small.at[t], gathered.at[plane], small_s.at[t], small_r.at[plane], plane_id(tile_plane(t))).wait_send()

    @pl.when(owner)
    def _():
        @pl.loop(1, NZ)
        def _(k):
            zz = lax.rem(z + k, NZ)
            remote(crossed.at[z], crossed.at[z], cross_s.at[k - 1], cross_r.at[k - 1], z_id(zz)).wait_send()

        @pl.loop(1, 32)
        def _(k):
            p = lax.rem(plane + k, 32)
            remote(final.at[chip], final.at[chip], final_s.at[k - 1], final_r.at[chip], plane_id(p)).wait_send()


def finish(fg_in, kg_in, sums, lg_in, fg_ref, kg_ref, mod_ref, vec_ref, lg_ref):
    fg_ref[...] = fg_in[...]
    kg_ref[...] = kg_in[:, 0:ROWS]
    for t in range(8):
        block, half = t // 2, t % 2
        mod_ref[block // 2, (block % 2) * 8 : (block % 2) * 8 + 8, half * 128 : (half + 1) * 128] = sums[t]
    for half in range(2):
        vec_ref[:, half * 128 : (half + 1) * 128] = sums[8 + half, 0:4]
    lg_ref[0, 0] = lg_in[:, 0:CZ]


def local(features, grad_out, mean_saved, rstd_saved, latent, *others):
    operands = (features, grad_out, mean_saved, rstd_saved, jnp.transpose(latent, (0, 2, 3, 1))) + others
    vmem = pl.BlockSpec(memory_space=pltpu.VMEM)
    dma = pltpu.SemaphoreType.DMA
    buffers = []
    for first_z, count, axis in PARTS:
        wide = (16, count * 128)
        low, high = span_of(first_z, count)
        first = (16, high - low) if axis == "x" else (4,) + wide
        buffers += [
            pltpu.VMEM((16, high - low + 128) if axis == "x" else (4,) + first, F32),
            pltpu.VMEM((4,) + first, BF16),
            pltpu.VMEM((4,) + first, BF16),
            pltpu.VMEM((4,) + first, BF16),
            pltpu.VMEM((3,) + first, BF16),
            pltpu.VMEM((4,) + wide, F32),
            pltpu.VMEM((3,) + wide, F32),
        ]
    parts = len(PARTS)
    partial = pl.pallas_call(
        body,
        out_shape=(
            jax.ShapeDtypeStruct((1, 2, H, W, C), BF16),
            jax.ShapeDtypeStruct((16, 128), F32),
            jax.ShapeDtypeStruct((TILES, 8, 128), F32),
            jax.ShapeDtypeStruct((8, 128), F32),
        ),
        in_specs=[pl.BlockSpec(memory_space=pltpu.HBM)] * 12,
        out_specs=(pl.BlockSpec(memory_space=pl.ANY),) + (vmem,) * 3,
        scratch_shapes=[
            pltpu.VMEM((1, 2, H, W, C), BF16),
            pltpu.VMEM((1, 2, H, W, CO), BF16),
            pltpu.VMEM((1, G), F32),
            pltpu.VMEM((1, G), F32),
            pltpu.VMEM((1, CZ, LP, NCTX // 2), F32),
            pltpu.VMEM((C,), F32),
            pltpu.VMEM((C,), F32),
            pltpu.VMEM((CZ, C), F32),
            pltpu.VMEM((C,), F32),
            pltpu.VMEM((CZ, C), F32),
            pltpu.VMEM((C,), F32),
            pltpu.VMEM((27 * C, CO), BF16),
            pltpu.VMEM((2, H, W, CO), BF16),
            pltpu.VMEM((2 * PX, C), BF16),
            pltpu.VMEM((2 * H, W, C), F32),
            pltpu.VMEM((2 * H, W, C), F32),
            pltpu.VMEM((4 * PX, 9 * CO), BF16),
            pltpu.VMEM((CO, 27 * C + 128), F32),
            pltpu.VMEM((2 * PX, C), F32),
            pltpu.VMEM((LP, C), F32),
            pltpu.VMEM((2, 2, W, C), F32),
            pltpu.VMEM((2, 2, W, C), F32),
            pltpu.VMEM((NZ, 16, 128), F32),
            pltpu.VMEM((NZ, 16, 128), BF16),
            pltpu.VMEM((NZ - 1, 16, 128), BF16),
            pltpu.VMEM((TILES, 8, 128), F32),
            pltpu.VMEM((32, 8, 128), F32),
            pltpu.VMEM((NZ, 8, 128), F32),
            pltpu.VMEM((16, 128), F32),
            pltpu.VMEM((16, 128), F32),
            dma((12,)),
            dma((2,)),
            dma((2,)),
            dma((parts,)),
            dma((parts,)),
            dma((parts, 3)),
            dma((parts, 3)),
            dma((parts, 3)),
            dma((parts, 3)),
            dma((NZ - 1,)),
            dma((NZ - 1,)),
            dma((TILES,)),
            dma((32,)),
            dma((NZ - 1,)),
            dma((NZ - 1,)),
            dma((31,)),
            dma((TILES,)),
            dma,
            dma,
            pltpu.SemaphoreType.REGULAR,
            pltpu.SemaphoreType.REGULAR,
            pltpu.SemaphoreType.REGULAR,
            pltpu.SemaphoreType.REGULAR,
            pltpu.VMEM((1, 2, H, W, C), BF16),
            dma,
        ]
        + buffers,
        compiler_params=pltpu.CompilerParams(
            collective_id=0, has_side_effects=True, vmem_limit_bytes=36 * 1024 * 1024
        ),
    )(*(pltpu.with_memory_space_constraint(value, pltpu.HBM) for value in operands))
    fg, kg, mod, vec, lg = pl.pallas_call(
        finish,
        out_shape=(
            jax.ShapeDtypeStruct((1, 2, H, W, C), BF16),
            jax.ShapeDtypeStruct((16, ROWS), F32),
            jax.ShapeDtypeStruct((2, CZ, C), F32),
            jax.ShapeDtypeStruct((4, C), F32),
            jax.ShapeDtypeStruct((1, 1, LP // 2, CZ), F32),
        ),
        in_specs=[vmem] * 4,
        out_specs=(vmem,) * 5,
        compiler_params=pltpu.CompilerParams(vmem_limit_bytes=8 * 1024 * 1024),
    )(*partial)
    return fg, kg.T, mod, vec, jnp.swapaxes(lg, 2, 3)


def solution(mesh):
    placed = (
        P("vid", "ctx", None, None, None),
        P("vid", "ctx", None, None, None),
        P("vid", None),
        P("vid", None),
        P("vid", None, None, None),
        P(),
        P(),
        P(),
        P(),
        P(),
        P(),
        P(),
    )
    return jax.shard_map(
        local,
        mesh=mesh,
        in_specs=placed,
        out_specs=(
            P("vid", "ctx", None, None, None),
            P("ctx", "vid"),
            P(),
            P(),
            P("vid", "ctx", None, None),
        ),
        check_vma=False,
    )
```

```python
import jax
import jax.numpy as jnp
from jax import lax
from jax.experimental import pallas as pl
from jax.experimental.pallas import tpu as pltpu
from jax.sharding import PartitionSpec as P

MESH = pl.DeviceIdType.MESH
F32 = jnp.float32
BF16 = jnp.bfloat16
HIGHEST = lax.Precision.HIGHEST

NX, NY, NZ = 4, 4, 16
NCTX = NY * NZ
H, W, C, CO, CZ, G, LP = 8, 32, 256, 128, 16, 32, 16
PX = H * W
ROWS = 108
TILES = 10
PARTS = ((11, 5, "x"), (6, 3, "x"), (9, 2, "y"), (0, 3, "x"), (3, 3, "y"))
GROUPS = ((11, 16), (6, 11), (0, 6))
FAR_FIRST = (8, 7, 9, 6, 10, 5, 11, 4, 12, 3, 13, 2, 14, 1, 15)


def span_of(first_z, count):
    low = ROWS * NY * first_z // 128
    high = -(-ROWS * NY * (first_z + count) // 128)
    return low * 128, high * 128


def exact(lhs, rhs, dims):
    return lax.dot_general(lhs, rhs, (dims, ((), ())), precision=HIGHEST, preferred_element_type=F32)


def wide_dot(lhs, rhs, dims):
    return lax.dot_general(lhs, rhs, (dims, ((), ())), preferred_element_type=F32)


def body(
    feat_hbm, grad_hbm, mean_hbm, rstd_hbm, lat_hbm, gamma_hbm, beta_hbm, ws_hbm, bs_hbm, wh_hbm, bh_hbm, kern_hbm,
    fg_ref, kg_ref, final, lg_ref,
    feat_ref, grad_ref, mean_ref, rstd_ref, lat_ref, gamma_ref, beta_ref, ws_ref, bs_ref, wh_ref, bh_ref, kern,
    halo, act, dmod, norm, patch, gsum, agrad, tabs, maps, pools,
    zo, zs, zr, small, gathered, crossed, ls, lr,
    load_sems, halo_s, halo_r, core_s, core_r, first_s, first_r, second_s, second_r, z_s, z_r,
    small_s, small_r, cross_s, cross_r, final_s, final_r, lat_s, lat_r, relay, relay_far, relay_plane, relay_mate, image, image_s,
    *part_refs,
):
    ctx = lax.axis_index("ctx")
    vid = lax.axis_index("vid")
    z, y = lax.div(ctx, NY), lax.rem(ctx, NY)
    x, core = lax.div(vid, 2), lax.rem(vid, 2)
    plane = y * 8 + vid

    def plane_id(p):
        return (z * NY + lax.div(p, 8), lax.rem(p, 8))

    def z_id(zz):
        return (zz * NY + y, vid)

    def x_id(xx):
        return (ctx, 2 * xx + core)

    def y_id(yy):
        return (z * NY + yy, vid)

    mate = (ctx, vid + 1 - 2 * core)
    sharer = (ctx + 1 - 2 * lax.rem(ctx, 2), vid)
    before = (lax.rem(ctx + NCTX - 1, NCTX), vid)
    after = (lax.rem(ctx + 1, NCTX), vid)

    loads = [
        pltpu.make_async_copy(source, target, load_sems.at[n])
        for n, (source, target) in enumerate(
            (
                (lat_hbm, lat_ref),
                (mean_hbm, mean_ref),
                (rstd_hbm, rstd_ref),
                (ws_hbm, ws_ref),
                (wh_hbm, wh_ref),
                (bs_hbm, bs_ref),
                (bh_hbm, bh_ref),
                (gamma_hbm, gamma_ref),
                (beta_hbm, beta_ref),
                (feat_hbm, feat_ref),
                (grad_hbm, grad_ref),
                (kern_hbm, kern),
            )
        )
    ]
    for load in loads:
        load.start()

    barrier = pltpu.get_barrier_semaphore()

    def signal(semaphore, device):
        pl.semaphore_signal(semaphore, inc=1, device_id=device, device_id_type=MESH)

    signal(barrier, before)
    signal(barrier, after)
    signal(barrier, mate)
    for k in range(1, 4):
        signal(barrier, x_id(lax.rem(x + k, NX)))
        signal(barrier, y_id(lax.rem(y + k, NY)))
    for k in (2, NZ - 2, 1, NZ - 1):
        signal(barrier, z_id(lax.rem(z + k, NZ)))

    def remote(src, dst, send, recv, device):
        return pltpu.make_async_remote_copy(
            src_ref=src, dst_ref=dst, send_sem=send, recv_sem=recv, device_id=device, device_id_type=MESH
        )

    pl.semaphore_wait(barrier, 13)
    halo_copies = [
        remote(grad_hbm.at[0, f], halo.at[f], halo_s, halo_r.at[f], before) for f in range(2)
    ]
    for copy in halo_copies:
        copy.start()
    signal(relay, z_id(lax.rem(z + 2, NZ)))
    signal(relay, z_id(lax.rem(z + NZ - 2, NZ)))
    for k in range(1, 4):
        signal(relay_plane, y_id(lax.rem(y + k, NY)))

    for load in loads[:9]:
        load.wait()

    pick = (lax.broadcasted_iota(jnp.int32, (G, C), 1) // (C // G) == lax.broadcasted_iota(jnp.int32, (G, C), 0)).astype(F32)
    saved = jnp.concatenate([mean_ref[...], rstd_ref[...], jnp.zeros((6, G), F32)], axis=0)
    saved = exact(saved, pick, ((1,), (0,)))
    mean_c, rstd_c = saved[0:1], saved[1:2]
    gamma = gamma_ref[...].reshape(1, C)
    beta = beta_ref[...].reshape(1, C)
    here = (lax.broadcasted_iota(jnp.int32, (NCTX // 2, 128), 0) == lax.div(ctx, 2)).astype(F32)
    lat = exact(lat_ref[0].reshape(CZ * LP, NCTX // 2), here, ((1,), (0,))).reshape(CZ, LP, 128)
    corner = lax.broadcasted_iota(jnp.int32, (CZ, LP, 128), 1) == lax.broadcasted_iota(jnp.int32, (CZ, LP, 128), 2)
    lat = jnp.sum(jnp.where(corner, lat, 0.0), axis=1)[:, :LP]
    weights = jnp.concatenate([ws_ref[...], wh_ref[...]], axis=1)
    bias = jnp.concatenate([bs_ref[...].reshape(1, C), bh_ref[...].reshape(1, C)], axis=1)
    both_tabs = exact(lat, weights, ((0,), (0,))) + bias
    tabs[...] = both_tabs[:, :C]
    pix = lax.broadcasted_iota(jnp.int32, (2 * W, LP), 0)
    latent_pixel = lax.broadcasted_iota(jnp.int32, (2 * W, LP), 1)
    spread = ((pix // W) * (W // 4) + (pix % W) // 4 == latent_pixel).astype(F32)
    both_maps = exact(spread, both_tabs, ((1,), (0,)))
    maps[0] = both_maps[:, :C].reshape(2, W, C)
    maps[1] = both_maps[:, C:].reshape(2, W, C)

    loads[9].wait()

    @pl.loop(0, 2 * H, unroll=4)
    def _(i):
        f, h = lax.div(i, H), lax.rem(i, H)
        hh = lax.div(h, 4)
        normed = (feat_ref[0, f, h].astype(F32) - mean_c) * rstd_c
        modulated = (normed * gamma + beta) * maps[0, hh] + maps[1, hh]
        s = jax.nn.sigmoid(modulated)
        norm[i] = normed
        dmod[i] = s * (1.0 + modulated * (1.0 - s))
        act[pl.ds(pl.multiple_of(i * W, W), W), :] = (modulated * s).astype(BF16)

    loads[10].wait()
    col = lax.broadcasted_iota(jnp.int32, (PX, CO), 0) % W

    def lay_patches(f, g):
        for c in range(3):
            if c == 0:
                moved = jnp.where(col == W - 1, 0.0, pltpu.roll(g, PX - 1, 0))
            elif c == 1:
                moved = g
            else:
                moved = jnp.where(col == 0, 0.0, pltpu.roll(g, 1, 0))
            moved = moved.astype(BF16)
            blank = jnp.zeros((W, CO), BF16)
            for b in range(3):
                lanes = slice((b * 3 + c) * CO, (b * 3 + c + 1) * CO)
                base = f * PX
                if b == 0:
                    patch[base : base + PX - W, lanes] = moved[W:]
                    patch[base + PX - W : base + PX, lanes] = blank
                elif b == 1:
                    patch[base : base + PX, lanes] = moved
                else:
                    patch[base : base + W, lanes] = blank
                    patch[base + W : base + PX, lanes] = moved[: PX - W]

    for f in range(2):
        lay_patches(f, grad_ref[0, f].astype(F32).reshape(PX, CO))

    def filter_term(a, first, last, images):
        for bc in range(9):
            lanes = slice(bc * CO, (bc + 1) * CO)
            tap = a * 9 + bc
            yield slice(tap * C, (tap + 1) * C), wide_dot(patch[first:last, lanes], images, ((0,), (0,)))

    def taps(a):
        return jnp.concatenate([kern[(a * 9 + bc) * C : (a * 9 + bc + 1) * C, :] for bc in range(9)], axis=1)

    def input_term(a, first, last):
        return wide_dot(patch[first:last, :], taps(a), ((1,), (1,)))

    lane = lax.broadcasted_iota(jnp.int32, (16, 128), 1)
    parts = []
    refs = list(part_refs)
    for n, (first_z, count, axis) in enumerate(PARTS):
        places = (x, y) if axis == "x" else (y, x)
        ids = (x_id, y_id) if axis == "x" else (y_id, x_id)
        names = ("own", "cs", "cr", "fs", "fr", "line", "ss", "sr")
        part = dict(zip(names, refs[: len(names)]))
        del refs[: len(names)]
        part.update(n=n, first_z=first_z, count=count, axis=axis, places=places, ids=ids)
        parts.append(part)

    def owned(place, parity):
        return pl.ds(pl.multiple_of((2 * place + parity) * 16, 16), 16)

    def shifted(low, high, off, turn):
        return jnp.where(lane < 128 - off, pltpu.roll(low, turn, 1), pltpu.roll(high, turn, 1))

    def deal(part):
        own, cs, n = part["own"], part["cs"], part["n"]
        if part["axis"] == "x":
            low, high = span_of(part["first_z"], part["count"])
            part["core"] = [
                remote(gsum.at[owned(xx, 1 - core), low:high], part["cr"].at[xx], core_s.at[n], core_r.at[n], mate)
                for xx in range(NX)
            ]
        else:

            @pl.loop(0, part["count"] * NY, unroll=4)
            def _(i):
                zl, yy = lax.div(i, NY), lax.rem(i, NY)
                start = ROWS * ((part["first_z"] + zl) * NY + yy)
                tile = lax.div(start, 128)
                off = start - tile * 128
                turn = lax.rem(128 - off, 128)
                first = pl.ds(pl.multiple_of(tile * 128, 128), 128)
                second = pl.ds(pl.multiple_of(tile * 128 + 128, 128), 128)
                lanes = pl.ds(pl.multiple_of(zl * 128, 128), 128)
                for xx in range(NX):
                    mine, theirs = owned(xx, core), owned(xx, 1 - core)
                    cs[yy, xx, :, lanes] = shifted(gsum[theirs, first], gsum[theirs, second], off, turn)
                    own[yy, xx, :, lanes] = shifted(gsum[mine, first], gsum[mine, second], off, turn)

            part["core"] = [remote(cs, part["cr"], core_s.at[n], core_r.at[n], mate)]
        for copy in part["core"]:
            copy.start()

    def first_stage(part):
        own, cr, fs, n = part["own"], part["cr"], part["fs"], part["n"]
        remote(cr, cr, core_s.at[n], core_r.at[n], mate).wait_recv()
        if part["axis"] == "x":
            low, high = span_of(part["first_z"], part["count"])
            for xx in range(NX):
                fs[xx] = (gsum[owned(xx, core), low:high] + cr[xx]).astype(BF16)
        else:

            @pl.loop(0, 16, unroll=2)
            def _(i):
                j, m = lax.div(i, 4), lax.rem(i, 4)
                total = own[j, m] + cr[j, m]
                own[j, m] = total
                fs[j, m] = total.astype(BF16)

        part["first"] = []
        for k in (2, 1, 3):
            there = lax.rem(part["places"][0] + k, 4)
            copy = remote(fs.at[there], part["fr"].at[k - 1], first_s.at[n], first_r.at[n], part["ids"][0](there))
            copy.start()
            part["first"].append(copy)

    def second_stage(part):
        own, cr, fr, line, ss, n = part["own"], part["cr"], part["fr"], part["line"], part["ss"], part["n"]
        remote(fr, fr, first_s.at[n], first_r.at[n], mate).wait_recv()
        if part["axis"] == "x":
            low, high = span_of(part["first_z"], part["count"])
            width = high - low
            own[:, 0:width] = (
                gsum[owned(x, core), low:high]
                + cr[x]
                + fr[0].astype(F32)
                + fr[1].astype(F32)
                + fr[2].astype(F32)
            )
            own[:, width:] = jnp.zeros((16, 128), F32)
            for i in range(part["count"] * NY):
                zl, yy = i // NY, i % NY
                start = ROWS * (part["first_z"] * NY + i) - low
                tile, off = start // 128, start % 128
                block = own[:, tile * 128 : tile * 128 + 128]
                if off:
                    block = shifted(block, own[:, tile * 128 + 128 : tile * 128 + 256], off, 128 - off)
                line[yy, :, zl * 128 : zl * 128 + 128] = block
        else:
            for j in range(4):
                line[j] = own[y, j] + fr[0, j].astype(F32) + fr[1, j].astype(F32) + fr[2, j].astype(F32)
        for j in range(4):
            ss[j] = line[j].astype(BF16)
        part["second"] = []
        for k in (2, 1, 3):
            there = lax.rem(part["places"][1] + k, 4)
            copy = remote(ss.at[there], part["sr"].at[k - 1], second_s.at[n], second_r.at[n], part["ids"][1](there))
            copy.start()
            part["second"].append(copy)

    def settle(part):
        sr, n = part["sr"], part["n"]
        remote(sr, sr, second_s.at[n], second_r.at[n], mate).wait_recv()
        total = part["line"][part["places"][1]] + sr[0].astype(F32) + sr[1].astype(F32) + sr[2].astype(F32)
        for j in range(part["count"]):
            piece = total[:, j * 128 : (j + 1) * 128]
            zo[part["first_z"] + j] = piece
            zs[part["first_z"] + j] = piece.astype(BF16)

    def z_copy(k):
        zz = lax.rem(z + k, NZ)
        return zz, remote(zs.at[zz], zr.at[k - 1], z_s, z_r, z_id(zz))

    def send_along_z(first, last):
        for k in FAR_FIRST:
            zz, copy = z_copy(k)

            @pl.when(jnp.logical_and(zz >= first, zz < last))
            def _():
                copy.start()

    gsum[:, 27 * C :] = jnp.zeros((CO, 128), F32)
    for span, term in filter_term(2, 0, 2 * PX, act[...]):
        gsum[:, span] = term
    deal(parts[0])
    for span, term in filter_term(1, PX, 2 * PX, act[0:PX]):
        gsum[:, span] = term
    loads[11].wait()
    agrad[...] = input_term(2, 0, 2 * PX)
    agrad[0:PX, :] += input_term(1, PX, 2 * PX)
    pl.semaphore_wait(relay, 2)
    signal(relay_far, z_id(lax.rem(z + 4, NZ)))
    signal(relay_far, z_id(lax.rem(z + NZ - 4, NZ)))
    pl.semaphore_wait(relay_plane, 3)
    signal(relay_mate, mate)
    first_stage(parts[0])

    @pl.when(ctx == 0)
    def _():
        for span, term in filter_term(1, 0, PX, act[0:PX]):
            gsum[:, span] += term
        for span, term in filter_term(0, 0, PX, act[0:PX]):
            gsum[:, span] = term
        for span, term in filter_term(0, PX, 2 * PX, act[0:PX]):
            gsum[:, span] += term
        agrad[0:PX, :] += input_term(1, 0, PX) + input_term(0, 0, PX) + input_term(0, PX, 2 * PX)

    @pl.when(ctx != 0)
    def _():
        gsum[:, 0 : 9 * C] = jnp.zeros((CO, 9 * C), F32)

    def take_halo(f):
        halo_copies[f].wait_recv()
        lay_patches(2 + f, jnp.where(ctx == NCTX - 1, 0.0, halo[f].astype(F32).reshape(PX, CO)))

    take_halo(0)
    for span, term in filter_term(1, 2 * PX, 3 * PX, act[PX : 2 * PX]):
        gsum[:, span] += term
    deal(parts[1])
    deal(parts[2])
    take_halo(1)
    agrad[...] += input_term(0, 2 * PX, 4 * PX)
    agrad[PX : 2 * PX, :] += input_term(1, 2 * PX, 3 * PX)

    pools[...] = jnp.zeros_like(pools)

    @pl.loop(0, 2 * H, unroll=4)
    def _(i):
        f, h = lax.div(i, H), lax.rem(i, H)
        hh = lax.div(h, 4)
        pre = agrad[pl.ds(pl.multiple_of(i * W, W), W), :] * dmod[i]
        image[0, f, h] = (pre * maps[0, hh] * gamma * rstd_c).astype(BF16)
        pools[0, hh] += pre * norm[i]
        pools[1, hh] += pre

    write_image = pltpu.make_async_copy(image, fg_ref, image_s)
    write_image.start()
    normed_pool = exact(spread, pools[0].reshape(2 * W, C), ((0,), (0,)))
    shift_pool = exact(spread, pools[1].reshape(2 * W, C), ((0,), (0,)))
    scale_pool = normed_pool * gamma + shift_pool * beta
    tab = tabs[...]
    rows = [
        exact(lat, scale_pool, ((1,), (0,))),
        exact(lat, shift_pool, ((1,), (0,))),
        jnp.concatenate(
            [
                jnp.sum(tab * normed_pool, axis=0, keepdims=True),
                jnp.sum(tab * shift_pool, axis=0, keepdims=True),
                jnp.sum(scale_pool, axis=0, keepdims=True),
                jnp.sum(shift_pool, axis=0, keepdims=True),
                jnp.zeros((4, C), F32),
            ],
            axis=0,
        ),
    ]
    for t in range(TILES):
        block, half = t // 2, t % 2
        source = rows[block // 2][(block % 2) * 8 : (block % 2) * 8 + 8]
        small[t] = source[:, half * 128 : (half + 1) * 128]

    chip = y * NX + x
    owner = jnp.logical_and(core == 0, chip < TILES)

    def tile_plane(t):
        return lax.div(t, NX) * 8 + 2 * lax.rem(t, NX)

    pl.semaphore_wait(relay_mate, 1)

    @pl.loop(0, TILES)
    def _(t):
        @pl.when(tile_plane(t) != plane)
        def _():
            remote(small.at[t], gathered.at[plane], small_s, small_r, plane_id(tile_plane(t))).start()

    first_stage(parts[1])
    first_stage(parts[2])
    for span, term in filter_term(0, 2 * PX, 4 * PX, act[...]):
        gsum[:, span] += term
    deal(parts[3])
    deal(parts[4])
    for part in parts[3:]:
        first_stage(part)

    second_stage(parts[0])
    latent_sum = exact(scale_pool, ws_ref[...], ((1,), (1,))) + exact(shift_pool, wh_ref[...], ((1,), (1,)))
    ls[...] = jnp.zeros_like(ls)
    ls[:, 0:CZ] = latent_sum
    lat_copy = remote(ls, lr, lat_s, lat_r, sharer)
    lat_copy.start()

    pl.semaphore_wait(relay_far, 2)
    @pl.when(owner)
    def _():
        others = gathered.at[0:31]
        remote(others, others, small_s, small_r, mate).wait_recv()

        gathered[plane] = small[chip]
        crossed[z] = jnp.sum(gathered[...], axis=0)

        @pl.loop(1, NZ)
        def _(k):
            zz = lax.rem(z + k, NZ)
            remote(crossed.at[z], crossed.at[z], cross_s, cross_r, z_id(zz)).start()

    second_stage(parts[1])
    second_stage(parts[2])
    second_stage(parts[3])
    second_stage(parts[4])
    settle(parts[0])
    send_along_z(*GROUPS[0])

    settle(parts[1])
    settle(parts[2])
    send_along_z(*GROUPS[1])
    settle(parts[3])
    settle(parts[4])
    send_along_z(*GROUPS[2])

    @pl.when(owner)
    def _():
        others = crossed.at[0 : NZ - 1]
        remote(others, others, cross_s, cross_r, mate).wait_recv()
        final[chip] = jnp.sum(crossed[...], axis=0)

        @pl.loop(1, 32)
        def _(k):
            p = lax.rem(plane + k, 32)
            remote(final.at[chip], final.at[chip], final_s, final_r, plane_id(p)).start()

    lat_copy.wait_recv()
    half = pl.ds(pl.multiple_of(lax.rem(ctx, 2) * 8, 8), 8)
    lg_ref[...] = ls[half, :] + lr[half, :]

    remote(zr, zr, z_s, z_r, mate).wait_recv()
    total = zo[z]
    for k in range(NZ - 1):
        total = total + zr[k].astype(F32)
    kg_ref[...] = total

    @pl.when(owner)
    def _():
        others = final.at[0 : TILES - 1]
        remote(others, others, final_s, final_r, mate).wait_recv()

    @pl.when(jnp.logical_not(owner))
    def _():
        remote(final, final, final_s, final_r, mate).wait_recv()

    write_image.wait()
    remote(halo, halo, halo_s, halo_r.at[0], mate).wait_send()
    lat_copy.wait_send()
    for part in parts:
        n = part["n"]
        remote(part["cr"], part["cr"], core_s.at[n], core_r.at[n], mate).wait_send()
        remote(part["fr"], part["fr"], first_s.at[n], first_r.at[n], mate).wait_send()
        remote(part["sr"], part["sr"], second_s.at[n], second_r.at[n], mate).wait_send()
    remote(zr, zr, z_s, z_r, mate).wait_send()

    @pl.when(owner)
    def _():
        tiles = small.at[0 : TILES - 1]
        remote(tiles, tiles, small_s, small_r, mate).wait_send()
        places = crossed.at[0 : NZ - 1]
        remote(places, places, cross_s, cross_r, mate).wait_send()
        copies = gathered.at[0:31]
        remote(copies, copies, final_s, final_r, mate).wait_send()

    @pl.when(jnp.logical_not(owner))
    def _():
        remote(small, small, small_s, small_r, mate).wait_send()


def finish(fg_in, kg_in, sums, lg_in, fg_ref, kg_ref, mod_ref, vec_ref, lg_ref):
    fg_ref[...] = fg_in[...]
    kg_ref[...] = kg_in[:, 0:ROWS]
    for t in range(8):
        block, half = t // 2, t % 2
        mod_ref[block // 2, (block % 2) * 8 : (block % 2) * 8 + 8, half * 128 : (half + 1) * 128] = sums[t]
    for half in range(2):
        vec_ref[:, half * 128 : (half + 1) * 128] = sums[8 + half, 0:4]
    lg_ref[0, 0] = lg_in[:, 0:CZ]


def local(features, grad_out, mean_saved, rstd_saved, latent, *others):
    operands = (features, grad_out, mean_saved, rstd_saved, jnp.transpose(latent, (0, 2, 3, 1))) + others
    vmem = pl.BlockSpec(memory_space=pltpu.VMEM)
    dma = pltpu.SemaphoreType.DMA
    buffers = []
    for first_z, count, axis in PARTS:
        wide = (16, count * 128)
        low, high = span_of(first_z, count)
        first = (16, high - low) if axis == "x" else (4,) + wide
        buffers += [
            pltpu.VMEM((16, high - low + 128) if axis == "x" else (4,) + first, F32),
            pltpu.VMEM((8, 128) if axis == "x" else (4,) + first, F32),
            pltpu.VMEM((4,) + first, F32),
            pltpu.VMEM((4,) + first, BF16),
            pltpu.VMEM((3,) + first, BF16),
            pltpu.VMEM((4,) + wide, F32),
            pltpu.VMEM((4,) + wide, BF16),
            pltpu.VMEM((3,) + wide, BF16),
        ]
    parts = len(PARTS)
    partial = pl.pallas_call(
        body,
        out_shape=(
            jax.ShapeDtypeStruct((1, 2, H, W, C), BF16),
            jax.ShapeDtypeStruct((16, 128), F32),
            jax.ShapeDtypeStruct((TILES, 8, 128), F32),
            jax.ShapeDtypeStruct((8, 128), F32),
        ),
        in_specs=[pl.BlockSpec(memory_space=pltpu.HBM)] * 12,
        out_specs=(pl.BlockSpec(memory_space=pl.ANY),) + (vmem,) * 3,
        scratch_shapes=[
            pltpu.VMEM((1, 2, H, W, C), BF16),
            pltpu.VMEM((1, 2, H, W, CO), BF16),
            pltpu.VMEM((1, G), F32),
            pltpu.VMEM((1, G), F32),
            pltpu.VMEM((1, CZ, LP, NCTX // 2), F32),
            pltpu.VMEM((C,), F32),
            pltpu.VMEM((C,), F32),
            pltpu.VMEM((CZ, C), F32),
            pltpu.VMEM((C,), F32),
            pltpu.VMEM((CZ, C), F32),
            pltpu.VMEM((C,), F32),
            pltpu.VMEM((27 * C, CO), BF16),
            pltpu.VMEM((2, H, W, CO), BF16),
            pltpu.VMEM((2 * PX, C), BF16),
            pltpu.VMEM((2 * H, W, C), F32),
            pltpu.VMEM((2 * H, W, C), F32),
            pltpu.VMEM((4 * PX, 9 * CO), BF16),
            pltpu.VMEM((CO, 27 * C + 128), F32),
            pltpu.VMEM((2 * PX, C), F32),
            pltpu.VMEM((LP, C), F32),
            pltpu.VMEM((2, 2, W, C), F32),
            pltpu.VMEM((2, 2, W, C), F32),
            pltpu.VMEM((NZ, 16, 128), F32),
            pltpu.VMEM((NZ, 16, 128), BF16),
            pltpu.VMEM((NZ - 1, 16, 128), BF16),
            pltpu.VMEM((TILES, 8, 128), F32),
            pltpu.VMEM((32, 8, 128), F32),
            pltpu.VMEM((NZ, 8, 128), F32),
            pltpu.VMEM((16, 128), F32),
            pltpu.VMEM((16, 128), F32),
            dma((12,)),
            dma,
            dma((2,)),
            dma((parts,)),
            dma((parts,)),
            dma((parts,)),
            dma((parts,)),
            dma((parts,)),
            dma((parts,)),
            dma,
            dma,
            dma,
            dma,
            dma,
            dma,
            dma,
            dma,
            dma,
            dma,
            pltpu.SemaphoreType.REGULAR,
            pltpu.SemaphoreType.REGULAR,
            pltpu.SemaphoreType.REGULAR,
            pltpu.SemaphoreType.REGULAR,
            pltpu.VMEM((1, 2, H, W, C), BF16),
            dma,
        ]
        + buffers,
        compiler_params=pltpu.CompilerParams(
            collective_id=0, has_side_effects=True, vmem_limit_bytes=36 * 1024 * 1024
        ),
    )(*(pltpu.with_memory_space_constraint(value, pltpu.HBM) for value in operands))
    fg, kg, mod, vec, lg = pl.pallas_call(
        finish,
        out_shape=(
            jax.ShapeDtypeStruct((1, 2, H, W, C), BF16),
            jax.ShapeDtypeStruct((16, ROWS), F32),
            jax.ShapeDtypeStruct((2, CZ, C), F32),
            jax.ShapeDtypeStruct((4, C), F32),
            jax.ShapeDtypeStruct((1, 1, LP // 2, CZ), F32),
        ),
        in_specs=[vmem] * 4,
        out_specs=(vmem,) * 5,
        compiler_params=pltpu.CompilerParams(vmem_limit_bytes=8 * 1024 * 1024),
    )(*partial)
    return fg, kg.T, mod, vec, jnp.swapaxes(lg, 2, 3)


def solution(mesh):
    placed = (
        P("vid", "ctx", None, None, None),
        P("vid", "ctx", None, None, None),
        P("vid", None),
        P("vid", None),
        P("vid", None, None, None),
        P(),
        P(),
        P(),
        P(),
        P(),
        P(),
        P(),
    )
    return jax.shard_map(
        local,
        mesh=mesh,
        in_specs=placed,
        out_specs=(
            P("vid", "ctx", None, None, None),
            P("ctx", "vid"),
            P(),
            P(),
            P("vid", "ctx", None, None),
        ),
        check_vma=False,
    )
```

```python
import jax
import jax.numpy as jnp
from jax import lax
from jax.experimental import pallas as pl
from jax.experimental.pallas import tpu as pltpu
from jax.sharding import PartitionSpec as P

MESH = pl.DeviceIdType.MESH
F32 = jnp.float32
BF16 = jnp.bfloat16
HIGHEST = lax.Precision.HIGHEST

NX, NY, NZ = 4, 4, 16
NCTX = NY * NZ
H, W, C, CO, CZ, G, LP = 8, 32, 256, 128, 16, 32, 16
PX = H * W
ROWS = 108
TILES = 10
PARTS = ((11, 5, "x"), (6, 3, "x"), (9, 2, "y"), (0, 3, "x"), (3, 3, "y"))
GROUPS = ((11, 16), (6, 11), (0, 6))
FAR_FIRST = (8, 7, 9, 6, 10, 5, 11, 4, 12, 3, 13, 2, 14, 1, 15)


def span_of(first_z, count):
    low = ROWS * NY * first_z // 128
    high = -(-ROWS * NY * (first_z + count) // 128)
    return low * 128, high * 128


def exact(lhs, rhs, dims):
    return lax.dot_general(lhs, rhs, (dims, ((), ())), precision=HIGHEST, preferred_element_type=F32)


def wide_dot(lhs, rhs, dims):
    return lax.dot_general(lhs, rhs, (dims, ((), ())), preferred_element_type=F32)


def body(
    feat_hbm, grad_hbm, mean_hbm, rstd_hbm, lat_hbm, gamma_hbm, beta_hbm, ws_hbm, bs_hbm, wh_hbm, bh_hbm, kern_hbm,
    fg_ref, kg_ref, final, lg_ref,
    feat_ref, grad_ref, mean_ref, rstd_ref, lat_ref, gamma_ref, beta_ref, ws_ref, bs_ref, wh_ref, bh_ref, kern,
    halo, act, dmod, norm, patch, gsum, agrad, tabs, maps, pools,
    zo, zs, zr, small, gathered, crossed, ls, lr,
    load_sems, halo_s, halo_r, core_s, core_r, first_s, first_r, second_s, second_r, z_s, z_r,
    small_s, small_r, cross_s, cross_r, final_s, final_r, lat_s, lat_r, relay, relay_far, relay_plane, relay_mate, image, image_s, turned,
    *part_refs,
):
    ctx = lax.axis_index("ctx")
    vid = lax.axis_index("vid")
    z, y = lax.div(ctx, NY), lax.rem(ctx, NY)
    x, core = lax.div(vid, 2), lax.rem(vid, 2)
    plane = y * 8 + vid

    def plane_id(p):
        return (z * NY + lax.div(p, 8), lax.rem(p, 8))

    def z_id(zz):
        return (zz * NY + y, vid)

    def x_id(xx):
        return (ctx, 2 * xx + core)

    def y_id(yy):
        return (z * NY + yy, vid)

    mate = (ctx, vid + 1 - 2 * core)
    sharer = (ctx + 1 - 2 * lax.rem(ctx, 2), vid)
    before = (lax.rem(ctx + NCTX - 1, NCTX), vid)
    after = (lax.rem(ctx + 1, NCTX), vid)

    loads = [
        pltpu.make_async_copy(source, target, load_sems.at[n])
        for n, (source, target) in enumerate(
            (
                (lat_hbm, lat_ref),
                (mean_hbm, mean_ref),
                (rstd_hbm, rstd_ref),
                (ws_hbm, ws_ref),
                (wh_hbm, wh_ref),
                (bs_hbm, bs_ref),
                (bh_hbm, bh_ref),
                (gamma_hbm, gamma_ref),
                (beta_hbm, beta_ref),
                (feat_hbm, feat_ref),
                (grad_hbm, grad_ref),
                (kern_hbm, kern),
            )
        )
    ]
    for load in loads:
        load.start()

    barrier = pltpu.get_barrier_semaphore()

    def signal(semaphore, device):
        pl.semaphore_signal(semaphore, inc=1, device_id=device, device_id_type=MESH)

    signal(barrier, before)
    signal(barrier, after)
    signal(barrier, mate)
    for k in range(1, 4):
        signal(barrier, x_id(lax.rem(x + k, NX)))
        signal(barrier, y_id(lax.rem(y + k, NY)))
    for k in (2, NZ - 2, 1, NZ - 1):
        signal(barrier, z_id(lax.rem(z + k, NZ)))

    def remote(src, dst, send, recv, device):
        return pltpu.make_async_remote_copy(
            src_ref=src, dst_ref=dst, send_sem=send, recv_sem=recv, device_id=device, device_id_type=MESH
        )

    pl.semaphore_wait(barrier, 13)
    halo_copies = [
        remote(grad_hbm.at[0, f], halo.at[f], halo_s, halo_r.at[f], before) for f in range(2)
    ]
    for copy in halo_copies:
        copy.start()
    signal(relay, z_id(lax.rem(z + 2, NZ)))
    signal(relay, z_id(lax.rem(z + NZ - 2, NZ)))
    for k in range(1, 4):
        signal(relay_plane, y_id(lax.rem(y + k, NY)))

    for load in loads[:9]:
        load.wait()

    pick = (lax.broadcasted_iota(jnp.int32, (G, C), 1) // (C // G) == lax.broadcasted_iota(jnp.int32, (G, C), 0)).astype(F32)
    saved = jnp.concatenate([mean_ref[...], rstd_ref[...], jnp.zeros((6, G), F32)], axis=0)
    saved = exact(saved, pick, ((1,), (0,)))
    mean_c, rstd_c = saved[0:1], saved[1:2]
    gamma = gamma_ref[...].reshape(1, C)
    beta = beta_ref[...].reshape(1, C)
    here = (lax.broadcasted_iota(jnp.int32, (NCTX // 2, 128), 0) == lax.div(ctx, 2)).astype(F32)
    lat = exact(lat_ref[0].reshape(CZ * LP, NCTX // 2), here, ((1,), (0,))).reshape(CZ, LP, 128)
    corner = lax.broadcasted_iota(jnp.int32, (CZ, LP, 128), 1) == lax.broadcasted_iota(jnp.int32, (CZ, LP, 128), 2)
    lat = jnp.sum(jnp.where(corner, lat, 0.0), axis=1)[:, :LP]
    weights = jnp.concatenate([ws_ref[...], wh_ref[...]], axis=1)
    bias = jnp.concatenate([bs_ref[...].reshape(1, C), bh_ref[...].reshape(1, C)], axis=1)
    both_tabs = exact(lat, weights, ((0,), (0,))) + bias
    tabs[...] = both_tabs[:, :C]
    pix = lax.broadcasted_iota(jnp.int32, (2 * W, LP), 0)
    latent_pixel = lax.broadcasted_iota(jnp.int32, (2 * W, LP), 1)
    spread = ((pix // W) * (W // 4) + (pix % W) // 4 == latent_pixel).astype(F32)
    both_maps = exact(spread, both_tabs, ((1,), (0,)))
    maps[0] = both_maps[:, :C].reshape(2, W, C)
    maps[1] = both_maps[:, C:].reshape(2, W, C)

    loads[9].wait()

    @pl.loop(0, 2 * H, unroll=4)
    def _(i):
        f, h = lax.div(i, H), lax.rem(i, H)
        hh = lax.div(h, 4)
        normed = (feat_ref[0, f, h].astype(F32) - mean_c) * rstd_c
        modulated = (normed * gamma + beta) * maps[0, hh] + maps[1, hh]
        s = jax.nn.sigmoid(modulated)
        norm[i] = normed
        dmod[i] = s * (1.0 + modulated * (1.0 - s))
        act[pl.ds(pl.multiple_of(i * W, W), W), :] = (modulated * s).astype(BF16)

    loads[10].wait()
    col = lax.broadcasted_iota(jnp.int32, (PX, CO), 0) % W

    def lay_patches(f, g):
        for c in range(3):
            if c == 0:
                moved = jnp.where(col == W - 1, 0.0, pltpu.roll(g, PX - 1, 0))
            elif c == 1:
                moved = g
            else:
                moved = jnp.where(col == 0, 0.0, pltpu.roll(g, 1, 0))
            moved = moved.astype(BF16)
            blank = jnp.zeros((W, CO), BF16)
            for b in range(3):
                lanes = slice((b * 3 + c) * CO, (b * 3 + c + 1) * CO)
                base = f * PX
                if b == 0:
                    patch[base : base + PX - W, lanes] = moved[W:]
                    patch[base + PX - W : base + PX, lanes] = blank
                elif b == 1:
                    patch[base : base + PX, lanes] = moved
                else:
                    patch[base : base + W, lanes] = blank
                    patch[base + W : base + PX, lanes] = moved[: PX - W]

    for f in range(2):
        lay_patches(f, grad_ref[0, f].astype(F32).reshape(PX, CO))

    def filter_term(a, first, last, images):
        for bc in range(9):
            lanes = slice(bc * CO, (bc + 1) * CO)
            tap = a * 9 + bc
            yield slice(tap * C, (tap + 1) * C), wide_dot(patch[first:last, lanes], images, ((0,), (0,)))

    def turn_taps(a):
        for bc in range(9):
            tap = a * 9 + bc
            turned[a, bc * CO : (bc + 1) * CO, :] = kern[tap * C : (tap + 1) * C, :].T

    def input_term(a, first, last):
        return wide_dot(patch[first:last, :], turned[a], ((1,), (0,)))

    lane = lax.broadcasted_iota(jnp.int32, (16, 128), 1)
    parts = []
    refs = list(part_refs)
    for n, (first_z, count, axis) in enumerate(PARTS):
        places = (x, y) if axis == "x" else (y, x)
        ids = (x_id, y_id) if axis == "x" else (y_id, x_id)
        names = ("own", "cs", "cr", "fs", "fr", "line", "ss", "sr")
        part = dict(zip(names, refs[: len(names)]))
        del refs[: len(names)]
        part.update(n=n, first_z=first_z, count=count, axis=axis, places=places, ids=ids)
        parts.append(part)

    def owned(place, parity):
        return pl.ds(pl.multiple_of((2 * place + parity) * 16, 16), 16)

    def shifted(low, high, off, turn):
        return jnp.where(lane < 128 - off, pltpu.roll(low, turn, 1), pltpu.roll(high, turn, 1))

    def deal(part):
        own, cs, n = part["own"], part["cs"], part["n"]
        if part["axis"] == "x":
            low, high = span_of(part["first_z"], part["count"])
            part["core"] = [
                remote(gsum.at[owned(xx, 1 - core), low:high], part["cr"].at[xx], core_s.at[n], core_r.at[n], mate)
                for xx in range(NX)
            ]
        else:

            @pl.loop(0, part["count"] * NY, unroll=4)
            def _(i):
                zl, yy = lax.div(i, NY), lax.rem(i, NY)
                start = ROWS * ((part["first_z"] + zl) * NY + yy)
                tile = lax.div(start, 128)
                off = start - tile * 128
                turn = lax.rem(128 - off, 128)
                first = pl.ds(pl.multiple_of(tile * 128, 128), 128)
                second = pl.ds(pl.multiple_of(tile * 128 + 128, 128), 128)
                lanes = pl.ds(pl.multiple_of(zl * 128, 128), 128)
                for xx in range(NX):
                    mine, theirs = owned(xx, core), owned(xx, 1 - core)
                    cs[yy, xx, :, lanes] = shifted(gsum[theirs, first], gsum[theirs, second], off, turn)
                    own[yy, xx, :, lanes] = shifted(gsum[mine, first], gsum[mine, second], off, turn)

            part["core"] = [remote(cs, part["cr"], core_s.at[n], core_r.at[n], mate)]
        for copy in part["core"]:
            copy.start()

    def first_stage(part):
        own, cr, fs, n = part["own"], part["cr"], part["fs"], part["n"]
        remote(cr, cr, core_s.at[n], core_r.at[n], mate).wait_recv()
        if part["axis"] == "x":
            low, high = span_of(part["first_z"], part["count"])
            for xx in range(NX):
                fs[xx] = (gsum[owned(xx, core), low:high] + cr[xx]).astype(BF16)
        else:

            @pl.loop(0, 16, unroll=2)
            def _(i):
                j, m = lax.div(i, 4), lax.rem(i, 4)
                total = own[j, m] + cr[j, m]
                own[j, m] = total
                fs[j, m] = total.astype(BF16)

        part["first"] = []
        for k in (2, 1, 3):
            there = lax.rem(part["places"][0] + k, 4)
            copy = remote(fs.at[there], part["fr"].at[k - 1], first_s.at[n], first_r.at[n], part["ids"][0](there))
            copy.start()
            part["first"].append(copy)

    def second_stage(part):
        own, cr, fr, line, ss, n = part["own"], part["cr"], part["fr"], part["line"], part["ss"], part["n"]
        remote(fr, fr, first_s.at[n], first_r.at[n], mate).wait_recv()
        if part["axis"] == "x":
            low, high = span_of(part["first_z"], part["count"])
            width = high - low
            own[:, 0:width] = (
                gsum[owned(x, core), low:high]
                + cr[x]
                + fr[0].astype(F32)
                + fr[1].astype(F32)
                + fr[2].astype(F32)
            )
            own[:, width:] = jnp.zeros((16, 128), F32)
            for i in range(part["count"] * NY):
                zl, yy = i // NY, i % NY
                start = ROWS * (part["first_z"] * NY + i) - low
                tile, off = start // 128, start % 128
                block = own[:, tile * 128 : tile * 128 + 128]
                if off:
                    block = shifted(block, own[:, tile * 128 + 128 : tile * 128 + 256], off, 128 - off)
                line[yy, :, zl * 128 : zl * 128 + 128] = block
        else:
            for j in range(4):
                line[j] = own[y, j] + fr[0, j].astype(F32) + fr[1, j].astype(F32) + fr[2, j].astype(F32)
        for j in range(4):
            ss[j] = line[j].astype(BF16)
        part["second"] = []
        for k in (2, 1, 3):
            there = lax.rem(part["places"][1] + k, 4)
            copy = remote(ss.at[there], part["sr"].at[k - 1], second_s.at[n], second_r.at[n], part["ids"][1](there))
            copy.start()
            part["second"].append(copy)

    def settle(part):
        sr, n = part["sr"], part["n"]
        remote(sr, sr, second_s.at[n], second_r.at[n], mate).wait_recv()
        total = part["line"][part["places"][1]] + sr[0].astype(F32) + sr[1].astype(F32) + sr[2].astype(F32)
        for j in range(part["count"]):
            piece = total[:, j * 128 : (j + 1) * 128]
            zo[part["first_z"] + j] = piece
            zs[part["first_z"] + j] = piece.astype(BF16)

    def z_copy(k):
        zz = lax.rem(z + k, NZ)
        return zz, remote(zs.at[zz], zr.at[k - 1], z_s, z_r, z_id(zz))

    def send_along_z(first, last):
        for k in FAR_FIRST:
            zz, copy = z_copy(k)

            @pl.when(jnp.logical_and(zz >= first, zz < last))
            def _():
                copy.start()

    gsum[:, 27 * C :] = jnp.zeros((CO, 128), F32)
    for span, term in filter_term(2, 0, 2 * PX, act[...]):
        gsum[:, span] = term
    deal(parts[0])
    for span, term in filter_term(1, PX, 2 * PX, act[0:PX]):
        gsum[:, span] = term
    loads[11].wait()
    for a in (2, 1, 0):
        turn_taps(a)
    agrad[...] = input_term(2, 0, 2 * PX)
    agrad[0:PX, :] += input_term(1, PX, 2 * PX)
    pl.semaphore_wait(relay, 2)
    signal(relay_far, z_id(lax.rem(z + 4, NZ)))
    signal(relay_far, z_id(lax.rem(z + NZ - 4, NZ)))
    pl.semaphore_wait(relay_plane, 3)
    signal(relay_mate, mate)
    first_stage(parts[0])

    @pl.when(ctx == 0)
    def _():
        for span, term in filter_term(1, 0, PX, act[0:PX]):
            gsum[:, span] += term
        for span, term in filter_term(0, 0, PX, act[0:PX]):
            gsum[:, span] = term
        for span, term in filter_term(0, PX, 2 * PX, act[0:PX]):
            gsum[:, span] += term
        agrad[0:PX, :] += input_term(1, 0, PX) + input_term(0, 0, PX) + input_term(0, PX, 2 * PX)

    @pl.when(ctx != 0)
    def _():
        gsum[:, 0 : 9 * C] = jnp.zeros((CO, 9 * C), F32)

    def take_halo(f):
        halo_copies[f].wait_recv()
        lay_patches(2 + f, jnp.where(ctx == NCTX - 1, 0.0, halo[f].astype(F32).reshape(PX, CO)))

    take_halo(0)
    for span, term in filter_term(1, 2 * PX, 3 * PX, act[PX : 2 * PX]):
        gsum[:, span] += term
    deal(parts[1])
    deal(parts[2])
    take_halo(1)
    agrad[...] += input_term(0, 2 * PX, 4 * PX)
    agrad[PX : 2 * PX, :] += input_term(1, 2 * PX, 3 * PX)

    pools[...] = jnp.zeros_like(pools)

    @pl.loop(0, 2 * H, unroll=4)
    def _(i):
        f, h = lax.div(i, H), lax.rem(i, H)
        hh = lax.div(h, 4)
        pre = agrad[pl.ds(pl.multiple_of(i * W, W), W), :] * dmod[i]
        image[0, f, h] = (pre * maps[0, hh] * gamma * rstd_c).astype(BF16)
        pools[0, hh] += pre * norm[i]
        pools[1, hh] += pre

    write_image = pltpu.make_async_copy(image, fg_ref, image_s)
    write_image.start()
    fields = jnp.concatenate([pools[0].reshape(2 * W, C), pools[1].reshape(2 * W, C)], axis=1)
    pooled = exact(spread, fields, ((0,), (0,)))
    normed_pool, shift_pool = pooled[:, :C], pooled[:, C:]
    scale_pool = normed_pool * gamma + shift_pool * beta
    projected = exact(lat, jnp.concatenate([scale_pool, shift_pool], axis=1), ((1,), (0,)))
    tab = tabs[...]
    rows = [
        projected[:, :C],
        projected[:, C:],
        jnp.concatenate(
            [
                jnp.sum(tab * normed_pool, axis=0, keepdims=True),
                jnp.sum(tab * shift_pool, axis=0, keepdims=True),
                jnp.sum(scale_pool, axis=0, keepdims=True),
                jnp.sum(shift_pool, axis=0, keepdims=True),
                jnp.zeros((4, C), F32),
            ],
            axis=0,
        ),
    ]
    for t in range(TILES):
        block, half = t // 2, t % 2
        source = rows[block // 2][(block % 2) * 8 : (block % 2) * 8 + 8]
        small[t] = source[:, half * 128 : (half + 1) * 128]

    chip = y * NX + x
    owner = jnp.logical_and(core == 0, chip < TILES)

    def tile_plane(t):
        return lax.div(t, NX) * 8 + 2 * lax.rem(t, NX)

    pl.semaphore_wait(relay_mate, 1)

    @pl.loop(0, TILES)
    def _(t):
        @pl.when(tile_plane(t) != plane)
        def _():
            remote(small.at[t], gathered.at[plane], small_s, small_r, plane_id(tile_plane(t))).start()

    first_stage(parts[1])
    first_stage(parts[2])
    for span, term in filter_term(0, 2 * PX, 4 * PX, act[...]):
        gsum[:, span] += term
    deal(parts[3])
    deal(parts[4])
    for part in parts[3:]:
        first_stage(part)

    second_stage(parts[0])
    latent_sum = exact(scale_pool, ws_ref[...], ((1,), (1,))) + exact(shift_pool, wh_ref[...], ((1,), (1,)))
    ls[...] = jnp.zeros_like(ls)
    ls[:, 0:CZ] = latent_sum
    lat_copy = remote(ls, lr, lat_s, lat_r, sharer)
    lat_copy.start()

    second_stage(parts[1])
    second_stage(parts[2])
    pl.semaphore_wait(relay_far, 2)
    @pl.when(owner)
    def _():
        others = gathered.at[0:31]
        remote(others, others, small_s, small_r, mate).wait_recv()

        gathered[plane] = small[chip]
        crossed[z] = jnp.sum(gathered[...], axis=0)

        @pl.loop(1, NZ)
        def _(k):
            zz = lax.rem(z + k, NZ)
            remote(crossed.at[z], crossed.at[z], cross_s, cross_r, z_id(zz)).start()

    second_stage(parts[3])
    second_stage(parts[4])
    settle(parts[0])
    send_along_z(*GROUPS[0])

    settle(parts[1])
    settle(parts[2])
    send_along_z(*GROUPS[1])
    settle(parts[3])
    settle(parts[4])
    send_along_z(*GROUPS[2])

    @pl.when(owner)
    def _():
        others = crossed.at[0 : NZ - 1]
        remote(others, others, cross_s, cross_r, mate).wait_recv()
        final[chip] = jnp.sum(crossed[...], axis=0)

        @pl.loop(1, 32)
        def _(k):
            p = lax.rem(plane + k, 32)
            remote(final.at[chip], final.at[chip], final_s, final_r, plane_id(p)).start()

    lat_copy.wait_recv()
    half = pl.ds(pl.multiple_of(lax.rem(ctx, 2) * 8, 8), 8)
    lg_ref[...] = ls[half, :] + lr[half, :]

    remote(zr, zr, z_s, z_r, mate).wait_recv()
    total = zo[z]
    for k in range(NZ - 1):
        total = total + zr[k].astype(F32)
    kg_ref[...] = total

    @pl.when(owner)
    def _():
        others = final.at[0 : TILES - 1]
        remote(others, others, final_s, final_r, mate).wait_recv()

    @pl.when(jnp.logical_not(owner))
    def _():
        remote(final, final, final_s, final_r, mate).wait_recv()

    write_image.wait()
    remote(halo, halo, halo_s, halo_r.at[0], mate).wait_send()
    lat_copy.wait_send()
    for part in parts:
        n = part["n"]
        remote(part["cr"], part["cr"], core_s.at[n], core_r.at[n], mate).wait_send()
        remote(part["fr"], part["fr"], first_s.at[n], first_r.at[n], mate).wait_send()
        remote(part["sr"], part["sr"], second_s.at[n], second_r.at[n], mate).wait_send()
    remote(zr, zr, z_s, z_r, mate).wait_send()

    @pl.when(owner)
    def _():
        tiles = small.at[0 : TILES - 1]
        remote(tiles, tiles, small_s, small_r, mate).wait_send()
        places = crossed.at[0 : NZ - 1]
        remote(places, places, cross_s, cross_r, mate).wait_send()
        copies = gathered.at[0:31]
        remote(copies, copies, final_s, final_r, mate).wait_send()

    @pl.when(jnp.logical_not(owner))
    def _():
        remote(small, small, small_s, small_r, mate).wait_send()


def finish(fg_in, kg_in, sums, lg_in, fg_ref, kg_ref, mod_ref, vec_ref, lg_ref):
    fg_ref[...] = fg_in[...]
    kg_ref[...] = kg_in[:, 0:ROWS]
    for t in range(8):
        block, half = t // 2, t % 2
        mod_ref[block // 2, (block % 2) * 8 : (block % 2) * 8 + 8, half * 128 : (half + 1) * 128] = sums[t]
    for half in range(2):
        vec_ref[:, half * 128 : (half + 1) * 128] = sums[8 + half, 0:4]
    lg_ref[0, 0] = lg_in[:, 0:CZ]


def local(features, grad_out, mean_saved, rstd_saved, latent, *others):
    operands = (features, grad_out, mean_saved, rstd_saved, jnp.transpose(latent, (0, 2, 3, 1))) + others
    vmem = pl.BlockSpec(memory_space=pltpu.VMEM)
    dma = pltpu.SemaphoreType.DMA
    buffers = []
    for first_z, count, axis in PARTS:
        wide = (16, count * 128)
        low, high = span_of(first_z, count)
        first = (16, high - low) if axis == "x" else (4,) + wide
        buffers += [
            pltpu.VMEM((16, high - low + 128) if axis == "x" else (4,) + first, F32),
            pltpu.VMEM((8, 128) if axis == "x" else (4,) + first, F32),
            pltpu.VMEM((4,) + first, F32),
            pltpu.VMEM((4,) + first, BF16),
            pltpu.VMEM((3,) + first, BF16),
            pltpu.VMEM((4,) + wide, F32),
            pltpu.VMEM((4,) + wide, BF16),
            pltpu.VMEM((3,) + wide, BF16),
        ]
    parts = len(PARTS)
    partial = pl.pallas_call(
        body,
        out_shape=(
            jax.ShapeDtypeStruct((1, 2, H, W, C), BF16),
            jax.ShapeDtypeStruct((16, 128), F32),
            jax.ShapeDtypeStruct((TILES, 8, 128), F32),
            jax.ShapeDtypeStruct((8, 128), F32),
        ),
        in_specs=[pl.BlockSpec(memory_space=pltpu.HBM)] * 12,
        out_specs=(pl.BlockSpec(memory_space=pl.ANY),) + (vmem,) * 3,
        scratch_shapes=[
            pltpu.VMEM((1, 2, H, W, C), BF16),
            pltpu.VMEM((1, 2, H, W, CO), BF16),
            pltpu.VMEM((1, G), F32),
            pltpu.VMEM((1, G), F32),
            pltpu.VMEM((1, CZ, LP, NCTX // 2), F32),
            pltpu.VMEM((C,), F32),
            pltpu.VMEM((C,), F32),
            pltpu.VMEM((CZ, C), F32),
            pltpu.VMEM((C,), F32),
            pltpu.VMEM((CZ, C), F32),
            pltpu.VMEM((C,), F32),
            pltpu.VMEM((27 * C, CO), BF16),
            pltpu.VMEM((2, H, W, CO), BF16),
            pltpu.VMEM((2 * PX, C), BF16),
            pltpu.VMEM((2 * H, W, C), F32),
            pltpu.VMEM((2 * H, W, C), F32),
            pltpu.VMEM((4 * PX, 9 * CO), BF16),
            pltpu.VMEM((CO, 27 * C + 128), F32),
            pltpu.VMEM((2 * PX, C), F32),
            pltpu.VMEM((LP, C), F32),
            pltpu.VMEM((2, 2, W, C), F32),
            pltpu.VMEM((2, 2, W, C), F32),
            pltpu.VMEM((NZ, 16, 128), F32),
            pltpu.VMEM((NZ, 16, 128), BF16),
            pltpu.VMEM((NZ - 1, 16, 128), BF16),
            pltpu.VMEM((TILES, 8, 128), F32),
            pltpu.VMEM((32, 8, 128), F32),
            pltpu.VMEM((NZ, 8, 128), F32),
            pltpu.VMEM((16, 128), F32),
            pltpu.VMEM((16, 128), F32),
            dma((12,)),
            dma,
            dma((2,)),
            dma((parts,)),
            dma((parts,)),
            dma((parts,)),
            dma((parts,)),
            dma((parts,)),
            dma((parts,)),
            dma,
            dma,
            dma,
            dma,
            dma,
            dma,
            dma,
            dma,
            dma,
            dma,
            pltpu.SemaphoreType.REGULAR,
            pltpu.SemaphoreType.REGULAR,
            pltpu.SemaphoreType.REGULAR,
            pltpu.SemaphoreType.REGULAR,
            pltpu.VMEM((1, 2, H, W, C), BF16),
            dma,
            pltpu.VMEM((3, 9 * CO, C), BF16),
        ]
        + buffers,
        compiler_params=pltpu.CompilerParams(
            collective_id=0, has_side_effects=True, vmem_limit_bytes=36 * 1024 * 1024
        ),
    )(*(pltpu.with_memory_space_constraint(value, pltpu.HBM) for value in operands))
    fg, kg, mod, vec, lg = pl.pallas_call(
        finish,
        out_shape=(
            jax.ShapeDtypeStruct((1, 2, H, W, C), BF16),
            jax.ShapeDtypeStruct((16, ROWS), F32),
            jax.ShapeDtypeStruct((2, CZ, C), F32),
            jax.ShapeDtypeStruct((4, C), F32),
            jax.ShapeDtypeStruct((1, 1, LP // 2, CZ), F32),
        ),
        in_specs=[vmem] * 4,
        out_specs=(vmem,) * 5,
        compiler_params=pltpu.CompilerParams(vmem_limit_bytes=8 * 1024 * 1024),
    )(*partial)
    return fg, kg.T, mod, vec, jnp.swapaxes(lg, 2, 3)


def solution(mesh):
    placed = (
        P("vid", "ctx", None, None, None),
        P("vid", "ctx", None, None, None),
        P("vid", None),
        P("vid", None),
        P("vid", None, None, None),
        P(),
        P(),
        P(),
        P(),
        P(),
        P(),
        P(),
    )
    return jax.shard_map(
        local,
        mesh=mesh,
        in_specs=placed,
        out_specs=(
            P("vid", "ctx", None, None, None),
            P("ctx", "vid"),
            P(),
            P(),
            P("vid", "ctx", None, None),
        ),
        check_vma=False,
    )
```

```python
import jax
import jax.numpy as jnp
from jax import lax
from jax.experimental import pallas as pl
from jax.experimental.pallas import tpu as pltpu
from jax.sharding import PartitionSpec as P

MESH = pl.DeviceIdType.MESH
F32 = jnp.float32
BF16 = jnp.bfloat16
HIGHEST = lax.Precision.HIGHEST

NX, NY, NZ = 4, 4, 16
NCTX = NY * NZ
H, W, C, CO, CZ, G, LP = 8, 32, 256, 128, 16, 32, 16
PX = H * W
ROWS = 108
TILES = 10
PARTS = ((11, 5, "x"), (6, 3, "x"), (9, 2, "y"), (0, 3, "x"), (3, 3, "y"))
GROUPS = ((11, 16), (6, 11), (0, 6))
FAR_FIRST = (8, 7, 9, 6, 10, 5, 11, 4, 12, 3, 13, 2, 14, 1, 15)


def span_of(first_z, count):
    low = ROWS * NY * first_z // 128
    high = -(-ROWS * NY * (first_z + count) // 128)
    return low * 128, high * 128


def exact(lhs, rhs, dims):
    return lax.dot_general(lhs, rhs, (dims, ((), ())), precision=HIGHEST, preferred_element_type=F32)


def wide_dot(lhs, rhs, dims):
    return lax.dot_general(lhs, rhs, (dims, ((), ())), preferred_element_type=F32)


def body(
    feat_hbm, grad_hbm, mean_hbm, rstd_hbm, lat_hbm, gamma_hbm, beta_hbm, ws_hbm, bs_hbm, wh_hbm, bh_hbm, kern_hbm,
    fg_ref, kg_ref, final, lg_ref,
    feat_ref, grad_ref, mean_ref, rstd_ref, lat_ref, gamma_ref, beta_ref, ws_ref, bs_ref, wh_ref, bh_ref, kern,
    halo, act, dmod, norm, patch, gsum, agrad, tabs, maps, pools,
    zo, zs, zr, small, gathered, crossed, ls, lr,
    load_sems, halo_s, halo_r, core_s, core_r, first_s, first_r, second_s, second_r, z_s, z_r,
    small_s, small_r, cross_s, cross_r, final_s, final_r, lat_s, lat_r, relay, relay_far, relay_plane, relay_mate, image, image_s, turned,
    *part_refs,
):
    ctx = lax.axis_index("ctx")
    vid = lax.axis_index("vid")
    z, y = lax.div(ctx, NY), lax.rem(ctx, NY)
    x, core = lax.div(vid, 2), lax.rem(vid, 2)
    plane = y * 8 + vid

    def plane_id(p):
        return (z * NY + lax.div(p, 8), lax.rem(p, 8))

    def z_id(zz):
        return (zz * NY + y, vid)

    def x_id(xx):
        return (ctx, 2 * xx + core)

    def y_id(yy):
        return (z * NY + yy, vid)

    mate = (ctx, vid + 1 - 2 * core)
    sharer = (ctx + 1 - 2 * lax.rem(ctx, 2), vid)
    before = (lax.rem(ctx + NCTX - 1, NCTX), vid)
    after = (lax.rem(ctx + 1, NCTX), vid)

    loads = [
        pltpu.make_async_copy(source, target, load_sems.at[n])
        for n, (source, target) in enumerate(
            (
                (lat_hbm, lat_ref),
                (mean_hbm, mean_ref),
                (rstd_hbm, rstd_ref),
                (ws_hbm, ws_ref),
                (wh_hbm, wh_ref),
                (bs_hbm, bs_ref),
                (bh_hbm, bh_ref),
                (gamma_hbm, gamma_ref),
                (beta_hbm, beta_ref),
                (feat_hbm, feat_ref),
                (grad_hbm, grad_ref),
                (kern_hbm, kern),
            )
        )
    ]
    for load in loads:
        load.start()

    barrier = pltpu.get_barrier_semaphore()

    def signal(semaphore, device):
        pl.semaphore_signal(semaphore, inc=1, device_id=device, device_id_type=MESH)

    signal(barrier, before)
    signal(barrier, after)
    signal(barrier, mate)
    for k in range(1, 4):
        signal(barrier, x_id(lax.rem(x + k, NX)))
        signal(barrier, y_id(lax.rem(y + k, NY)))
    for k in (2, NZ - 2, 1, NZ - 1):
        signal(barrier, z_id(lax.rem(z + k, NZ)))

    def remote(src, dst, send, recv, device):
        return pltpu.make_async_remote_copy(
            src_ref=src, dst_ref=dst, send_sem=send, recv_sem=recv, device_id=device, device_id_type=MESH
        )

    pl.semaphore_wait(barrier, 13)
    halo_copies = [
        remote(grad_hbm.at[0, f], halo.at[f], halo_s, halo_r.at[f], before) for f in range(2)
    ]
    for copy in halo_copies:
        copy.start()
    signal(relay, z_id(lax.rem(z + 2, NZ)))
    signal(relay, z_id(lax.rem(z + NZ - 2, NZ)))
    for k in range(1, 4):
        signal(relay_plane, y_id(lax.rem(y + k, NY)))

    for load in loads[:9]:
        load.wait()

    pick = (lax.broadcasted_iota(jnp.int32, (G, C), 1) // (C // G) == lax.broadcasted_iota(jnp.int32, (G, C), 0)).astype(F32)
    saved = jnp.concatenate([mean_ref[...], rstd_ref[...], jnp.zeros((6, G), F32)], axis=0)
    saved = exact(saved, pick, ((1,), (0,)))
    mean_c, rstd_c = saved[0:1], saved[1:2]
    gamma = gamma_ref[...].reshape(1, C)
    beta = beta_ref[...].reshape(1, C)
    here = (lax.broadcasted_iota(jnp.int32, (NCTX // 2, 128), 0) == lax.div(ctx, 2)).astype(F32)
    lat = exact(lat_ref[0].reshape(CZ * LP, NCTX // 2), here, ((1,), (0,))).reshape(CZ, LP, 128)
    corner = lax.broadcasted_iota(jnp.int32, (CZ, LP, 128), 1) == lax.broadcasted_iota(jnp.int32, (CZ, LP, 128), 2)
    lat = jnp.sum(jnp.where(corner, lat, 0.0), axis=1)[:, :LP]
    weights = jnp.concatenate([ws_ref[...], wh_ref[...]], axis=1)
    bias = jnp.concatenate([bs_ref[...].reshape(1, C), bh_ref[...].reshape(1, C)], axis=1)
    both_tabs = exact(lat, weights, ((0,), (0,))) + bias
    tabs[...] = both_tabs[:, :C]
    pix = lax.broadcasted_iota(jnp.int32, (2 * W, LP), 0)
    latent_pixel = lax.broadcasted_iota(jnp.int32, (2 * W, LP), 1)
    spread = ((pix // W) * (W // 4) + (pix % W) // 4 == latent_pixel).astype(F32)
    both_maps = exact(spread, both_tabs, ((1,), (0,)))
    maps[0] = both_maps[:, :C].reshape(2, W, C)
    maps[1] = both_maps[:, C:].reshape(2, W, C)

    loads[9].wait()

    @pl.loop(0, 2 * H, unroll=4)
    def _(i):
        f, h = lax.div(i, H), lax.rem(i, H)
        hh = lax.div(h, 4)
        normed = (feat_ref[0, f, h].astype(F32) - mean_c) * rstd_c
        modulated = (normed * gamma + beta) * maps[0, hh] + maps[1, hh]
        s = jax.nn.sigmoid(modulated)
        norm[i] = normed
        dmod[i] = s * (1.0 + modulated * (1.0 - s))
        act[pl.ds(pl.multiple_of(i * W, W), W), :] = (modulated * s).astype(BF16)

    loads[10].wait()
    col = lax.broadcasted_iota(jnp.int32, (PX, CO), 0) % W

    def lay_patches(f, g):
        for c in range(3):
            if c == 0:
                moved = jnp.where(col == W - 1, 0.0, pltpu.roll(g, PX - 1, 0))
            elif c == 1:
                moved = g
            else:
                moved = jnp.where(col == 0, 0.0, pltpu.roll(g, 1, 0))
            moved = moved.astype(BF16)
            blank = jnp.zeros((W, CO), BF16)
            for b in range(3):
                lanes = slice((b * 3 + c) * CO, (b * 3 + c + 1) * CO)
                base = f * PX
                if b == 0:
                    patch[base : base + PX - W, lanes] = moved[W:]
                    patch[base + PX - W : base + PX, lanes] = blank
                elif b == 1:
                    patch[base : base + PX, lanes] = moved
                else:
                    patch[base : base + W, lanes] = blank
                    patch[base + W : base + PX, lanes] = moved[: PX - W]

    for f in range(2):
        lay_patches(f, grad_ref[0, f].astype(F32).reshape(PX, CO))

    def filter_term(a, first, last, images):
        for bc in range(9):
            lanes = slice(bc * CO, (bc + 1) * CO)
            tap = a * 9 + bc
            yield slice(tap * C, (tap + 1) * C), wide_dot(patch[first:last, lanes], images, ((0,), (0,)))

    def turn_taps(a):
        for bc in range(9):
            tap = a * 9 + bc
            turned[a, bc * CO : (bc + 1) * CO, :] = kern[tap * C : (tap + 1) * C, :].T

    def input_term(a, first, last):
        return wide_dot(patch[first:last, :], turned[a], ((1,), (0,)))

    lane = lax.broadcasted_iota(jnp.int32, (16, 128), 1)
    parts = []
    refs = list(part_refs)
    for n, (first_z, count, axis) in enumerate(PARTS):
        places = (x, y) if axis == "x" else (y, x)
        ids = (x_id, y_id) if axis == "x" else (y_id, x_id)
        names = ("own", "cs", "cr", "fs", "fr", "line", "ss", "sr")
        part = dict(zip(names, refs[: len(names)]))
        del refs[: len(names)]
        part.update(n=n, first_z=first_z, count=count, axis=axis, places=places, ids=ids)
        parts.append(part)

    def owned(place, parity):
        return pl.ds(pl.multiple_of((2 * place + parity) * 16, 16), 16)

    def shifted(low, high, off, turn):
        return jnp.where(lane < 128 - off, pltpu.roll(low, turn, 1), pltpu.roll(high, turn, 1))

    def deal(part):
        own, cs, n = part["own"], part["cs"], part["n"]
        if part["axis"] == "x":
            low, high = span_of(part["first_z"], part["count"])
            part["core"] = [
                remote(gsum.at[owned(xx, 1 - core), low:high], part["cr"].at[xx], core_s.at[n], core_r.at[n], mate)
                for xx in range(NX)
            ]
        else:

            @pl.loop(0, part["count"] * NY, unroll=4)
            def _(i):
                zl, yy = lax.div(i, NY), lax.rem(i, NY)
                start = ROWS * ((part["first_z"] + zl) * NY + yy)
                tile = lax.div(start, 128)
                off = start - tile * 128
                turn = lax.rem(128 - off, 128)
                first = pl.ds(pl.multiple_of(tile * 128, 128), 128)
                second = pl.ds(pl.multiple_of(tile * 128 + 128, 128), 128)
                lanes = pl.ds(pl.multiple_of(zl * 128, 128), 128)
                for xx in range(NX):
                    mine, theirs = owned(xx, core), owned(xx, 1 - core)
                    cs[yy, xx, :, lanes] = shifted(gsum[theirs, first], gsum[theirs, second], off, turn)
                    own[yy, xx, :, lanes] = shifted(gsum[mine, first], gsum[mine, second], off, turn)

            part["core"] = [remote(cs, part["cr"], core_s.at[n], core_r.at[n], mate)]
        for copy in part["core"]:
            copy.start()

    def first_stage(part):
        own, cr, fs, n = part["own"], part["cr"], part["fs"], part["n"]
        remote(cr, cr, core_s.at[n], core_r.at[n], mate).wait_recv()
        if part["axis"] == "x":
            low, high = span_of(part["first_z"], part["count"])
            for xx in range(NX):
                fs[xx] = (gsum[owned(xx, core), low:high] + cr[xx]).astype(BF16)
        else:

            @pl.loop(0, 16, unroll=2)
            def _(i):
                j, m = lax.div(i, 4), lax.rem(i, 4)
                total = own[j, m] + cr[j, m]
                own[j, m] = total
                fs[j, m] = total.astype(BF16)

        part["first"] = []
        for k in (2, 1, 3):
            there = lax.rem(part["places"][0] + k, 4)
            copy = remote(fs.at[there], part["fr"].at[k - 1], first_s.at[n], first_r.at[n], part["ids"][0](there))
            copy.start()
            part["first"].append(copy)

    def second_stage(part):
        own, cr, fr, line, ss, n = part["own"], part["cr"], part["fr"], part["line"], part["ss"], part["n"]
        remote(fr, fr, first_s.at[n], first_r.at[n], mate).wait_recv()
        if part["axis"] == "x":
            low, high = span_of(part["first_z"], part["count"])
            width = high - low
            own[:, 0:width] = (
                gsum[owned(x, core), low:high]
                + cr[x]
                + fr[0].astype(F32)
                + fr[1].astype(F32)
                + fr[2].astype(F32)
            )
            own[:, width:] = jnp.zeros((16, 128), F32)
            for i in range(part["count"] * NY):
                zl, yy = i // NY, i % NY
                start = ROWS * (part["first_z"] * NY + i) - low
                tile, off = start // 128, start % 128
                block = own[:, tile * 128 : tile * 128 + 128]
                if off:
                    block = shifted(block, own[:, tile * 128 + 128 : tile * 128 + 256], off, 128 - off)
                line[yy, :, zl * 128 : zl * 128 + 128] = block
        else:
            for j in range(4):
                line[j] = own[y, j] + fr[0, j].astype(F32) + fr[1, j].astype(F32) + fr[2, j].astype(F32)
        for j in range(4):
            ss[j] = line[j].astype(BF16)
        part["second"] = []
        for k in (2, 1, 3):
            there = lax.rem(part["places"][1] + k, 4)
            copy = remote(ss.at[there], part["sr"].at[k - 1], second_s.at[n], second_r.at[n], part["ids"][1](there))
            copy.start()
            part["second"].append(copy)

    def settle(part):
        sr, n = part["sr"], part["n"]
        remote(sr, sr, second_s.at[n], second_r.at[n], mate).wait_recv()
        total = part["line"][part["places"][1]] + sr[0].astype(F32) + sr[1].astype(F32) + sr[2].astype(F32)
        for j in range(part["count"]):
            piece = total[:, j * 128 : (j + 1) * 128]
            zo[part["first_z"] + j] = piece
            zs[part["first_z"] + j] = piece.astype(BF16)

    def z_copy(k):
        zz = lax.rem(z + k, NZ)
        return zz, remote(zs.at[zz], zr.at[k - 1], z_s, z_r, z_id(zz))

    def send_along_z(first, last):
        for k in FAR_FIRST:
            zz, copy = z_copy(k)

            @pl.when(jnp.logical_and(zz >= first, zz < last))
            def _():
                copy.start()

    gsum[:, 27 * C :] = jnp.zeros((CO, 128), F32)
    for span, term in filter_term(2, 0, 2 * PX, act[...]):
        gsum[:, span] = term
    deal(parts[0])
    for span, term in filter_term(1, PX, 2 * PX, act[0:PX]):
        gsum[:, span] = term
    loads[11].wait()
    for a in (2, 1, 0):
        turn_taps(a)
    agrad[...] = input_term(2, 0, 2 * PX)
    agrad[0:PX, :] += input_term(1, PX, 2 * PX)
    pl.semaphore_wait(relay, 2)
    signal(relay_far, z_id(lax.rem(z + 4, NZ)))
    signal(relay_far, z_id(lax.rem(z + NZ - 4, NZ)))
    pl.semaphore_wait(relay_plane, 3)
    signal(relay_mate, mate)
    first_stage(parts[0])

    @pl.when(ctx == 0)
    def _():
        for span, term in filter_term(1, 0, PX, act[0:PX]):
            gsum[:, span] += term
        for span, term in filter_term(0, 0, PX, act[0:PX]):
            gsum[:, span] = term
        for span, term in filter_term(0, PX, 2 * PX, act[0:PX]):
            gsum[:, span] += term
        agrad[0:PX, :] += input_term(1, 0, PX) + input_term(0, 0, PX) + input_term(0, PX, 2 * PX)

    @pl.when(ctx != 0)
    def _():
        gsum[:, 0 : 9 * C] = jnp.zeros((CO, 9 * C), F32)

    def take_halo(f):
        halo_copies[f].wait_recv()
        lay_patches(2 + f, jnp.where(ctx == NCTX - 1, 0.0, halo[f].astype(F32).reshape(PX, CO)))

    take_halo(0)
    for span, term in filter_term(1, 2 * PX, 3 * PX, act[PX : 2 * PX]):
        gsum[:, span] += term
    deal(parts[1])
    deal(parts[2])
    take_halo(1)
    agrad[...] += input_term(0, 2 * PX, 4 * PX)
    agrad[PX : 2 * PX, :] += input_term(1, 2 * PX, 3 * PX)

    pools[...] = jnp.zeros_like(pools)

    @pl.loop(0, 2 * H, unroll=4)
    def _(i):
        f, h = lax.div(i, H), lax.rem(i, H)
        hh = lax.div(h, 4)
        pre = agrad[pl.ds(pl.multiple_of(i * W, W), W), :] * dmod[i]
        image[0, f, h] = (pre * maps[0, hh] * gamma * rstd_c).astype(BF16)
        pools[0, hh] += pre * norm[i]
        pools[1, hh] += pre

    write_image = pltpu.make_async_copy(image, fg_ref, image_s)
    write_image.start()
    fields = jnp.concatenate([pools[0].reshape(2 * W, C), pools[1].reshape(2 * W, C)], axis=1)
    pooled = exact(spread, fields, ((0,), (0,)))
    normed_pool, shift_pool = pooled[:, :C], pooled[:, C:]
    scale_pool = normed_pool * gamma + shift_pool * beta
    projected = exact(lat, jnp.concatenate([scale_pool, shift_pool], axis=1), ((1,), (0,)))
    tab = tabs[...]
    rows = [
        projected[:, :C],
        projected[:, C:],
        jnp.concatenate(
            [
                jnp.sum(tab * normed_pool, axis=0, keepdims=True),
                jnp.sum(tab * shift_pool, axis=0, keepdims=True),
                jnp.sum(scale_pool, axis=0, keepdims=True),
                jnp.sum(shift_pool, axis=0, keepdims=True),
                jnp.zeros((4, C), F32),
            ],
            axis=0,
        ),
    ]
    for t in range(TILES):
        block, half = t // 2, t % 2
        source = rows[block // 2][(block % 2) * 8 : (block % 2) * 8 + 8]
        small[t] = source[:, half * 128 : (half + 1) * 128]

    chip = y * NX + x
    owner = jnp.logical_and(core == 0, chip < TILES)

    def tile_plane(t):
        return lax.div(t, NX) * 8 + 2 * lax.rem(t, NX)

    pl.semaphore_wait(relay_mate, 1)

    @pl.loop(0, TILES)
    def _(t):
        @pl.when(tile_plane(t) != plane)
        def _():
            remote(small.at[t], gathered.at[plane], small_s, small_r, plane_id(tile_plane(t))).start()

    for span, term in filter_term(0, 2 * PX, 4 * PX, act[...]):
        gsum[:, span] += term
    first_stage(parts[1])
    first_stage(parts[2])
    deal(parts[3])
    deal(parts[4])
    for part in parts[3:]:
        first_stage(part)

    second_stage(parts[0])
    latent_sum = exact(scale_pool, ws_ref[...], ((1,), (1,))) + exact(shift_pool, wh_ref[...], ((1,), (1,)))
    ls[...] = jnp.zeros_like(ls)
    ls[:, 0:CZ] = latent_sum
    lat_copy = remote(ls, lr, lat_s, lat_r, sharer)
    lat_copy.start()

    second_stage(parts[1])
    second_stage(parts[2])
    pl.semaphore_wait(relay_far, 2)
    @pl.when(owner)
    def _():
        others = gathered.at[0:31]
        remote(others, others, small_s, small_r, mate).wait_recv()

        gathered[plane] = small[chip]
        crossed[z] = jnp.sum(gathered[...], axis=0)

        @pl.loop(1, NZ)
        def _(k):
            zz = lax.rem(z + k, NZ)
            remote(crossed.at[z], crossed.at[z], cross_s, cross_r, z_id(zz)).start()

    second_stage(parts[3])
    second_stage(parts[4])
    settle(parts[0])
    send_along_z(*GROUPS[0])

    settle(parts[1])
    settle(parts[2])
    send_along_z(*GROUPS[1])
    @pl.when(owner)
    def _():
        others = crossed.at[0 : NZ - 1]
        remote(others, others, cross_s, cross_r, mate).wait_recv()
        final[chip] = jnp.sum(crossed[...], axis=0)

        @pl.loop(1, 32)
        def _(k):
            p = lax.rem(plane + k, 32)
            remote(final.at[chip], final.at[chip], final_s, final_r, plane_id(p)).start()

    settle(parts[3])
    settle(parts[4])
    send_along_z(*GROUPS[2])

    lat_copy.wait_recv()
    half = pl.ds(pl.multiple_of(lax.rem(ctx, 2) * 8, 8), 8)
    lg_ref[...] = ls[half, :] + lr[half, :]

    remote(zr, zr, z_s, z_r, mate).wait_recv()
    total = zo[z]
    for k in range(NZ - 1):
        total = total + zr[k].astype(F32)
    kg_ref[...] = total

    @pl.when(owner)
    def _():
        others = final.at[0 : TILES - 1]
        remote(others, others, final_s, final_r, mate).wait_recv()

    @pl.when(jnp.logical_not(owner))
    def _():
        remote(final, final, final_s, final_r, mate).wait_recv()

    write_image.wait()
    remote(halo, halo, halo_s, halo_r.at[0], mate).wait_send()
    lat_copy.wait_send()
    for part in parts:
        n = part["n"]
        remote(part["cr"], part["cr"], core_s.at[n], core_r.at[n], mate).wait_send()
        remote(part["fr"], part["fr"], first_s.at[n], first_r.at[n], mate).wait_send()
        remote(part["sr"], part["sr"], second_s.at[n], second_r.at[n], mate).wait_send()
    remote(zr, zr, z_s, z_r, mate).wait_send()

    @pl.when(owner)
    def _():
        tiles = small.at[0 : TILES - 1]
        remote(tiles, tiles, small_s, small_r, mate).wait_send()
        places = crossed.at[0 : NZ - 1]
        remote(places, places, cross_s, cross_r, mate).wait_send()
        copies = gathered.at[0:31]
        remote(copies, copies, final_s, final_r, mate).wait_send()

    @pl.when(jnp.logical_not(owner))
    def _():
        remote(small, small, small_s, small_r, mate).wait_send()


def finish(fg_in, kg_in, sums, lg_in, fg_ref, kg_ref, mod_ref, vec_ref, lg_ref):
    fg_ref[...] = fg_in[...]
    kg_ref[...] = kg_in[:, 0:ROWS]
    for t in range(8):
        block, half = t // 2, t % 2
        mod_ref[block // 2, (block % 2) * 8 : (block % 2) * 8 + 8, half * 128 : (half + 1) * 128] = sums[t]
    for half in range(2):
        vec_ref[:, half * 128 : (half + 1) * 128] = sums[8 + half, 0:4]
    lg_ref[0, 0] = lg_in[:, 0:CZ]


def local(features, grad_out, mean_saved, rstd_saved, latent, *others):
    operands = (features, grad_out, mean_saved, rstd_saved, jnp.transpose(latent, (0, 2, 3, 1))) + others
    vmem = pl.BlockSpec(memory_space=pltpu.VMEM)
    dma = pltpu.SemaphoreType.DMA
    buffers = []
    for first_z, count, axis in PARTS:
        wide = (16, count * 128)
        low, high = span_of(first_z, count)
        first = (16, high - low) if axis == "x" else (4,) + wide
        buffers += [
            pltpu.VMEM((16, high - low + 128) if axis == "x" else (4,) + first, F32),
            pltpu.VMEM((8, 128) if axis == "x" else (4,) + first, F32),
            pltpu.VMEM((4,) + first, F32),
            pltpu.VMEM((4,) + first, BF16),
            pltpu.VMEM((3,) + first, BF16),
            pltpu.VMEM((4,) + wide, F32),
            pltpu.VMEM((4,) + wide, BF16),
            pltpu.VMEM((3,) + wide, BF16),
        ]
    parts = len(PARTS)
    partial = pl.pallas_call(
        body,
        out_shape=(
            jax.ShapeDtypeStruct((1, 2, H, W, C), BF16),
            jax.ShapeDtypeStruct((16, 128), F32),
            jax.ShapeDtypeStruct((TILES, 8, 128), F32),
            jax.ShapeDtypeStruct((8, 128), F32),
        ),
        in_specs=[pl.BlockSpec(memory_space=pltpu.HBM)] * 12,
        out_specs=(pl.BlockSpec(memory_space=pl.ANY),) + (vmem,) * 3,
        scratch_shapes=[
            pltpu.VMEM((1, 2, H, W, C), BF16),
            pltpu.VMEM((1, 2, H, W, CO), BF16),
            pltpu.VMEM((1, G), F32),
            pltpu.VMEM((1, G), F32),
            pltpu.VMEM((1, CZ, LP, NCTX // 2), F32),
            pltpu.VMEM((C,), F32),
            pltpu.VMEM((C,), F32),
            pltpu.VMEM((CZ, C), F32),
            pltpu.VMEM((C,), F32),
            pltpu.VMEM((CZ, C), F32),
            pltpu.VMEM((C,), F32),
            pltpu.VMEM((27 * C, CO), BF16),
            pltpu.VMEM((2, H, W, CO), BF16),
            pltpu.VMEM((2 * PX, C), BF16),
            pltpu.VMEM((2 * H, W, C), F32),
            pltpu.VMEM((2 * H, W, C), F32),
            pltpu.VMEM((4 * PX, 9 * CO), BF16),
            pltpu.VMEM((CO, 27 * C + 128), F32),
            pltpu.VMEM((2 * PX, C), F32),
            pltpu.VMEM((LP, C), F32),
            pltpu.VMEM((2, 2, W, C), F32),
            pltpu.VMEM((2, 2, W, C), F32),
            pltpu.VMEM((NZ, 16, 128), F32),
            pltpu.VMEM((NZ, 16, 128), BF16),
            pltpu.VMEM((NZ - 1, 16, 128), BF16),
            pltpu.VMEM((TILES, 8, 128), F32),
            pltpu.VMEM((32, 8, 128), F32),
            pltpu.VMEM((NZ, 8, 128), F32),
            pltpu.VMEM((16, 128), F32),
            pltpu.VMEM((16, 128), F32),
            dma((12,)),
            dma,
            dma((2,)),
            dma((parts,)),
            dma((parts,)),
            dma((parts,)),
            dma((parts,)),
            dma((parts,)),
            dma((parts,)),
            dma,
            dma,
            dma,
            dma,
            dma,
            dma,
            dma,
            dma,
            dma,
            dma,
            pltpu.SemaphoreType.REGULAR,
            pltpu.SemaphoreType.REGULAR,
            pltpu.SemaphoreType.REGULAR,
            pltpu.SemaphoreType.REGULAR,
            pltpu.VMEM((1, 2, H, W, C), BF16),
            dma,
            pltpu.VMEM((3, 9 * CO, C), BF16),
        ]
        + buffers,
        compiler_params=pltpu.CompilerParams(
            collective_id=0, has_side_effects=True, vmem_limit_bytes=36 * 1024 * 1024
        ),
    )(*(pltpu.with_memory_space_constraint(value, pltpu.HBM) for value in operands))
    fg, kg, mod, vec, lg = pl.pallas_call(
        finish,
        out_shape=(
            jax.ShapeDtypeStruct((1, 2, H, W, C), BF16),
            jax.ShapeDtypeStruct((16, ROWS), F32),
            jax.ShapeDtypeStruct((2, CZ, C), F32),
            jax.ShapeDtypeStruct((4, C), F32),
            jax.ShapeDtypeStruct((1, 1, LP // 2, CZ), F32),
        ),
        in_specs=[vmem] * 4,
        out_specs=(vmem,) * 5,
        compiler_params=pltpu.CompilerParams(vmem_limit_bytes=8 * 1024 * 1024),
    )(*partial)
    return fg, kg.T, mod, vec, jnp.swapaxes(lg, 2, 3)


def solution(mesh):
    placed = (
        P("vid", "ctx", None, None, None),
        P("vid", "ctx", None, None, None),
        P("vid", None),
        P("vid", None),
        P("vid", None, None, None),
        P(),
        P(),
        P(),
        P(),
        P(),
        P(),
        P(),
    )
    return jax.shard_map(
        local,
        mesh=mesh,
        in_specs=placed,
        out_specs=(
            P("vid", "ctx", None, None, None),
            P("ctx", "vid"),
            P(),
            P(),
            P("vid", "ctx", None, None),
        ),
        check_vma=False,
    )
```

```python
import jax
import jax.numpy as jnp
from jax import lax
from jax.experimental import pallas as pl
from jax.experimental.pallas import tpu as pltpu
from jax.sharding import PartitionSpec as P

MESH = pl.DeviceIdType.MESH
F32 = jnp.float32
BF16 = jnp.bfloat16
HIGHEST = lax.Precision.HIGHEST

NX, NY, NZ = 4, 4, 16
NCTX = NY * NZ
H, W, C, CO, CZ, G, LP = 8, 32, 256, 128, 16, 32, 16
PX = H * W
ROWS = 108
TILES = 10
PARTS = ((11, 5, "x"), (6, 3, "x"), (9, 2, "y"), (0, 4, "x"), (4, 2, "y"))
GROUPS = ((11, 16), (6, 11), (0, 6))
FAR_FIRST = (8, 7, 9, 6, 10, 5, 11, 4, 12, 3, 13, 2, 14, 1, 15)


def span_of(first_z, count):
    low = ROWS * NY * first_z // 128
    high = -(-ROWS * NY * (first_z + count) // 128)
    return low * 128, high * 128


def exact(lhs, rhs, dims):
    return lax.dot_general(lhs, rhs, (dims, ((), ())), precision=HIGHEST, preferred_element_type=F32)


def wide_dot(lhs, rhs, dims):
    return lax.dot_general(lhs, rhs, (dims, ((), ())), preferred_element_type=F32)


def body(
    feat_hbm, grad_hbm, mean_hbm, rstd_hbm, lat_hbm, gamma_hbm, beta_hbm, ws_hbm, bs_hbm, wh_hbm, bh_hbm, kern_hbm,
    fg_ref, kg_ref, final, lg_ref,
    feat_ref, grad_ref, mean_ref, rstd_ref, lat_ref, gamma_ref, beta_ref, ws_ref, bs_ref, wh_ref, bh_ref, kern,
    halo, act, dmod, norm, patch, gsum, agrad, tabs, maps, pools,
    zo, zs, zr, small, gathered, crossed, ls, lr,
    load_sems, halo_s, halo_r, core_s, core_r, first_s, first_r, second_s, second_r, z_s, z_r,
    small_s, small_r, cross_s, cross_r, final_s, final_r, lat_s, lat_r, relay, relay_far, relay_plane, relay_mate, image, image_s, turned,
    *part_refs,
):
    ctx = lax.axis_index("ctx")
    vid = lax.axis_index("vid")
    z, y = lax.div(ctx, NY), lax.rem(ctx, NY)
    x, core = lax.div(vid, 2), lax.rem(vid, 2)
    plane = y * 8 + vid

    def plane_id(p):
        return (z * NY + lax.div(p, 8), lax.rem(p, 8))

    def z_id(zz):
        return (zz * NY + y, vid)

    def x_id(xx):
        return (ctx, 2 * xx + core)

    def y_id(yy):
        return (z * NY + yy, vid)

    mate = (ctx, vid + 1 - 2 * core)
    sharer = (ctx + 1 - 2 * lax.rem(ctx, 2), vid)
    before = (lax.rem(ctx + NCTX - 1, NCTX), vid)
    after = (lax.rem(ctx + 1, NCTX), vid)

    loads = [
        pltpu.make_async_copy(source, target, load_sems.at[n])
        for n, (source, target) in enumerate(
            (
                (lat_hbm, lat_ref),
                (mean_hbm, mean_ref),
                (rstd_hbm, rstd_ref),
                (ws_hbm, ws_ref),
                (wh_hbm, wh_ref),
                (bs_hbm, bs_ref),
                (bh_hbm, bh_ref),
                (gamma_hbm, gamma_ref),
                (beta_hbm, beta_ref),
                (feat_hbm, feat_ref),
                (grad_hbm, grad_ref),
                (kern_hbm, kern),
            )
        )
    ]
    for load in loads:
        load.start()

    barrier = pltpu.get_barrier_semaphore()

    def signal(semaphore, device):
        pl.semaphore_signal(semaphore, inc=1, device_id=device, device_id_type=MESH)

    signal(barrier, before)
    signal(barrier, after)
    signal(barrier, mate)
    for k in range(1, 4):
        signal(barrier, x_id(lax.rem(x + k, NX)))
        signal(barrier, y_id(lax.rem(y + k, NY)))
    for k in (2, NZ - 2, 1, NZ - 1):
        signal(barrier, z_id(lax.rem(z + k, NZ)))

    def remote(src, dst, send, recv, device):
        return pltpu.make_async_remote_copy(
            src_ref=src, dst_ref=dst, send_sem=send, recv_sem=recv, device_id=device, device_id_type=MESH
        )

    pl.semaphore_wait(barrier, 13)
    halo_copies = [
        remote(grad_hbm.at[0, f], halo.at[f], halo_s, halo_r.at[f], before) for f in range(2)
    ]
    for copy in halo_copies:
        copy.start()
    signal(relay, z_id(lax.rem(z + 2, NZ)))
    signal(relay, z_id(lax.rem(z + NZ - 2, NZ)))
    for k in range(1, 4):
        signal(relay_plane, y_id(lax.rem(y + k, NY)))

    for load in loads[:9]:
        load.wait()

    pick = (lax.broadcasted_iota(jnp.int32, (G, C), 1) // (C // G) == lax.broadcasted_iota(jnp.int32, (G, C), 0)).astype(F32)
    saved = jnp.concatenate([mean_ref[...], rstd_ref[...], jnp.zeros((6, G), F32)], axis=0)
    saved = exact(saved, pick, ((1,), (0,)))
    mean_c, rstd_c = saved[0:1], saved[1:2]
    gamma = gamma_ref[...].reshape(1, C)
    beta = beta_ref[...].reshape(1, C)
    here = (lax.broadcasted_iota(jnp.int32, (NCTX // 2, 128), 0) == lax.div(ctx, 2)).astype(F32)
    lat = exact(lat_ref[0].reshape(CZ * LP, NCTX // 2), here, ((1,), (0,))).reshape(CZ, LP, 128)
    corner = lax.broadcasted_iota(jnp.int32, (CZ, LP, 128), 1) == lax.broadcasted_iota(jnp.int32, (CZ, LP, 128), 2)
    lat = jnp.sum(jnp.where(corner, lat, 0.0), axis=1)[:, :LP]
    weights = jnp.concatenate([ws_ref[...], wh_ref[...]], axis=1)
    bias = jnp.concatenate([bs_ref[...].reshape(1, C), bh_ref[...].reshape(1, C)], axis=1)
    both_tabs = exact(lat, weights, ((0,), (0,))) + bias
    tabs[...] = both_tabs[:, :C]
    pix = lax.broadcasted_iota(jnp.int32, (2 * W, LP), 0)
    latent_pixel = lax.broadcasted_iota(jnp.int32, (2 * W, LP), 1)
    spread = ((pix // W) * (W // 4) + (pix % W) // 4 == latent_pixel).astype(F32)
    both_maps = exact(spread, both_tabs, ((1,), (0,)))
    maps[0] = both_maps[:, :C].reshape(2, W, C)
    maps[1] = both_maps[:, C:].reshape(2, W, C)

    loads[9].wait()

    @pl.loop(0, 2 * H, unroll=4)
    def _(i):
        f, h = lax.div(i, H), lax.rem(i, H)
        hh = lax.div(h, 4)
        normed = (feat_ref[0, f, h].astype(F32) - mean_c) * rstd_c
        modulated = (normed * gamma + beta) * maps[0, hh] + maps[1, hh]
        s = jax.nn.sigmoid(modulated)
        norm[i] = normed
        dmod[i] = s * (1.0 + modulated * (1.0 - s))
        act[pl.ds(pl.multiple_of(i * W, W), W), :] = (modulated * s).astype(BF16)

    loads[10].wait()
    col = lax.broadcasted_iota(jnp.int32, (PX, CO), 0) % W

    def lay_patches(f, g):
        for c in range(3):
            if c == 0:
                moved = jnp.where(col == W - 1, 0.0, pltpu.roll(g, PX - 1, 0))
            elif c == 1:
                moved = g
            else:
                moved = jnp.where(col == 0, 0.0, pltpu.roll(g, 1, 0))
            moved = moved.astype(BF16)
            blank = jnp.zeros((W, CO), BF16)
            for b in range(3):
                lanes = slice((b * 3 + c) * CO, (b * 3 + c + 1) * CO)
                base = f * PX
                if b == 0:
                    patch[base : base + PX - W, lanes] = moved[W:]
                    patch[base + PX - W : base + PX, lanes] = blank
                elif b == 1:
                    patch[base : base + PX, lanes] = moved
                else:
                    patch[base : base + W, lanes] = blank
                    patch[base + W : base + PX, lanes] = moved[: PX - W]

    for f in range(2):
        lay_patches(f, grad_ref[0, f].astype(F32).reshape(PX, CO))

    def filter_term(a, first, last, images):
        for bc in range(9):
            lanes = slice(bc * CO, (bc + 1) * CO)
            tap = a * 9 + bc
            yield slice(tap * C, (tap + 1) * C), wide_dot(patch[first:last, lanes], images, ((0,), (0,)))

    def turn_taps(a):
        for bc in range(9):
            tap = a * 9 + bc
            turned[a, bc * CO : (bc + 1) * CO, :] = kern[tap * C : (tap + 1) * C, :].T

    def input_term(a, first, last):
        return wide_dot(patch[first:last, :], turned[a], ((1,), (0,)))

    lane = lax.broadcasted_iota(jnp.int32, (16, 128), 1)
    parts = []
    refs = list(part_refs)
    for n, (first_z, count, axis) in enumerate(PARTS):
        places = (x, y) if axis == "x" else (y, x)
        ids = (x_id, y_id) if axis == "x" else (y_id, x_id)
        names = ("own", "cs", "cr", "fs", "fr", "line", "ss", "sr")
        part = dict(zip(names, refs[: len(names)]))
        del refs[: len(names)]
        part.update(n=n, first_z=first_z, count=count, axis=axis, places=places, ids=ids)
        parts.append(part)

    def owned(place, parity):
        return pl.ds(pl.multiple_of((2 * place + parity) * 16, 16), 16)

    def shifted(low, high, off, turn):
        return jnp.where(lane < 128 - off, pltpu.roll(low, turn, 1), pltpu.roll(high, turn, 1))

    def deal(part):
        own, cs, n = part["own"], part["cs"], part["n"]
        if part["axis"] == "x":
            low, high = span_of(part["first_z"], part["count"])
            part["core"] = [
                remote(gsum.at[owned(xx, 1 - core), low:high], part["cr"].at[xx], core_s.at[n], core_r.at[n], mate)
                for xx in range(NX)
            ]
        else:

            @pl.loop(0, part["count"] * NY, unroll=4)
            def _(i):
                zl, yy = lax.div(i, NY), lax.rem(i, NY)
                start = ROWS * ((part["first_z"] + zl) * NY + yy)
                tile = lax.div(start, 128)
                off = start - tile * 128
                turn = lax.rem(128 - off, 128)
                first = pl.ds(pl.multiple_of(tile * 128, 128), 128)
                second = pl.ds(pl.multiple_of(tile * 128 + 128, 128), 128)
                lanes = pl.ds(pl.multiple_of(zl * 128, 128), 128)
                for xx in range(NX):
                    mine, theirs = owned(xx, core), owned(xx, 1 - core)
                    cs[yy, xx, :, lanes] = shifted(gsum[theirs, first], gsum[theirs, second], off, turn)
                    own[yy, xx, :, lanes] = shifted(gsum[mine, first], gsum[mine, second], off, turn)

            part["core"] = [remote(cs, part["cr"], core_s.at[n], core_r.at[n], mate)]
        for copy in part["core"]:
            copy.start()

    def first_stage(part):
        own, cr, fs, n = part["own"], part["cr"], part["fs"], part["n"]
        remote(cr, cr, core_s.at[n], core_r.at[n], mate).wait_recv()
        if part["axis"] == "x":
            low, high = span_of(part["first_z"], part["count"])
            for xx in range(NX):
                fs[xx] = (gsum[owned(xx, core), low:high] + cr[xx]).astype(BF16)
        else:

            @pl.loop(0, 16, unroll=2)
            def _(i):
                j, m = lax.div(i, 4), lax.rem(i, 4)
                total = own[j, m] + cr[j, m]
                own[j, m] = total
                fs[j, m] = total.astype(BF16)

        part["first"] = []
        for k in (2, 1, 3):
            there = lax.rem(part["places"][0] + k, 4)
            copy = remote(fs.at[there], part["fr"].at[k - 1], first_s.at[n], first_r.at[n], part["ids"][0](there))
            copy.start()
            part["first"].append(copy)

    def second_stage(part):
        own, cr, fr, line, ss, n = part["own"], part["cr"], part["fr"], part["line"], part["ss"], part["n"]
        remote(fr, fr, first_s.at[n], first_r.at[n], mate).wait_recv()
        if part["axis"] == "x":
            low, high = span_of(part["first_z"], part["count"])
            width = high - low
            own[:, 0:width] = (
                gsum[owned(x, core), low:high]
                + cr[x]
                + fr[0].astype(F32)
                + fr[1].astype(F32)
                + fr[2].astype(F32)
            )
            own[:, width:] = jnp.zeros((16, 128), F32)
            for i in range(part["count"] * NY):
                zl, yy = i // NY, i % NY
                start = ROWS * (part["first_z"] * NY + i) - low
                tile, off = start // 128, start % 128
                block = own[:, tile * 128 : tile * 128 + 128]
                if off:
                    block = shifted(block, own[:, tile * 128 + 128 : tile * 128 + 256], off, 128 - off)
                line[yy, :, zl * 128 : zl * 128 + 128] = block
        else:
            for j in range(4):
                line[j] = own[y, j] + fr[0, j].astype(F32) + fr[1, j].astype(F32) + fr[2, j].astype(F32)
        for j in range(4):
            ss[j] = line[j].astype(BF16)
        part["second"] = []
        for k in (2, 1, 3):
            there = lax.rem(part["places"][1] + k, 4)
            copy = remote(ss.at[there], part["sr"].at[k - 1], second_s.at[n], second_r.at[n], part["ids"][1](there))
            copy.start()
            part["second"].append(copy)

    def settle(part):
        sr, n = part["sr"], part["n"]
        remote(sr, sr, second_s.at[n], second_r.at[n], mate).wait_recv()
        total = part["line"][part["places"][1]] + sr[0].astype(F32) + sr[1].astype(F32) + sr[2].astype(F32)
        for j in range(part["count"]):
            piece = total[:, j * 128 : (j + 1) * 128]
            zo[part["first_z"] + j] = piece
            zs[part["first_z"] + j] = piece.astype(BF16)

    def z_copy(k):
        zz = lax.rem(z + k, NZ)
        return zz, remote(zs.at[zz], zr.at[k - 1], z_s, z_r, z_id(zz))

    def send_along_z(first, last):
        for k in FAR_FIRST:
            zz, copy = z_copy(k)

            @pl.when(jnp.logical_and(zz >= first, zz < last))
            def _():
                copy.start()

    gsum[:, 27 * C :] = jnp.zeros((CO, 128), F32)
    for span, term in filter_term(2, 0, 2 * PX, act[...]):
        gsum[:, span] = term
    deal(parts[0])
    for span, term in filter_term(1, PX, 2 * PX, act[0:PX]):
        gsum[:, span] = term
    loads[11].wait()
    for a in (2, 1, 0):
        turn_taps(a)
    agrad[...] = input_term(2, 0, 2 * PX)
    agrad[0:PX, :] += input_term(1, PX, 2 * PX)
    pl.semaphore_wait(relay, 2)
    signal(relay_far, z_id(lax.rem(z + 4, NZ)))
    signal(relay_far, z_id(lax.rem(z + NZ - 4, NZ)))
    pl.semaphore_wait(relay_plane, 3)
    signal(relay_mate, mate)
    first_stage(parts[0])

    @pl.when(ctx == 0)
    def _():
        for span, term in filter_term(1, 0, PX, act[0:PX]):
            gsum[:, span] += term
        for span, term in filter_term(0, 0, PX, act[0:PX]):
            gsum[:, span] = term
        for span, term in filter_term(0, PX, 2 * PX, act[0:PX]):
            gsum[:, span] += term
        agrad[0:PX, :] += input_term(1, 0, PX) + input_term(0, 0, PX) + input_term(0, PX, 2 * PX)

    @pl.when(ctx != 0)
    def _():
        gsum[:, 0 : 9 * C] = jnp.zeros((CO, 9 * C), F32)

    def take_halo(f):
        halo_copies[f].wait_recv()
        lay_patches(2 + f, jnp.where(ctx == NCTX - 1, 0.0, halo[f].astype(F32).reshape(PX, CO)))

    take_halo(0)
    for span, term in filter_term(1, 2 * PX, 3 * PX, act[PX : 2 * PX]):
        gsum[:, span] += term
    deal(parts[1])
    deal(parts[2])
    take_halo(1)
    agrad[...] += input_term(0, 2 * PX, 4 * PX)
    agrad[PX : 2 * PX, :] += input_term(1, 2 * PX, 3 * PX)

    pools[...] = jnp.zeros_like(pools)

    @pl.loop(0, 2 * H, unroll=4)
    def _(i):
        f, h = lax.div(i, H), lax.rem(i, H)
        hh = lax.div(h, 4)
        pre = agrad[pl.ds(pl.multiple_of(i * W, W), W), :] * dmod[i]
        image[0, f, h] = (pre * maps[0, hh] * gamma * rstd_c).astype(BF16)
        pools[0, hh] += pre * norm[i]
        pools[1, hh] += pre

    write_image = pltpu.make_async_copy(image, fg_ref, image_s)
    write_image.start()
    first_stage(parts[1])
    first_stage(parts[2])
    fields = jnp.concatenate([pools[0].reshape(2 * W, C), pools[1].reshape(2 * W, C)], axis=1)
    pooled = exact(spread, fields, ((0,), (0,)))
    normed_pool, shift_pool = pooled[:, :C], pooled[:, C:]
    scale_pool = normed_pool * gamma + shift_pool * beta
    projected = exact(lat, jnp.concatenate([scale_pool, shift_pool], axis=1), ((1,), (0,)))
    tab = tabs[...]
    rows = [
        projected[:, :C],
        projected[:, C:],
        jnp.concatenate(
            [
                jnp.sum(tab * normed_pool, axis=0, keepdims=True),
                jnp.sum(tab * shift_pool, axis=0, keepdims=True),
                jnp.sum(scale_pool, axis=0, keepdims=True),
                jnp.sum(shift_pool, axis=0, keepdims=True),
                jnp.zeros((4, C), F32),
            ],
            axis=0,
        ),
    ]
    for t in range(TILES):
        block, half = t // 2, t % 2
        source = rows[block // 2][(block % 2) * 8 : (block % 2) * 8 + 8]
        small[t] = source[:, half * 128 : (half + 1) * 128]

    chip = y * NX + x
    owner = jnp.logical_and(core == 0, chip < TILES)

    def tile_plane(t):
        return lax.div(t, NX) * 8 + 2 * lax.rem(t, NX)

    pl.semaphore_wait(relay_mate, 1)

    @pl.loop(0, TILES)
    def _(t):
        @pl.when(tile_plane(t) != plane)
        def _():
            remote(small.at[t], gathered.at[plane], small_s, small_r, plane_id(tile_plane(t))).start()

    for span, term in filter_term(0, 2 * PX, 4 * PX, act[...]):
        gsum[:, span] += term
    deal(parts[3])
    deal(parts[4])
    for part in parts[3:]:
        first_stage(part)

    second_stage(parts[0])
    latent_sum = exact(scale_pool, ws_ref[...], ((1,), (1,))) + exact(shift_pool, wh_ref[...], ((1,), (1,)))
    ls[...] = jnp.zeros_like(ls)
    ls[:, 0:CZ] = latent_sum
    lat_copy = remote(ls, lr, lat_s, lat_r, sharer)
    lat_copy.start()

    second_stage(parts[1])
    second_stage(parts[2])
    pl.semaphore_wait(relay_far, 2)
    @pl.when(owner)
    def _():
        others = gathered.at[0:31]
        remote(others, others, small_s, small_r, mate).wait_recv()

        gathered[plane] = small[chip]
        crossed[z] = jnp.sum(gathered[...], axis=0)

        @pl.loop(1, NZ)
        def _(k):
            zz = lax.rem(z + k, NZ)
            remote(crossed.at[z], crossed.at[z], cross_s, cross_r, z_id(zz)).start()

    second_stage(parts[3])
    second_stage(parts[4])
    settle(parts[0])
    send_along_z(*GROUPS[0])

    settle(parts[1])
    settle(parts[2])
    send_along_z(*GROUPS[1])
    settle(parts[3])
    settle(parts[4])
    send_along_z(*GROUPS[2])

    @pl.when(owner)
    def _():
        others = crossed.at[0 : NZ - 1]
        remote(others, others, cross_s, cross_r, mate).wait_recv()
        final[chip] = jnp.sum(crossed[...], axis=0)

        @pl.loop(1, 32)
        def _(k):
            p = lax.rem(plane + k, 32)
            remote(final.at[chip], final.at[chip], final_s, final_r, plane_id(p)).start()

    lat_copy.wait_recv()
    half = pl.ds(pl.multiple_of(lax.rem(ctx, 2) * 8, 8), 8)
    lg_ref[...] = ls[half, :] + lr[half, :]

    remote(zr, zr, z_s, z_r, mate).wait_recv()
    total = zo[z]
    for k in range(NZ - 1):
        total = total + zr[k].astype(F32)
    kg_ref[...] = total

    @pl.when(owner)
    def _():
        others = final.at[0 : TILES - 1]
        remote(others, others, final_s, final_r, mate).wait_recv()

    @pl.when(jnp.logical_not(owner))
    def _():
        remote(final, final, final_s, final_r, mate).wait_recv()

    write_image.wait()
    remote(halo, halo, halo_s, halo_r.at[0], mate).wait_send()
    lat_copy.wait_send()
    for part in parts:
        n = part["n"]
        remote(part["cr"], part["cr"], core_s.at[n], core_r.at[n], mate).wait_send()
        remote(part["fr"], part["fr"], first_s.at[n], first_r.at[n], mate).wait_send()
        remote(part["sr"], part["sr"], second_s.at[n], second_r.at[n], mate).wait_send()
    remote(zr, zr, z_s, z_r, mate).wait_send()

    @pl.when(owner)
    def _():
        tiles = small.at[0 : TILES - 1]
        remote(tiles, tiles, small_s, small_r, mate).wait_send()
        places = crossed.at[0 : NZ - 1]
        remote(places, places, cross_s, cross_r, mate).wait_send()
        copies = gathered.at[0:31]
        remote(copies, copies, final_s, final_r, mate).wait_send()

    @pl.when(jnp.logical_not(owner))
    def _():
        remote(small, small, small_s, small_r, mate).wait_send()


def finish(fg_in, kg_in, sums, lg_in, fg_ref, kg_ref, mod_ref, vec_ref, lg_ref):
    fg_ref[...] = fg_in[...]
    kg_ref[...] = kg_in[:, 0:ROWS]
    for t in range(8):
        block, half = t // 2, t % 2
        mod_ref[block // 2, (block % 2) * 8 : (block % 2) * 8 + 8, half * 128 : (half + 1) * 128] = sums[t]
    for half in range(2):
        vec_ref[:, half * 128 : (half + 1) * 128] = sums[8 + half, 0:4]
    lg_ref[0, 0] = lg_in[:, 0:CZ]


def local(features, grad_out, mean_saved, rstd_saved, latent, *others):
    operands = (features, grad_out, mean_saved, rstd_saved, jnp.transpose(latent, (0, 2, 3, 1))) + others
    vmem = pl.BlockSpec(memory_space=pltpu.VMEM)
    dma = pltpu.SemaphoreType.DMA
    buffers = []
    for first_z, count, axis in PARTS:
        wide = (16, count * 128)
        low, high = span_of(first_z, count)
        first = (16, high - low) if axis == "x" else (4,) + wide
        buffers += [
            pltpu.VMEM((16, high - low + 128) if axis == "x" else (4,) + first, F32),
            pltpu.VMEM((8, 128) if axis == "x" else (4,) + first, F32),
            pltpu.VMEM((4,) + first, F32),
            pltpu.VMEM((4,) + first, BF16),
            pltpu.VMEM((3,) + first, BF16),
            pltpu.VMEM((4,) + wide, F32),
            pltpu.VMEM((4,) + wide, BF16),
            pltpu.VMEM((3,) + wide, BF16),
        ]
    parts = len(PARTS)
    partial = pl.pallas_call(
        body,
        out_shape=(
            jax.ShapeDtypeStruct((1, 2, H, W, C), BF16),
            jax.ShapeDtypeStruct((16, 128), F32),
            jax.ShapeDtypeStruct((TILES, 8, 128), F32),
            jax.ShapeDtypeStruct((8, 128), F32),
        ),
        in_specs=[pl.BlockSpec(memory_space=pltpu.HBM)] * 12,
        out_specs=(pl.BlockSpec(memory_space=pl.ANY),) + (vmem,) * 3,
        scratch_shapes=[
            pltpu.VMEM((1, 2, H, W, C), BF16),
            pltpu.VMEM((1, 2, H, W, CO), BF16),
            pltpu.VMEM((1, G), F32),
            pltpu.VMEM((1, G), F32),
            pltpu.VMEM((1, CZ, LP, NCTX // 2), F32),
            pltpu.VMEM((C,), F32),
            pltpu.VMEM((C,), F32),
            pltpu.VMEM((CZ, C), F32),
            pltpu.VMEM((C,), F32),
            pltpu.VMEM((CZ, C), F32),
            pltpu.VMEM((C,), F32),
            pltpu.VMEM((27 * C, CO), BF16),
            pltpu.VMEM((2, H, W, CO), BF16),
            pltpu.VMEM((2 * PX, C), BF16),
            pltpu.VMEM((2 * H, W, C), F32),
            pltpu.VMEM((2 * H, W, C), F32),
            pltpu.VMEM((4 * PX, 9 * CO), BF16),
            pltpu.VMEM((CO, 27 * C + 128), F32),
            pltpu.VMEM((2 * PX, C), F32),
            pltpu.VMEM((LP, C), F32),
            pltpu.VMEM((2, 2, W, C), F32),
            pltpu.VMEM((2, 2, W, C), F32),
            pltpu.VMEM((NZ, 16, 128), F32),
            pltpu.VMEM((NZ, 16, 128), BF16),
            pltpu.VMEM((NZ - 1, 16, 128), BF16),
            pltpu.VMEM((TILES, 8, 128), F32),
            pltpu.VMEM((32, 8, 128), F32),
            pltpu.VMEM((NZ, 8, 128), F32),
            pltpu.VMEM((16, 128), F32),
            pltpu.VMEM((16, 128), F32),
            dma((12,)),
            dma,
            dma((2,)),
            dma((parts,)),
            dma((parts,)),
            dma((parts,)),
            dma((parts,)),
            dma((parts,)),
            dma((parts,)),
            dma,
            dma,
            dma,
            dma,
            dma,
            dma,
            dma,
            dma,
            dma,
            dma,
            pltpu.SemaphoreType.REGULAR,
            pltpu.SemaphoreType.REGULAR,
            pltpu.SemaphoreType.REGULAR,
            pltpu.SemaphoreType.REGULAR,
            pltpu.VMEM((1, 2, H, W, C), BF16),
            dma,
            pltpu.VMEM((3, 9 * CO, C), BF16),
        ]
        + buffers,
        compiler_params=pltpu.CompilerParams(
            collective_id=0, has_side_effects=True, vmem_limit_bytes=36 * 1024 * 1024
        ),
    )(*(pltpu.with_memory_space_constraint(value, pltpu.HBM) for value in operands))
    fg, kg, mod, vec, lg = pl.pallas_call(
        finish,
        out_shape=(
            jax.ShapeDtypeStruct((1, 2, H, W, C), BF16),
            jax.ShapeDtypeStruct((16, ROWS), F32),
            jax.ShapeDtypeStruct((2, CZ, C), F32),
            jax.ShapeDtypeStruct((4, C), F32),
            jax.ShapeDtypeStruct((1, 1, LP // 2, CZ), F32),
        ),
        in_specs=[vmem] * 4,
        out_specs=(vmem,) * 5,
        compiler_params=pltpu.CompilerParams(vmem_limit_bytes=8 * 1024 * 1024),
    )(*partial)
    return fg, kg.T, mod, vec, jnp.swapaxes(lg, 2, 3)


def solution(mesh):
    placed = (
        P("vid", "ctx", None, None, None),
        P("vid", "ctx", None, None, None),
        P("vid", None),
        P("vid", None),
        P("vid", None, None, None),
        P(),
        P(),
        P(),
        P(),
        P(),
        P(),
        P(),
    )
    return jax.shard_map(
        local,
        mesh=mesh,
        in_specs=placed,
        out_specs=(
            P("vid", "ctx", None, None, None),
            P("ctx", "vid"),
            P(),
            P(),
            P("vid", "ctx", None, None),
        ),
        check_vma=False,
    )
```
